32 devices in a mesh: wide: 8 (over z, y), narrow: 4 (over x, core).
Axes of the slice: x: 2, y: 2, z: 4, core: 2. Of those that a mesh axis runs over, the one named last changes fastest.
Arguments:
- image_tokens: bfloat16 [16, 1024, 1024], P('wide', 'narrow'), may hold values from -6 to 6
- text_states: bfloat16 [16, 128, 1024], P('wide', 'narrow'), may hold values from -6 to 6
- caption_lengths: int32 [16], P('wide'), may hold values from 1 to 128, as said below
- text_mask: int32 [16, 128], P('wide'), may hold values 0 or 1
- self_qkv: bfloat16 [3, 1024, 1024], replicated, may hold values from -0.1875 to 0.1875
- self_out: bfloat16 [1024, 1024], replicated, may hold values from -0.75 to 0.75
- cross_query: bfloat16 [1024, 1024], replicated, may hold values from -0.1875 to 0.1875
- cross_kv: bfloat16 [2, 1024, 1024], replicated, may hold values from -0.1875 to 0.1875
- cross_out: bfloat16 [1024, 1024], replicated, may hold values from -0.5 to 0.5
- mlp_in: bfloat16 [1024, 4096], replicated, may hold values from -0.1875 to 0.1875
- mlp_out: bfloat16 [4096, 1024], replicated, may hold values from -0.09375 to 0.09375
- norm_gains: float32 [3, 1024], replicated, may hold values from 0.1 to 1.9
- norm_shifts: float32 [3, 1024], replicated, may hold values from -3 to 3
- out_biases: float32 [3, 1024], replicated, may hold values from -3 to 3
- mlp_bias: float32 [4096], replicated, may hold values from -3 to 3
- cotangent: bfloat16 [16, 1024, 1024], P('wide', 'narrow'), may hold values from -6 to 6
Outputs:
- layer_out: float32 [16, 1024, 1024], P('wide', 'narrow')
- grad_image: float32 [16, 1024, 1024], P('wide', 'narrow')
- grad_text: float32 [16, 128, 1024], P('wide', 'narrow')
- grad_self_qkv: float32 [3, 1024, 1024], P(None, 'wide', 'narrow')
- grad_self_out: float32 [1024, 1024], P('wide', 'narrow')
- grad_cross_query: float32 [1024, 1024], P('wide', 'narrow')
- grad_cross_kv: float32 [2, 1024, 1024], P(None, 'wide', 'narrow')
- grad_cross_out: float32 [1024, 1024], P('wide', 'narrow')
- grad_mlp_in: float32 [1024, 4096], P('wide', 'narrow')
- grad_mlp_out: float32 [4096, 1024], P('wide', 'narrow')
- grad_norm_gains: float32 [3, 1024], replicated
- grad_norm_shifts: float32 [3, 1024], replicated
- grad_out_biases: float32 [3, 1024], replicated
- grad_mlp_bias: float32 [4096], replicated
The draws below stay inside these ranges and needn't reach their ends.
Inputs may be any that keep to these rules, and one draw needn't show every extreme that they name: `caption_lengths`: in every aligned block of 2 items, one caption has all 128 slots.
All inputs are finite; a program needn't handle non-finite values. No bound on the sum of `text_mask` on one device may be relied on, other than what follows from the above.
Results may differ from the reference program's by a relative error of at most 0.023.
Values may be sent and summed in bfloat16 or wider, within the bound.
No kernel may reach another device: no remote copies, remote signals or barrier semaphores. Data moves between devices by JAX's collectives and lax.ppermute only.
A program may use at most 384 MiB of HBM per device.

```python
import jax
import jax.numpy as jnp
from jax import lax

D = 1024
HEADS = 16
HEAD_DIM = 64
FF = 4096
ITEM_LEN = 1024
TXT = 128
ITEMS_W = 2
ITEMS = 16


def draw_caption_lengths(key, part):
    short_key, tail_key, long_key, pick_key = jax.random.split(key, 4)
    short_len = jax.random.randint(short_key, (ITEMS,), 1, min(20, TXT) + 1)
    in_tail = jax.random.randint(tail_key, (ITEMS,), 0, 6) == 0
    long_len = jax.random.randint(long_key, (ITEMS,), min(21, TXT), TXT + 1)
    lengths = jnp.where(in_tail, long_len, short_len)
    chosen = jax.random.randint(pick_key, (ITEMS // ITEMS_W, 1), 0, ITEMS_W)
    filled = (jnp.arange(ITEMS_W)[None, :] == chosen).reshape(ITEMS)
    return jnp.where(filled, TXT, lengths).astype(jnp.int32)


def plant(values, stream_key, least, top_value):
    index_at = [jax.random.randint(jax.random.fold_in(stream_key, axis), (), 0, length) for axis, length in enumerate(values.shape)]
    longest = values.shape.index(max(values.shape))
    neighbour = index_at[:longest] + [(index_at[longest] + 1) % values.shape[longest]] + index_at[longest + 1:]
    return values.at[tuple(index_at)].set(least).at[tuple(neighbour)].set(top_value)


def levels(own_key, dims, cuts, smallest, largest):
    level = 1.0
    for position, blocks in cuts:
        steps = jax.random.uniform(jax.random.fold_in(jax.random.fold_in(own_key, 6), position), (blocks,), jnp.float32, smallest / len(cuts), largest / len(cuts))
        level = level * jnp.repeat(jnp.exp(steps), dims[position] // blocks).reshape((-1,) + (1,) * (len(dims) - 1 - position))
    return level


def gaussian(key, extent, spread, most, shards=(), kind=jnp.bfloat16):
    array = spread * jax.random.normal(key, extent, jnp.float32)
    if shards:
        array = array * levels(key, extent, shards, -0.22, 0.18)
    return jnp.clip(array, -most, most).astype(kind)


def setup_inputs(seed: int = 0) -> dict:
    arg_keys = jax.random.split(jax.random.key(seed), 17)
    return {
        "image_tokens": gaussian(arg_keys[0], (ITEMS, ITEM_LEN, D), 1.0, 6.0, ((0, 8), (1, 4))),
        "text_states": gaussian(arg_keys[1], (ITEMS, TXT, D), 1.0, 6.0, ((0, 8), (1, 4))),
        "caption_lengths": draw_caption_lengths(jax.random.fold_in(arg_keys[16], 71), 0),
        "text_mask": plant((jax.random.randint(arg_keys[3], (ITEMS, TXT), 0, 4) < 3).astype(jnp.int32), jax.random.fold_in(arg_keys[3], 1), 0, 1),
        "self_qkv": gaussian(arg_keys[4], (3, D, D), D ** -0.5, 0.1875),
        "self_out": gaussian(arg_keys[5], (D, D), (D // 16) ** -0.5, 0.75),
        "cross_query": gaussian(arg_keys[6], (D, D), D ** -0.5, 0.1875),
        "cross_kv": gaussian(arg_keys[7], (2, D, D), D ** -0.5, 0.1875),
        "cross_out": gaussian(arg_keys[8], (D, D), (D // 8) ** -0.5, 0.5),
        "mlp_in": gaussian(arg_keys[9], (D, FF), D ** -0.5, 0.1875),
        "mlp_out": gaussian(arg_keys[10], (FF, D), FF ** -0.5, 0.09375),
        "norm_gains": jnp.clip(1.0 + 0.18 * jax.random.normal(arg_keys[11], (3, D), jnp.float32), 0.1, 1.9),
        "norm_shifts": gaussian(arg_keys[12], (3, D), 0.3, 3.0, (), jnp.float32),
        "out_biases": gaussian(arg_keys[13], (3, D), 0.3, 3.0, (), jnp.float32),
        "mlp_bias": gaussian(arg_keys[14], (FF,), 0.3, 3.0, (), jnp.float32),
        "cotangent": gaussian(arg_keys[15], (ITEMS, ITEM_LEN, D), 1.0, 6.0, ((0, 8), (1, 4))),
    }


@jax.custom_vjp
def low(v):
    return lax.optimization_barrier(v.astype(jnp.bfloat16)).astype(jnp.float32)

@jax.custom_vjp
def low_back(v):
    return v

def low_keep(v):
    return (low(v), None)

def low_pass(kept, grad):
    return (grad,)

def back_keep(v):
    return (v, None)

def back_low(kept, grad):
    return (low(grad),)
low.defvjp(low_keep, low_pass)
low_back.defvjp(back_keep, back_low)
highest = lax.Precision.HIGHEST

def product(left, right):
    return jnp.dot(left, right, precision=highest, preferred_element_type=jnp.float32)

def gelu_tanh(pre_act):
    return 0.5 * pre_act * (1.0 + jnp.tanh(0.7978845608028654 * (pre_act + 0.044715 * pre_act * pre_act * pre_act)))

def layer_norm(hidden, gain, shift):
    centered = hidden - lax.optimization_barrier(jnp.mean(hidden, -1, keepdims=True))
    variance = lax.optimization_barrier(jnp.mean(centered * centered, -1, keepdims=True))
    return centered * lax.rsqrt(variance + 1e-05) * gain + shift

def attend(queries, keys_all, values_all, allowed):
    count_q = queries.shape[0]
    count_k = keys_all.shape[0]
    heads_q = queries.reshape(count_q, HEADS, HEAD_DIM)
    heads_k = keys_all.reshape(count_k, HEADS, HEAD_DIM)
    heads_v = values_all.reshape(count_k, HEADS, HEAD_DIM)
    raw_scores = jnp.einsum('qhd,khd->hqk', heads_q, heads_k, precision=highest) * HEAD_DIM ** (-0.5)
    scores = jnp.where(allowed[None], low_back(raw_scores), -1e+30)
    top_score = lax.optimization_barrier(jnp.max(scores, -1, keepdims=True))
    expo = jnp.exp(scores - top_score)
    probs = expo / lax.optimization_barrier(jnp.sum(expo, -1, keepdims=True))
    mixed = jnp.einsum('hqk,khd->qhd', low(probs), heads_v, precision=highest)
    return mixed.reshape(count_q, HEADS * HEAD_DIM)

def layer(params, image_rows, text_rows, allowed_self, allowed_text):
    w_qkv, w_self_out, w_cross_query, w_cross_kv, w_cross_out, w_up, w_down, gains, shifts, biases, hidden_bias = params
    normed_one = low(layer_norm(image_rows, gains[0], shifts[0]))
    query_self = low(low_back(product(normed_one, w_qkv[0])))
    key_self = low(low_back(product(normed_one, w_qkv[1])))
    value_self = low(low_back(product(normed_one, w_qkv[2])))
    mixed_self = low(low_back(attend(query_self, key_self, value_self, allowed_self)))
    after_self = image_rows + low_back(product(mixed_self, w_self_out) + biases[0])
    normed_two = low(layer_norm(after_self, gains[1], shifts[1]))
    query_cross = low(low_back(product(normed_two, w_cross_query)))
    text_key = low(low_back(product(text_rows, w_cross_kv[0])))
    text_value = low(low_back(product(text_rows, w_cross_kv[1])))
    mixed_cross = low(low_back(attend(query_cross, text_key, text_value, allowed_text)))
    after_cross = after_self + low_back(product(mixed_cross, w_cross_out) + biases[1])
    normed_three = low(layer_norm(after_cross, gains[2], shifts[2]))
    pre_act = low_back(product(normed_three, w_up) + hidden_bias)
    activated = low(low_back(gelu_tanh(pre_act)))
    return after_cross + low_back(product(activated, w_down) + biases[2])

def add_pair(first, second):
    return first + second

def reference(image_tokens, text_states, caption_lengths, text_mask, self_qkv, self_out, cross_query, cross_kv, cross_out, mlp_in, mlp_out, norm_gains, norm_shifts, out_biases, mlp_bias, cotangent):
    params = (self_qkv.astype(jnp.float32), self_out.astype(jnp.float32), cross_query.astype(jnp.float32), cross_kv.astype(jnp.float32), cross_out.astype(jnp.float32), mlp_in.astype(jnp.float32), mlp_out.astype(jnp.float32), norm_gains.astype(jnp.float32), norm_shifts.astype(jnp.float32), out_biases.astype(jnp.float32), mlp_bias.astype(jnp.float32))
    positions = jnp.arange(ITEM_LEN)
    allowed_self = positions[None, :] <= positions[:, None]
    slot_index = jnp.arange(TXT)

    def one_item(totals, inputs):
        image_item, text_item, length_item, mask_item, cot_item = inputs
        live_slots = (slot_index < length_item) & ((mask_item == 1) | (slot_index == 0))
        allowed_text = jnp.broadcast_to(live_slots[None, :], (ITEM_LEN, TXT))

        def run_item(weights, image_rows, text_rows):
            return layer(weights, image_rows, text_rows, allowed_self, allowed_text)
        result, pull = jax.vjp(run_item, params, image_item.astype(jnp.float32), text_item.astype(jnp.float32))
        grad_params, grad_rows, grad_texts = pull(cot_item.astype(jnp.float32))
        totals = jax.tree.map(add_pair, totals, grad_params)
        return (totals, (result, grad_rows, grad_texts))
    zeros = jax.tree.map(jnp.zeros_like, params)
    totals, outputs = lax.scan(one_item, zeros, (image_tokens, text_states, caption_lengths, text_mask, cotangent))
    layer_out, grad_image, grad_text = outputs
    return (layer_out, grad_image, grad_text, totals[0], totals[1], totals[2], totals[3], totals[4], totals[5], totals[6], totals[7], totals[8], totals[9], totals[10])
```

```python
import jax
import jax.numpy as jnp
from jax import lax
from jax.experimental import pallas as pl
from jax.experimental.pallas import tpu as pltpu
from jax.sharding import PartitionSpec as P

HEAD_DIM = 64
PAIR = 2 * HEAD_DIM
SCALE = HEAD_DIM**-0.5
NEG = -1e30
BF = jnp.bfloat16
F32 = jnp.float32
VMEM = 56 * 1024 * 1024


def dot(left, right, left_axis, right_axis):
    return lax.dot_general(
        left, right, (((left_axis,), (right_axis,)), ((), ())), preferred_element_type=F32
    )


def two_heads(rows):
    lane = lax.broadcasted_iota(jnp.int32, rows.shape, 1)
    zero = jnp.zeros_like(rows)
    return jnp.concatenate(
        [jnp.where(lane < HEAD_DIM, rows, zero), jnp.where(lane < HEAD_DIM, zero, rows)], 0
    )


def block_rows(here, block, size):
    return pl.ds(pl.multiple_of((here ^ block) * size, size), size)


def causal_mask(scores, size):
    key = lax.broadcasted_iota(jnp.int32, scores.shape, 0)
    query = lax.broadcasted_iota(jnp.int32, scores.shape, 1)
    return jnp.where(key <= lax.rem(query, size), scores, NEG)


def self_forward_kernel(here_ref, q_ref, k_ref, v_ref, o_ref, log_ref, *, blocks):
    here = here_ref[0]
    size = q_ref.shape[0] // blocks
    for p in range(blocks):
        rows = block_rows(here, p, size)
        queries = two_heads(q_ref[rows, :] * BF(SCALE))
        scores = []
        for j in range(p + 1):
            s = dot(k_ref[block_rows(here, j, size), :], queries, 1, 1)
            scores.append(causal_mask(s, size) if j == p else s)
        top = scores[0].max(0, keepdims=True)
        for s in scores[1:]:
            top = jnp.maximum(top, s.max(0, keepdims=True))
        total = jnp.zeros_like(top)
        mixed = [jnp.zeros((HEAD_DIM, size), F32)] * 2
        for j in range(p + 1):
            e = jnp.exp(scores[j] - top)
            total = total + e.sum(0, keepdims=True)
            low = e.astype(BF)
            values = v_ref[block_rows(here, j, size), :].T
            for h in range(2):
                mixed[h] = mixed[h] + dot(
                    values[h * HEAD_DIM : (h + 1) * HEAD_DIM],
                    low[:, h * size : (h + 1) * size],
                    1,
                    0,
                )
        inverse = 1.0 / total
        both = jnp.concatenate(
            [mixed[h] * inverse[:, h * size : (h + 1) * size] for h in range(2)], 0
        )
        o_ref[rows, :] = both.T.astype(BF)
        log_ref[0, :, 2 * size * p : 2 * size * (p + 1)] = top + jnp.log(total)


def row_dots(left, right):
    product = left.astype(F32).T * right.astype(F32).T
    return jnp.concatenate(
        [product[:HEAD_DIM].sum(0, keepdims=True), product[HEAD_DIM:].sum(0, keepdims=True)], 1
    )


def self_backward_kernel(
    here_ref, q_ref, k_ref, v_ref, o_ref, do_ref, log_ref, dq_ref, dk_ref, dv_ref, *, blocks
):
    here = here_ref[0]
    size = q_ref.shape[0] // blocks
    queries, grads, inner, dq = [], [], [], []
    for p in range(blocks):
        rows = block_rows(here, p, size)
        queries.append(two_heads(q_ref[rows, :] * BF(SCALE)))
        grads.append(two_heads(do_ref[rows, :]))
        inner.append(row_dots(do_ref[rows, :], o_ref[rows, :]))
        dq.append([jnp.zeros((HEAD_DIM, size), F32)] * 2)
    for j in range(blocks):
        rows = block_rows(here, j, size)
        keys, values = k_ref[rows, :], v_ref[rows, :]
        turned = keys.T
        dk = jnp.zeros(keys.shape, F32)
        dv = jnp.zeros(keys.shape, F32)
        for p in range(j, blocks):
            s = dot(keys, queries[p], 1, 1)
            if j == p:
                s = causal_mask(s, size)
            probs = jnp.exp(s - log_ref[0, :, 2 * size * p : 2 * size * (p + 1)])
            dprobs = dot(values, grads[p], 1, 1)
            ds = (probs * (dprobs - inner[p])).astype(BF)
            dv = dv + dot(probs.astype(BF), grads[p], 1, 0)
            dk = dk + dot(ds, queries[p], 1, 0)
            for h in range(2):
                dq[p][h] = dq[p][h] + dot(
                    turned[h * HEAD_DIM : (h + 1) * HEAD_DIM],
                    ds[:, h * size : (h + 1) * size],
                    1,
                    0,
                )
        dk_ref[rows, :] = dk.astype(BF)
        dv_ref[rows, :] = dv.astype(BF)
    for p in range(blocks):
        both = jnp.concatenate(dq[p], 0) * SCALE
        dq_ref[block_rows(here, p, size), :] = both.T.astype(BF)


def pair_spec(rows):
    return pl.BlockSpec((rows, PAIR), lambda i, *_: (0, i))


def log_spec(width):
    return pl.BlockSpec((1, 1, width), lambda i, *_: (i, 0, 0))


def self_forward(here, q, k, v, blocks):
    rows, width = q.shape
    pairs = width // PAIR
    spec = pair_spec(rows)
    return pl.pallas_call(
        lambda *refs: self_forward_kernel(*refs, blocks=blocks),
        name="self_forward",
        out_shape=(
            jax.ShapeDtypeStruct((rows, width), BF),
            jax.ShapeDtypeStruct((pairs, 1, 2 * rows), F32),
        ),
        grid_spec=pltpu.PrefetchScalarGridSpec(
            num_scalar_prefetch=1,
            grid=(pairs,),
            in_specs=[spec] * 3,
            out_specs=(spec, log_spec(2 * rows)),
        ),
        compiler_params=pltpu.CompilerParams(vmem_limit_bytes=VMEM),
        cost_estimate=pl.CostEstimate(
            flops=10 * pairs * rows * rows * PAIR,
            bytes_accessed=8 * rows * width,
            transcendentals=pairs * rows * rows,
        ),
    )(here, q, k, v)


def self_backward(here, q, k, v, o, do, log_total, blocks):
    rows, width = q.shape
    pairs = width // PAIR
    spec = pair_spec(rows)
    return pl.pallas_call(
        lambda *refs: self_backward_kernel(*refs, blocks=blocks),
        name="self_backward",
        out_shape=(jax.ShapeDtypeStruct((rows, width), BF),) * 3,
        grid_spec=pltpu.PrefetchScalarGridSpec(
            num_scalar_prefetch=1,
            grid=(pairs,),
            in_specs=[spec] * 5 + [log_spec(2 * rows)],
            out_specs=(spec,) * 3,
        ),
        compiler_params=pltpu.CompilerParams(vmem_limit_bytes=VMEM),
        cost_estimate=pl.CostEstimate(
            flops=20 * pairs * rows * rows * PAIR,
            bytes_accessed=16 * rows * width,
            transcendentals=pairs * rows * rows,
        ),
    )(here, q, k, v, o, do, log_total)


def cross_forward_kernel(live_ref, q_ref, k_ref, v_ref, o_ref, log_ref):
    size = q_ref.shape[0]
    queries = two_heads(q_ref[...] * BF(SCALE))
    s = dot(k_ref[...], queries, 1, 1)
    s = jnp.where(live_ref[...] > 0, s, NEG)
    top = s.max(0, keepdims=True)
    e = jnp.exp(s - top)
    total = e.sum(0, keepdims=True)
    low = e.astype(BF)
    values = v_ref[...].T
    inverse = 1.0 / total
    both = jnp.concatenate(
        [
            dot(
                values[h * HEAD_DIM : (h + 1) * HEAD_DIM],
                low[:, h * size : (h + 1) * size],
                1,
                0,
            )
            * inverse[:, h * size : (h + 1) * size]
            for h in range(2)
        ],
        0,
    )
    o_ref[...] = both.T.astype(BF)
    log_ref[0] = top + jnp.log(total)


def cross_backward_kernel(
    live_ref, q_ref, k_ref, v_ref, o_ref, do_ref, log_ref, dq_ref, dk_ref, dv_ref
):
    size = q_ref.shape[0]
    queries = two_heads(q_ref[...] * BF(SCALE))
    grads = two_heads(do_ref[...])
    inner = row_dots(do_ref[...], o_ref[...])
    keys = k_ref[...]
    s = dot(keys, queries, 1, 1)
    s = jnp.where(live_ref[...] > 0, s, NEG)
    probs = jnp.exp(s - log_ref[0])
    dprobs = dot(v_ref[...], grads, 1, 1)
    ds = (probs * (dprobs - inner)).astype(BF)
    dv_ref[...] = dot(probs.astype(BF), grads, 1, 0).astype(BF)
    dk_ref[...] = dot(ds, queries, 1, 0).astype(BF)
    turned = keys.T
    both = jnp.concatenate(
        [
            dot(
                turned[h * HEAD_DIM : (h + 1) * HEAD_DIM],
                ds[:, h * size : (h + 1) * size],
                1,
                0,
            )
            for h in range(2)
        ],
        0,
    )
    dq_ref[...] = (both * SCALE).T.astype(BF)


def cross_forward(live, q, k, v):
    rows, width = q.shape
    slots = k.shape[0]
    pairs = width // PAIR
    return pl.pallas_call(
        cross_forward_kernel,
        name="cross_forward",
        out_shape=(
            jax.ShapeDtypeStruct((rows, width), BF),
            jax.ShapeDtypeStruct((pairs, 1, 2 * rows), F32),
        ),
        grid=(pairs,),
        in_specs=[
            pl.BlockSpec((slots, 1), lambda i: (0, 0)),
            pair_spec(rows),
            pair_spec(slots),
            pair_spec(slots),
        ],
        out_specs=(pair_spec(rows), log_spec(2 * rows)),
        compiler_params=pltpu.CompilerParams(vmem_limit_bytes=VMEM),
        cost_estimate=pl.CostEstimate(
            flops=16 * pairs * rows * slots * PAIR,
            bytes_accessed=4 * (rows + slots) * width,
            transcendentals=2 * pairs * rows * slots,
        ),
    )(live, q, k, v)


def cross_backward(live, q, k, v, o, do, log_total):
    rows, width = q.shape
    slots = k.shape[0]
    pairs = width // PAIR
    return pl.pallas_call(
        cross_backward_kernel,
        name="cross_backward",
        out_shape=(
            jax.ShapeDtypeStruct((rows, width), BF),
            jax.ShapeDtypeStruct((slots, width), BF),
            jax.ShapeDtypeStruct((slots, width), BF),
        ),
        grid=(pairs,),
        in_specs=[
            pl.BlockSpec((slots, 1), lambda i: (0, 0)),
            pair_spec(rows),
            pair_spec(slots),
            pair_spec(slots),
            pair_spec(rows),
            pair_spec(rows),
            log_spec(2 * rows),
        ],
        out_specs=(pair_spec(rows), pair_spec(slots), pair_spec(slots)),
        compiler_params=pltpu.CompilerParams(vmem_limit_bytes=VMEM),
        cost_estimate=pl.CostEstimate(
            flops=40 * pairs * rows * slots * PAIR,
            bytes_accessed=8 * (rows + slots) * width,
            transcendentals=2 * pairs * rows * slots,
        ),
    )(live, q, k, v, o, do, log_total)


def standardize(rows):
    centered = rows - jnp.mean(rows, -1, keepdims=True)
    inverse = lax.rsqrt(jnp.mean(centered * centered, -1, keepdims=True) + 1e-05)
    return centered * inverse, inverse


def norm_back(grad_out, gain, unit_rows, inverse):
    grad_unit = grad_out * gain
    grad_in = inverse * (
        grad_unit
        - jnp.mean(grad_unit, -1, keepdims=True)
        - unit_rows * jnp.mean(grad_unit * unit_rows, -1, keepdims=True)
    )
    return grad_in, jnp.sum(grad_out * unit_rows, 0), jnp.sum(grad_out, 0)


def gelu_and_slope(pre):
    square = pre * pre
    bend = jnp.tanh(0.7978845608028654 * pre * (1.0 + 0.044715 * square))
    half = 0.5 * (1.0 + bend)
    slope = half + 0.5 * pre * (1.0 - bend * bend) * (
        0.7978845608028654 * (1.0 + 3.0 * 0.044715 * square)
    )
    return pre * half, slope


def body(
    image_tokens,
    text_states,
    caption_lengths,
    text_mask,
    self_qkv,
    self_out,
    cross_query,
    cross_kv,
    cross_out,
    mlp_in,
    mlp_out,
    norm_gains,
    norm_shifts,
    out_biases,
    mlp_bias,
    cotangent,
):
    _, block, width = image_tokens.shape
    blocks = lax.axis_size("narrow")
    wide_size = lax.axis_size("wide")
    here = lax.axis_index("narrow")
    line = lax.axis_index("wide")
    chip, core = here // 2, here % 2
    wide_bits = wide_size.bit_length() - 1
    mates = [(i, i ^ 1) for i in range(blocks)]
    across = [(i, i ^ 2) for i in range(blocks)]

    def to_mate(value):
        return lax.ppermute(value, "narrow", mates)

    def to_chip(value):
        return lax.ppermute(value, "narrow", across)

    def item(array, index):
        return lax.dynamic_index_in_dim(array, index, 0, keepdims=False)

    def woven(own, other):
        half = own.shape[0] // 2
        return jnp.concatenate([own[:half], other[:half], own[half:], other[half:]], 0)

    def columns(array, side):
        quarter = array.shape[-1] // 4
        return jnp.concatenate(
            [
                lax.dynamic_slice_in_dim(array, (2 * k + side) * quarter, quarter, array.ndim - 1)
                for k in range(2)
            ],
            -1,
        )

    def chosen(first, second):
        return jnp.where(core == 0, first, second), jnp.where(core == 0, second, first)

    def exchange(value, axis):
        if axis == "x":
            return to_chip(value)
        return lax.ppermute(value, "wide", [(i, i ^ (1 << axis)) for i in range(wide_size)])

    def scatter_sum(partial, order):
        rows, cols = partial.shape
        held = [partial.reshape((2,) * wide_bits + (rows // wide_size, cols))]

        def take(value, axis, mine):
            bit = chip if axis == "x" else (line >> axis) & 1
            bit = bit if mine else 1 - bit
            if axis == "x":
                return lax.dynamic_slice_in_dim(value, bit * (cols // 2), cols // 2, value.ndim - 1)
            return lax.dynamic_slice_in_dim(value, bit, 1, wide_bits - 1 - axis)

        for axis in order:
            sent = sum(take(h, axis, False).astype(F32) for h in held).astype(BF)
            held = [take(h, axis, True) for h in held] + [exchange(sent, axis)]
        total = sum(h.astype(F32) for h in held)
        return total.reshape(rows // wide_size, cols // 2)

    near = list(range(wide_bits))
    order_x = ["x"] + near
    order_y = near[:1] + ["x"] + near[1:]
    order_z = near[1:] + near[:1] + ["x"]

    def weight_grad(left, right, order):
        return scatter_sum(dot(left, right, 0, 0).astype(BF), order)

    x_own = item(image_tokens, chip)
    x_far = to_chip(item(image_tokens, 1 - chip))
    x_mate = to_mate(x_own)
    x_mate_far = to_mate(x_far)
    text_own = item(text_states, chip)
    text_far = to_chip(item(text_states, 1 - chip))
    text_two = jnp.concatenate([text_own, text_far], 0)
    text_all = jnp.concatenate(chosen(text_two, to_mate(text_two)), 0)
    slot_block = text_own.shape[0]
    slots = slot_block * blocks
    slot_order = jnp.stack([(2 * chip) ^ k for k in (0, 2, 1, 3)])
    slot = (slot_order[:, None] * slot_block + jnp.arange(slot_block)[None, :]).reshape(slots)
    kept = item(text_mask, chip).reshape(blocks, slot_block)
    kept = jnp.concatenate([item(kept, (2 * chip) ^ k) for k in (0, 2, 1, 3)], 0)
    length = item(caption_lengths, chip)
    live = ((slot < length) & ((kept == 1) | (slot == 0))).astype(F32).reshape(slots, 1)
    cot_own = item(cotangent, chip)
    cot_far = to_chip(item(cotangent, 1 - chip))
    e3 = jnp.concatenate([cot_own, cot_far], 0)

    x = jnp.concatenate([x_own, x_far], 0).astype(F32)
    x_full = jnp.concatenate([x_own, x_mate, x_far, x_mate_far], 0).astype(F32)
    unit_full, _ = standardize(x_full)
    a_full = (unit_full * norm_gains[0] + norm_shifts[0]).astype(BF)

    w_qkv_own, w_qkv_mate = columns(self_qkv, core), columns(self_qkv, 1 - core)
    def head_rows(side):
        quarter = width // 4
        return jnp.concatenate(
            [
                lax.dynamic_slice_in_dim(self_out, (2 * k + side) * quarter, quarter, 0)
                for k in range(2)
            ],
            0,
        )

    w_out_own, w_out_mate = head_rows(core), head_rows(1 - core)

    q, k, v = (dot(a_full, w_qkv_own[j], 1, 0).astype(BF) for j in range(3))
    place = here.reshape(1).astype(jnp.int32)
    os_heads, log_self = self_forward(place, q, k, v, blocks)

    def own_rows(array):
        return jnp.concatenate([array[:block], array[2 * block : 3 * block]], 0)

    def mate_rows(array):
        return jnp.concatenate([array[block : 2 * block], array[3 * block :]], 0)

    os_own = own_rows(os_heads)
    os_other = to_mate(mate_rows(os_heads))
    h1 = (
        x
        + dot(os_own, w_out_own, 1, 0)
        + dot(os_other, w_out_mate, 1, 0)
        + out_biases[0]
    )
    first, second = chosen(os_own, os_other)
    half = width // 4
    os_rows = jnp.concatenate([first[:, :half], second[:, :half], first[:, half:], second[:, half:]], 1)
    os_full = woven(os_rows, to_mate(os_rows))

    unit_two, inverse_two = standardize(h1)
    c = (unit_two * norm_gains[1] + norm_shifts[1]).astype(BF)
    qc = dot(c, cross_query, 1, 0).astype(BF)
    tk = dot(text_all, cross_kv[0], 1, 0).astype(BF)
    tv = dot(text_all, cross_kv[1], 1, 0).astype(BF)
    oc, log_cross = cross_forward(live, qc, tk, tv)
    h2 = h1 + dot(oc, cross_out, 1, 0) + out_biases[1]
    c_full = woven(c, to_mate(c))
    oc_full = woven(oc, to_mate(oc))

    unit_three, inverse_three = standardize(h2)
    m = (unit_three * norm_gains[2] + norm_shifts[2]).astype(BF)
    m_full = woven(m, to_mate(m))
    g, slope = gelu_and_slope(dot(m, mlp_in, 1, 0) + mlp_bias)
    g, slope = g.astype(BF), slope.astype(BF)
    g_full = woven(g, to_mate(g))
    layer_out = h2 + dot(g, mlp_out, 1, 0) + out_biases[2]

    e3_cols = woven(columns(e3, core), to_mate(columns(e3, 1 - core)))
    part_down = weight_grad(g_full, e3_cols, order_y)
    dpre = (dot(e3, mlp_out, 1, 1).astype(BF).astype(F32) * slope.astype(F32)).astype(BF)
    dpre_cols = woven(columns(dpre, core), to_mate(columns(dpre, 1 - core)))
    part_up = weight_grad(m_full, dpre_cols, order_z)
    grad_three, gain_three, shift_three = norm_back(
        dot(dpre, mlp_in, 1, 1), norm_gains[2], unit_three, inverse_three
    )
    e2 = e3.astype(F32) + grad_three
    f2 = e2.astype(BF)

    f2_cols = woven(columns(f2, core), to_mate(columns(f2, 1 - core)))
    part_cout = weight_grad(oc_full, f2_cols, order_x)
    doc = dot(f2, cross_out, 1, 1).astype(BF)
    dqc, dtk, dtv = cross_backward(live, qc, tk, tv, oc, doc, log_cross)
    dt = jnp.stack([dtk, dtv])
    dt = (dt.astype(F32) + to_mate(dt).astype(F32)).astype(BF)
    part_ckv = [
        weight_grad(text_all, columns(dt[j], core), order) for j, order in ((0, order_x), (1, order_z))
    ]
    dt_own = lax.dynamic_slice_in_dim(dt, core * 2 * slot_block, 2 * slot_block, 1)
    grad_text = dot(dt_own[0], cross_kv[0], 1, 1) + dot(dt_own[1], cross_kv[1], 1, 1)
    dqc_cols = woven(columns(dqc, core), to_mate(columns(dqc, 1 - core)))
    part_cq = weight_grad(c_full, dqc_cols, order_y)
    grad_two, gain_two, shift_two = norm_back(
        dot(dqc, cross_query, 1, 1), norm_gains[1], unit_two, inverse_two
    )
    e1 = e2 + grad_two
    f1 = e1.astype(BF)

    do_own = dot(f1, w_out_own, 1, 1).astype(BF)
    do_far = to_mate(dot(f1, w_out_mate, 1, 1).astype(BF))
    do_heads = woven(do_own, do_far)
    dq, dk, dv = self_backward(place, q, k, v, os_heads, do_heads, log_self, blocks)
    d_other = to_mate(jnp.stack([mate_rows(d) for d in (dq, dk, dv)]))
    part_qkv = [
        weight_grad(a_full, d, order)
        for d, order in ((dq, order_x), (dk, order_y), (dv, order_z))
    ]
    f1_cols = woven(columns(f1, core), to_mate(columns(f1, 1 - core)))
    part_sout = weight_grad(os_full, f1_cols, order_y)
    grad_a = sum(dot(own_rows(d), w_qkv_own[j], 1, 1) for j, d in enumerate((dq, dk, dv)))
    grad_a = grad_a + sum(dot(d_other[j], w_qkv_mate[j], 1, 1) for j in range(3))
    unit_one, inverse_one = standardize(x)
    grad_one, gain_one, shift_one = norm_back(grad_a, norm_gains[0], unit_one, inverse_one)
    grad_rows = e1 + grad_one

    def home(rows):
        half = rows.shape[0] // 2
        own, far = rows[:half], to_chip(rows[half:].astype(BF)).astype(F32)
        return jnp.stack([jnp.where(chip == 0, own, far), jnp.where(chip == 0, far, own)])

    def column_sum(rows):
        return jnp.sum(rows.astype(F32), 0)

    def all_sum(value):
        value = value + to_mate(value)
        value = value + to_chip(value)
        for bit in near:
            value = value + exchange(value, bit)
        return value

    early = all_sum(
        jnp.concatenate(
            [
                jnp.stack(
                    [gain_two, gain_three, shift_two, shift_three]
                    + [column_sum(v) for v in (f1, f2, e3)]
                ),
                column_sum(dpre).reshape(-1, width),
            ]
        )
    )
    late = all_sum(jnp.stack([gain_one, shift_one]))
    gains = jnp.stack([late[0], early[0], early[1]])
    shifts = jnp.stack([late[1], early[2], early[3]])
    return (
        home(layer_out),
        home(grad_rows),
        home(grad_text),
        jnp.stack(part_qkv),
        part_sout,
        part_cq,
        jnp.stack(part_ckv),
        part_cout,
        part_up,
        part_down,
        gains,
        shifts,
        early[4:7],
        early[7:].reshape(-1),
    )


def solution(mesh):
    rows = P("wide", "narrow", None)
    whole = P()
    return jax.shard_map(
        body,
        mesh=mesh,
        in_specs=(rows, rows, P("wide"), P("wide", None)) + (whole,) * 11 + (rows,),
        out_specs=(rows,) * 3
        + (
            P(None, "wide", "narrow"),
            P("wide", "narrow"),
            P("wide", "narrow"),
            P(None, "wide", "narrow"),
        )
        + (P("wide", "narrow"),) * 3
        + (whole,) * 4,
        check_vma=False,
    )
```

```python
import jax
import jax.numpy as jnp
from jax import lax
from jax.experimental import pallas as pl
from jax.experimental.pallas import tpu as pltpu
from jax.sharding import PartitionSpec as P

HEAD_DIM = 64
PAIR = 2 * HEAD_DIM
SCALE = HEAD_DIM**-0.5
NEG = -1e30
BF = jnp.bfloat16
F32 = jnp.float32
VMEM = 56 * 1024 * 1024
TILE = 512


def dot(left, right, left_axis, right_axis):
    return lax.dot_general(
        left, right, (((left_axis,), (right_axis,)), ((), ())), preferred_element_type=F32
    )


def two_heads(rows):
    lane = lax.broadcasted_iota(jnp.int32, rows.shape, 1)
    zero = jnp.zeros_like(rows)
    return jnp.concatenate(
        [jnp.where(lane < HEAD_DIM, rows, zero), jnp.where(lane < HEAD_DIM, zero, rows)], 0
    )


def block_rows(here, block, size):
    slot = here ^ block
    return pl.ds(pl.multiple_of(((slot & 1) * 2 + slot // 2) * size, size), size)


def slot_place(here, block, size):
    slot = here ^ block
    return slot & 1, pl.ds(pl.multiple_of((slot // 2) * size, size), size)


def causal_mask(scores, size):
    key = lax.broadcasted_iota(jnp.int32, scores.shape, 0)
    query = lax.broadcasted_iota(jnp.int32, scores.shape, 1)
    return jnp.where(key <= lax.rem(query, size), scores, NEG)


def self_forward_kernel(here_ref, q_ref, k_ref, v_ref, o_ref, log_ref, *, blocks):
    here = here_ref[0]
    size = q_ref.shape[0] // blocks
    for p in range(blocks):
        rows = block_rows(here, p, size)
        queries = two_heads(q_ref[rows, :] * BF(SCALE))
        scores = []
        for j in range(p + 1):
            s = dot(k_ref[block_rows(here, j, size), :], queries, 1, 1)
            scores.append(causal_mask(s, size) if j == p else s)
        top = scores[0].max(0, keepdims=True)
        for s in scores[1:]:
            top = jnp.maximum(top, s.max(0, keepdims=True))
        total = jnp.zeros_like(top)
        mixed = [jnp.zeros((HEAD_DIM, size), F32)] * 2
        for j in range(p + 1):
            e = jnp.exp(scores[j] - top)
            total = total + e.sum(0, keepdims=True)
            low = e.astype(BF)
            values = v_ref[block_rows(here, j, size), :].T
            for h in range(2):
                mixed[h] = mixed[h] + dot(
                    values[h * HEAD_DIM : (h + 1) * HEAD_DIM],
                    low[:, h * size : (h + 1) * size],
                    1,
                    0,
                )
        inverse = 1.0 / total
        both = jnp.concatenate(
            [mixed[h] * inverse[:, h * size : (h + 1) * size] for h in range(2)], 0
        )
        side, half = slot_place(here, p, size)
        o_ref[side, half, :] = both.T.astype(BF)
        log_ref[0, :, 2 * size * p : 2 * size * (p + 1)] = top + jnp.log(total)


def row_dots(left, right):
    product = left.astype(F32).T * right.astype(F32).T
    return jnp.concatenate(
        [product[:HEAD_DIM].sum(0, keepdims=True), product[HEAD_DIM:].sum(0, keepdims=True)], 1
    )


def self_backward_kernel(
    here_ref,
    q_ref,
    k_ref,
    v_ref,
    o_ref,
    do_ref,
    do_mate_ref,
    log_ref,
    d_ref,
    *,
    blocks,
):
    here = here_ref[0]
    size = q_ref.shape[0] // blocks
    queries, grads, inner, dq = [], [], [], []
    for p in range(blocks):
        rows = block_rows(here, p, size)
        queries.append(two_heads(q_ref[rows, :] * BF(SCALE)))
        side, half = slot_place(here, p, size)
        do = jnp.where(side == 0, do_ref[half, :], do_mate_ref[half, :])
        grads.append(two_heads(do))
        inner.append(row_dots(do, o_ref[side, half, :]))
        dq.append([jnp.zeros((HEAD_DIM, size), F32)] * 2)
    for j in range(blocks):
        rows = block_rows(here, j, size)
        keys, values = k_ref[rows, :], v_ref[rows, :]
        turned = keys.T
        dk = jnp.zeros(keys.shape, F32)
        dv = jnp.zeros(keys.shape, F32)
        for p in range(j, blocks):
            s = dot(keys, queries[p], 1, 1)
            if j == p:
                s = causal_mask(s, size)
            probs = jnp.exp(s - log_ref[0, :, 2 * size * p : 2 * size * (p + 1)])
            dprobs = dot(values, grads[p], 1, 1)
            ds = (probs * (dprobs - inner[p])).astype(BF)
            dv = dv + dot(probs.astype(BF), grads[p], 1, 0)
            dk = dk + dot(ds, queries[p], 1, 0)
            for h in range(2):
                dq[p][h] = dq[p][h] + dot(
                    turned[h * HEAD_DIM : (h + 1) * HEAD_DIM],
                    ds[:, h * size : (h + 1) * size],
                    1,
                    0,
                )
        side, half = slot_place(here, j, size)
        d_ref[side, 1, half, :] = dk.astype(BF)
        d_ref[side, 2, half, :] = dv.astype(BF)
    for p in range(blocks):
        both = jnp.concatenate(dq[p], 0) * SCALE
        side, half = slot_place(here, p, size)
        d_ref[side, 0, half, :] = both.T.astype(BF)


def pair_spec(rows):
    return pl.BlockSpec((rows, PAIR), lambda i, *_: (0, i))


def sides_spec(rows):
    return pl.BlockSpec((2, rows, PAIR), lambda i, *_: (0, 0, i))


def log_spec(width):
    return pl.BlockSpec((1, 1, width), lambda i, *_: (i, 0, 0))


def self_forward(here, q, k, v, blocks):
    rows, width = q.shape
    pairs = width // PAIR
    spec = pair_spec(rows)
    return pl.pallas_call(
        lambda *refs: self_forward_kernel(*refs, blocks=blocks),
        name="self_forward",
        out_shape=(
            jax.ShapeDtypeStruct((2, rows // 2, width), BF),
            jax.ShapeDtypeStruct((pairs, 1, 2 * rows), F32),
        ),
        grid_spec=pltpu.PrefetchScalarGridSpec(
            num_scalar_prefetch=1,
            grid=(pairs,),
            in_specs=[spec] * 3,
            out_specs=(sides_spec(rows // 2), log_spec(2 * rows)),
        ),
        compiler_params=pltpu.CompilerParams(vmem_limit_bytes=VMEM),
        cost_estimate=pl.CostEstimate(flops=10**6, bytes_accessed=10**5, transcendentals=0),
    )(here, q, k, v)


def self_backward(here, q, k, v, o, do, do_mate, log_total, blocks):
    rows, width = q.shape
    pairs = width // PAIR
    spec = pair_spec(rows)
    return pl.pallas_call(
        lambda *refs: self_backward_kernel(*refs, blocks=blocks),
        name="self_backward",
        out_shape=jax.ShapeDtypeStruct((2, 3, rows // 2, width), BF),
        grid_spec=pltpu.PrefetchScalarGridSpec(
            num_scalar_prefetch=1,
            grid=(pairs,),
            in_specs=[spec] * 3
            + [sides_spec(rows // 2)]
            + [pair_spec(rows // 2)] * 2
            + [log_spec(2 * rows)],
            out_specs=pl.BlockSpec((2, 3, rows // 2, PAIR), lambda i, *_: (0, 0, 0, i)),
        ),
        compiler_params=pltpu.CompilerParams(vmem_limit_bytes=VMEM),
        cost_estimate=pl.CostEstimate(flops=10**6, bytes_accessed=10**5, transcendentals=0),
    )(here, q, k, v, o, do, do_mate, log_total)


def standardize(rows):
    centered = rows - jnp.mean(rows, -1, keepdims=True)
    inverse = lax.rsqrt(jnp.mean(centered * centered, -1, keepdims=True) + 1e-05)
    return centered * inverse, inverse


def normed(rows, gain, shift):
    return (standardize(rows)[0] * gain + shift).astype(BF)


def norm_back(grad_out, gain, rows):
    unit, inverse = standardize(rows)
    grad_unit = grad_out * gain
    grad_in = inverse * (
        grad_unit
        - jnp.mean(grad_unit, -1, keepdims=True)
        - unit * jnp.mean(grad_unit * unit, -1, keepdims=True)
    )
    return grad_in, column_sum(grad_out * unit), column_sum(grad_out)


def column_sum(rows):
    return jnp.sum(rows.astype(F32), 0, keepdims=True)


def gelu_and_slope(pre):
    square = pre * pre
    bend = jnp.tanh(pre * (0.7978845608028654 + (0.7978845608028654 * 0.044715) * square))
    half = 0.5 + 0.5 * bend
    value = pre * half
    steep = 0.7978845608028654 + (3.0 * 0.7978845608028654 * 0.044715) * square
    return value, half + value * (1.0 - bend) * steep


def whole_spec(shape):
    return pl.BlockSpec(shape, lambda *_: (0,) * len(shape))


def row_spec(rows, cols, start=0):
    return pl.BlockSpec((rows, cols), lambda i, *_: (start + i, 0))


def call(kernel, name, out_shape, grid, in_specs, out_specs, scratch=(), aliases=None):
    return pl.pallas_call(
        kernel,
        name=name,
        out_shape=out_shape,
        grid_spec=pltpu.PrefetchScalarGridSpec(
            num_scalar_prefetch=1,
            grid=grid,
            in_specs=in_specs,
            out_specs=out_specs,
            scratch_shapes=scratch,
        ),
        input_output_aliases=aliases or {},
        compiler_params=pltpu.CompilerParams(vmem_limit_bytes=VMEM),
        cost_estimate=pl.CostEstimate(flops=10**6, bytes_accessed=10**5, transcendentals=0),
    )


def out_struct(rows, cols, kind=BF):
    return jax.ShapeDtypeStruct((rows, cols), kind)


def project(place, own, mate, qkv, gains, shifts, half, size, into):
    width = qkv.shape[1]
    quarter = width // 4

    def kernel(place_ref, own_ref, mate_ref, gain_ref, shift_ref, *refs):
        weights, outs = refs[:6], refs[-4:]
        rows = jnp.where(pl.program_id(0) == 0, own_ref[...], mate_ref[...]).astype(F32)
        a = normed(rows, gain_ref[0:1], shift_ref[0:1])
        outs[0][...] = a
        for j in range(3):
            pair = jnp.concatenate([weights[2 * j][0], weights[2 * j + 1][0]], 1)
            outs[1 + j][...] = dot(a, pair, 1, 0).astype(BF)

    def weight_spec(j, k):
        return pl.BlockSpec((1, width, quarter), lambda i, place: (j, 0, 2 * k + place[1]))

    def out_spec(cols):
        return pl.BlockSpec((size, cols), lambda i, place: (2 * i + half, 0))

    specs = [whole_spec((size, width))] * 2 + [whole_spec(gains.shape)] * 2
    specs += [weight_spec(j, k) for j in range(3) for k in range(2)]
    arrays = [own, mate, gains, shifts] + [qkv] * 6
    aliases = None
    if into is not None:
        aliases = {1 + len(arrays) + n: n for n in range(4)}
        arrays += list(into)
        specs += [pl.BlockSpec(memory_space=pl.ANY)] * 4
    rows = 4 * size
    return call(
        kernel,
        "project",
        (out_struct(rows, width),) + (out_struct(rows, width // 2),) * 3,
        (2,),
        specs,
        (out_spec(width),) + (out_spec(width // 2),) * 3,
        aliases=aliases,
    )(place, *arrays)


def head_row_specs(width):
    quarter = width // 4
    return [
        pl.BlockSpec((quarter, width), lambda i, place, k=k, flip=flip: (2 * k + (place[1] ^ flip), 0))
        for flip in range(2)
        for k in range(2)
    ]


def middle_forward(place, live, x, o, o_other, self_out, gains, shifts, biases, wq, tk, tv, wo, size):
    rows, width = x.shape
    quarter, slots, steps = width // 4, tk.shape[0], rows // size

    def kernel(
        place_ref,
        live_ref,
        x_ref,
        o_ref,
        other_ref,
        w0,
        w1,
        w2,
        w3,
        gain_ref,
        shift_ref,
        bias_ref,
        wq_ref,
        tk_ref,
        tv_ref,
        wo_ref,
        os_ref,
        h1_ref,
        c_ref,
        qc_ref,
        oc_ref,
        log_ref,
        h2_ref,
        m_ref,
    ):
        core = place_ref[1]
        h1 = x_ref[...].astype(F32) + bias_ref[0:1]
        for n, (ref, weight) in enumerate(
            ((o_ref, w0), (o_ref, w1), (other_ref, w2), (other_ref, w3))
        ):
            k, side = n % 2, core ^ (n // 2)
            part = ref[:, k * quarter : (k + 1) * quarter]
            at = pl.multiple_of((2 * k + side) * quarter, quarter)
            os_ref[:, pl.ds(at, quarter)] = part
            h1 = h1 + dot(part, weight[...], 1, 0)
        h1_ref[...] = h1
        c = normed(h1, gain_ref[1:2], shift_ref[1:2])
        c_ref[...] = c
        qc_ref[...] = dot(c, wq_ref[...], 1, 0).astype(BF)
        for pair in range(width // PAIR):
            lanes = slice(pair * PAIR, (pair + 1) * PAIR)
            queries = two_heads(qc_ref[:, lanes] * BF(SCALE))
            s = dot(tk_ref[:, lanes], queries, 1, 1)
            s = jnp.where(live_ref[...] > 0, s, NEG)
            top = s.max(0, keepdims=True)
            e = jnp.exp(s - top)
            total = e.sum(0, keepdims=True)
            low = e.astype(BF)
            values = tv_ref[:, lanes].T
            inverse = 1.0 / total
            both = jnp.concatenate(
                [
                    dot(
                        values[h * HEAD_DIM : (h + 1) * HEAD_DIM],
                        low[:, h * size : (h + 1) * size],
                        1,
                        0,
                    )
                    * inverse[:, h * size : (h + 1) * size]
                    for h in range(2)
                ],
                0,
            )
            oc_ref[:, lanes] = both.T.astype(BF)
            log_ref[0, pair : pair + 1] = top + jnp.log(total)
        h2 = h1 + dot(oc_ref[...], wo_ref[...], 1, 0) + bias_ref[1:2]
        h2_ref[...] = h2
        m_ref[...] = normed(h2, gain_ref[2:3], shift_ref[2:3])

    row = row_spec(size, width)
    square = whole_spec((width, width))
    low, high = out_struct(rows, width), out_struct(rows, width, F32)
    pairs = width // PAIR
    return call(
        kernel,
        "middle_forward",
        (low, high, low, low, low, jax.ShapeDtypeStruct((steps, pairs, 2 * size), F32), high, low),
        (steps,),
        [
            whole_spec((slots, 1)),
            row,
            pl.BlockSpec((None, size, width // 2), lambda i, *_: (0, i, 0)),
            row_spec(size, width // 2),
        ]
        + head_row_specs(width)
        + [whole_spec(gains.shape)] * 3
        + [square, whole_spec((slots, width)), whole_spec((slots, width)), square],
        (row,) * 5 + (pl.BlockSpec((1, pairs, 2 * size), lambda i, *_: (i, 0, 0)), row, row),
    )(place, live, x, o, o_other, *[self_out] * 4, gains, shifts, biases, wq, tk, tv, wo)


def middle_backward(
    place, live, dm, e3, h1, h2, qc, oc, logs, self_out, gains, wq, tk, tv, wo, size
):
    rows, width = h1.shape
    quarter, slots, steps = width // 4, tk.shape[0], rows // size

    def kernel(
        place_ref,
        live_ref,
        dm_ref,
        e3_ref,
        h1_ref,
        h2_ref,
        qc_ref,
        oc_ref,
        log_ref,
        w0,
        w1,
        w2,
        w3,
        gain_ref,
        wq_ref,
        tk_ref,
        tv_ref,
        wo_ref,
        f2_ref,
        dqc_ref,
        f1_ref,
        e1_ref,
        do_ref,
        other_ref,
        cols_ref,
        dt_ref,
        sum_ref,
        doc_ref,
        dtk_sum,
        dtv_sum,
    ):
        first = pl.program_id(0) == 0

        @pl.when(first)
        def _():
            dtk_sum[...] = jnp.zeros_like(dtk_sum)
            dtv_sum[...] = jnp.zeros_like(dtv_sum)

        e3 = e3_ref[...].astype(F32)
        grad, gain_three, shift_three = norm_back(dm_ref[...], gain_ref[2:3], h2_ref[...])
        e2 = e3 + grad
        f2 = e2.astype(BF)
        f2_ref[...] = f2
        doc_ref[...] = dot(f2, wo_ref[...], 1, 1).astype(BF)
        for pair in range(width // PAIR):
            lanes = slice(pair * PAIR, (pair + 1) * PAIR)
            queries = two_heads(qc_ref[:, lanes] * BF(SCALE))
            doc = doc_ref[:, lanes]
            grads = two_heads(doc)
            inner = row_dots(doc, oc_ref[:, lanes])
            keys = tk_ref[:, lanes]
            s = dot(keys, queries, 1, 1)
            s = jnp.where(live_ref[...] > 0, s, NEG)
            probs = jnp.exp(s - log_ref[0, pair : pair + 1])
            dprobs = dot(tv_ref[:, lanes], grads, 1, 1)
            ds = (probs * (dprobs - inner)).astype(BF)
            dtv_sum[:, lanes] += dot(probs.astype(BF), grads, 1, 0)
            dtk_sum[:, lanes] += dot(ds, queries, 1, 0)
            turned = keys.T
            both = jnp.concatenate(
                [
                    dot(
                        turned[h * HEAD_DIM : (h + 1) * HEAD_DIM],
                        ds[:, h * size : (h + 1) * size],
                        1,
                        0,
                    )
                    for h in range(2)
                ],
                0,
            )
            dqc_ref[:, lanes] = (both * SCALE).T.astype(BF)
        dc = dot(dqc_ref[...], wq_ref[...], 1, 1)
        grad, gain_two, shift_two = norm_back(dc, gain_ref[1:2], h1_ref[...])
        e1 = e2 + grad
        e1_ref[...] = e1
        f1 = e1.astype(BF)
        f1_ref[...] = f1
        for n, (ref, weight) in enumerate(
            ((do_ref, w0), (do_ref, w1), (other_ref, w2), (other_ref, w3))
        ):
            k = n % 2
            ref[:, k * quarter : (k + 1) * quarter] = dot(f1, weight[...], 1, 1).astype(BF)
        for n, ref in enumerate((f2_ref, dqc_ref, f1_ref)):
            for k in range(2):
                at = pl.multiple_of((2 * k + 1 - place_ref[1]) * quarter, quarter)
                cols_ref[n, :, k * quarter : (k + 1) * quarter] = ref[:, pl.ds(at, quarter)]
        sums = jnp.concatenate(
            [gain_two, gain_three, shift_two, shift_three]
            + [column_sum(v) for v in (f1, f2, e3)]
            + [jnp.zeros_like(gain_two)],
            0,
        )

        @pl.when(first)
        def _():
            sum_ref[...] = sums

        @pl.when(jnp.logical_not(first))
        def _():
            sum_ref[...] += sums

        @pl.when(pl.program_id(0) == steps - 1)
        def _():
            dt_ref[0] = dtk_sum[...].astype(BF)
            dt_ref[1] = dtv_sum[...].astype(BF)

    row, half = row_spec(size, width), row_spec(size, width // 2)
    square, text = whole_spec((width, width)), whole_spec((slots, width))
    low, narrow = out_struct(rows, width), out_struct(rows, width // 2)
    pairs = width // PAIR
    return call(
        kernel,
        "middle_backward",
        (low, low, low, out_struct(rows, width, F32), narrow, narrow)
        + (jax.ShapeDtypeStruct((3, rows, width // 2), BF),)
        + (jax.ShapeDtypeStruct((2, slots, width), BF),)
        + (out_struct(8, width, F32),),
        (steps,),
        [whole_spec((slots, 1))]
        + [row] * 6
        + [pl.BlockSpec((1, pairs, 2 * size), lambda i, *_: (i, 0, 0))]
        + head_row_specs(width)
        + [whole_spec(gains.shape), square, text, text, square],
        (row,) * 4
        + (half,) * 2
        + (pl.BlockSpec((3, size, width // 2), lambda i, *_: (0, i, 0)),)
        + (whole_spec((2, slots, width)),)
        + (whole_spec((8, width)),),
        scratch=[
            pltpu.VMEM((size, width), BF),
            pltpu.VMEM((slots, width), F32),
            pltpu.VMEM((slots, width), F32),
        ],
    )(place, live, dm, e3, h1, h2, qc, oc, logs, *[self_out] * 4, gains, wq, tk, tv, wo)


def mlp_part(place, m, e3, w_in, w_out, bias, start, dm_sum, part, tile):
    rows, width = m.shape
    hidden = w_in.shape[1] // 2
    steps = hidden // tile
    turn = steps // 2

    def column(t, place):
        ahead = t < turn
        side = jnp.where(ahead, 1 - place[1], place[1])
        return side * turn + jnp.where(ahead, t, t - turn)

    def kernel(place_ref, m_ref, e3_ref, in_ref, out_ref, bias_ref, *refs):
        starts, (g_ref, far_ref, near_ref, sum_ref, o_ref, dm_ref) = refs[:-6], refs[-6:]
        t = pl.program_id(0)

        @pl.when(t == 0)
        def _():
            o_ref[...] = starts[0][...] + starts[1][2:3] if part == 0 else starts[0][...]
            dm_ref[...] = jnp.zeros_like(dm_ref) if part == 0 else starts[1][...]

        g, slope = gelu_and_slope(dot(m_ref[...], in_ref[...], 1, 0) + bias_ref[...])
        g = g.astype(BF)
        g_ref[...] = g
        dg = dot(e3_ref[...], out_ref[...], 1, 1).astype(BF).astype(F32)
        d = (dg * slope).astype(BF)

        @pl.when(t < turn)
        def _():
            far_ref[...] = d

        @pl.when(t >= turn)
        def _():
            near_ref[...] = d

        sum_ref[...] = column_sum(d)
        o_ref[...] += dot(g, out_ref[...], 1, 0)
        dm_ref[...] += dot(d, in_ref[...], 1, 1)

    full = whole_spec((rows, width))
    wide = pl.BlockSpec((rows, tile), lambda t, place: (0, column(t, place)))
    second = whole_spec(dm_sum.shape)
    return call(
        kernel,
        "mlp",
        (out_struct(rows, hidden), out_struct(rows, hidden // 2), out_struct(rows, hidden // 2))
        + (out_struct(1, hidden, F32),)
        + (out_struct(rows, width, F32),) * 2,
        (steps,),
        [
            full,
            full,
            pl.BlockSpec((width, tile), lambda t, place: (0, part * steps + column(t, place))),
            pl.BlockSpec((tile, width), lambda t, place: (part * steps + column(t, place), 0)),
            pl.BlockSpec((1, tile), lambda t, place: (0, part * steps + column(t, place))),
            full,
            second,
        ],
        (
            wide,
            pl.BlockSpec((rows, tile), lambda t, place: (0, jnp.minimum(t, turn - 1))),
            pl.BlockSpec((rows, tile), lambda t, place: (0, jnp.maximum(t - turn, 0))),
            pl.BlockSpec((1, tile), lambda t, place: (0, column(t, place))),
            full,
            full,
        ),
    )(place, m, e3, w_in, w_out, bias, start, dm_sum)


def part_out(place_ref, write):
    core = place_ref[1]
    mine = jnp.where(core == 0, place_ref[2], place_ref[3])
    for ahead, output in ((1 - mine, 0), (mine, 1)):
        for behind in range(2):
            write(
                output,
                behind,
                jnp.where(core == 0, ahead, behind),
                jnp.where(core == 0, behind, ahead),
            )


def core_columns(rows, quarter):
    return [
        pl.BlockSpec((rows, quarter), lambda t, place, k=k: (0, 2 * k + place[1]))
        for k in range(2)
    ]


def pair_struct(shape):
    return (jax.ShapeDtypeStruct(shape, BF),) * 2


def grad_down(place, units, mate_units, e3, e3_mate, steps):
    rows, half = units.shape
    quarter = e3.shape[1] // 4
    tile = half // steps

    def kernel(place_ref, own, mate, *refs):
        sent, kept, turned, both = refs[-4:]

        @pl.when(pl.program_id(0) == 0)
        def _():
            for k in range(2):
                at = slice(k * quarter, (k + 1) * quarter)
                turned[at, :rows] = refs[k][...].T
                turned[at, rows:] = refs[2 + k][...].T

        total = dot(turned[:, :rows], own[...], 1, 0) + dot(turned[:, rows:], mate[...], 1, 0)
        for k in range(2):
            for y in range(2):
                both[y, k] = total[
                    k * quarter : (k + 1) * quarter, y * (tile // 2) : (y + 1) * (tile // 2)
                ].astype(BF)

        def write(output, behind, one, two):
            (sent, kept)[output][behind, 0] = both[one, two]

        part_out(place_ref, write)

    wide = pl.BlockSpec((rows, tile), lambda t, place: (0, t))
    out = pl.BlockSpec((2, 1, quarter, tile // 2), lambda t, place: (0, t, 0, 0))
    return call(
        kernel,
        "grad_down",
        pair_struct((2, steps, quarter, tile // 2)),
        (steps,),
        [wide, wide] + core_columns(rows, quarter) * 2,
        (out, out),
        scratch=[pltpu.VMEM((2 * quarter, 2 * rows), BF), pltpu.VMEM((2, 2, quarter, tile // 2), BF)],
    )(place, units, mate_units, e3, e3, e3_mate, e3_mate)


def transposed(place, array):
    def kernel(place_ref, from_ref, to_ref):
        to_ref[...] = from_ref[...].T

    rows, cols = array.shape
    return call(
        kernel,
        "transposed",
        jax.ShapeDtypeStruct((cols, rows), array.dtype),
        (1,),
        [whole_spec((rows, cols))],
        whole_spec((cols, rows)),
    )(place, array)


def row_blocks(one_bit, two_bit, count):
    at = []
    for rest in range(count // 4):
        low, high = min(one_bit, two_bit), max(one_bit, two_bit)
        rest = ((rest >> low) << (low + 1)) | (rest & ((1 << low) - 1))
        rest = ((rest >> high) << (high + 1)) | (rest & ((1 << high) - 1))
        at.append(rest)
    return at


def grad_up(place, m, m_mate, grads, mate_grads, bits, count):
    rows, depth = m.shape
    cols = grads.shape[1]
    size = depth // count
    others = row_blocks(*bits, count)

    def kernel(place_ref, m_ref, mate_ref, own, mate, *refs):
        sent, kept, both = refs[-3:]
        total = dot(m_ref[...].T, own[...], 1, 0) + dot(mate_ref[...].T, mate[...], 1, 0)
        for w in range(count):
            both[w] = total[w * size : (w + 1) * size].astype(BF)

        def write(output, behind, one, two):
            for n, rest in enumerate(others):
                (sent, kept)[output][behind, n] = both[
                    rest + (one << bits[0]) + (two << bits[1])
                ]

        part_out(place_ref, write)

    shape = (2, count // 4, size, cols)
    return call(
        kernel,
        "grad_up",
        pair_struct(shape),
        (1,),
        [whole_spec((rows, depth))] * 2 + [whole_spec((rows, cols))] * 2,
        (whole_spec(shape),) * 2,
        scratch=[pltpu.VMEM((count, size, cols), BF)],
    )(place, m, m_mate, grads, mate_grads)


def grad_square(place, members, count, bits=None):
    arrays, specs, plan = [], [], []
    known = {}
    for member in members:
        pieces = []
        for left, right, lead, whole in member:
            rows, depth = right.shape[-2], left.shape[1]
            quarter = right.shape[-1] // (4 if whole else 2)
            block = lead[0] if len(lead) == 2 else 0
            if (id(left), block) not in known:
                known[id(left), block] = len(arrays)
                arrays.append(left)
                specs.append(
                    pl.BlockSpec((rows, depth), lambda t, place, block=block: (block, 0))
                )
            pieces.append((known[id(left), block], len(arrays)))
            arrays += [right, right]
            for k in range(2):

                def column(t, place, k=k, lead=lead, whole=whole):
                    return (*lead, 0, 2 * k + place[1] if whole else k)

                specs.append(pl.BlockSpec((None,) * len(lead) + (rows, quarter), column))
        plan.append(pieces)
    size = depth // count
    others = row_blocks(*bits, count) if bits else range(count // 2)

    def kernel(place_ref, *refs):
        sent, kept, both = refs[-3:]
        turned = {}
        for n, pieces in enumerate(plan):
            total = 0.0
            for left, right in pieces:
                if left not in turned:
                    turned[left] = refs[left][...].T
                cols = jnp.concatenate([refs[right][...], refs[right + 1][...]], 1)
                total = total + dot(turned[left], cols, 1, 0)
            for w in range(count):
                rows = total[w * size : (w + 1) * size].astype(BF)
                if bits:
                    both[w] = rows
                else:
                    for k in range(2):
                        both[w, k] = rows[:, k * quarter : (k + 1) * quarter]

            def write(output, behind, one, two):
                for n_rest, rest in enumerate(others):
                    if bits:
                        found = both[rest + (one << bits[0]) + (two << bits[1])]
                    else:
                        found = both[2 * rest + one, two]
                    (sent, kept)[output][behind, n_rest, n] = found

            part_out(place_ref, write)

    tile = (size, 2 * quarter) if bits else (2, size, quarter)
    shape = (2, len(others), len(members)) + tile[-2:]
    return call(
        kernel,
        "grad_square",
        pair_struct(shape),
        (1,),
        specs,
        (whole_spec(shape),) * 2,
        scratch=[pltpu.VMEM((count,) + tile, BF)],
    )(place, *arrays)


def first_backward(place, d, d_other, qkv, gains, x, e1, size):
    rows, width = x.shape
    quarter, steps = width // 4, rows // size

    def kernel(place_ref, d_ref, other_ref, gain_ref, x_ref, e1_ref, *refs):
        weights, (own_ref, far_ref, sum_ref) = refs[:12], refs[12:]
        grad = jnp.zeros((size, width), F32)
        for j in range(3):
            for k in range(2):
                cols = slice(k * quarter, (k + 1) * quarter)
                grad = grad + dot(d_ref[j][:, cols], weights[4 * j + k][0], 1, 1)
                grad = grad + dot(other_ref[j][:, cols], weights[4 * j + 2 + k][0], 1, 1)
        grad, gain, shift = norm_back(grad, gain_ref[0:1], x_ref[...].astype(F32))
        total = e1_ref[...] + grad
        sums = jnp.concatenate([gain, shift], 0)

        @pl.when(pl.program_id(0) == 0)
        def _():
            own_ref[...] = total
            sum_ref[...] = sums

        @pl.when(pl.program_id(0) == 1)
        def _():
            far_ref[...] = total.astype(BF)
            sum_ref[...] += sums

    def weight_spec(j, flip, k):
        return pl.BlockSpec(
            (1, width, quarter), lambda i, place: (j, 0, 2 * k + (place[1] ^ flip))
        )

    return call(
        kernel,
        "first_backward",
        (out_struct(size, width, F32), out_struct(size, width), out_struct(2, width, F32)),
        (steps,),
        [
            pl.BlockSpec((None, 3, size, width // 2), lambda i, *_: (0, 0, i, 0)),
            pl.BlockSpec((3, size, width // 2), lambda i, *_: (0, i, 0)),
        ]
        + [whole_spec(gains.shape), row_spec(size, width), row_spec(size, width)]
        + [weight_spec(j, flip, k) for j in range(3) for flip in range(2) for k in range(2)],
        (whole_spec((size, width)), whole_spec((size, width)), whole_spec((2, width))),
    )(place, d, d_other, gains, x, e1, *[qkv] * 12)


def body(
    image_tokens,
    text_states,
    caption_lengths,
    text_mask,
    self_qkv,
    self_out,
    cross_query,
    cross_kv,
    cross_out,
    mlp_in,
    mlp_out,
    norm_gains,
    norm_shifts,
    out_biases,
    mlp_bias,
    cotangent,
):
    _, block, width = image_tokens.shape
    blocks = lax.axis_size("narrow")
    wide_size = lax.axis_size("wide")
    here = lax.axis_index("narrow")
    line = lax.axis_index("wide")
    chip, core = here // 2, here % 2
    wide_bits = wide_size.bit_length() - 1
    mates = [(i, i ^ 1) for i in range(blocks)]
    across = [(i, i ^ 2) for i in range(blocks)]

    def to_mate(value):
        return lax.ppermute(value, "narrow", mates)

    def to_chip(value):
        return lax.ppermute(value, "narrow", across)

    def item(array, index):
        return lax.dynamic_index_in_dim(array, index, 0, keepdims=False)

    def columns(array, side):
        quarter = array.shape[-1] // 4
        return jnp.concatenate(
            [
                lax.dynamic_slice_in_dim(array, (2 * k + side) * quarter, quarter, array.ndim - 1)
                for k in range(2)
            ],
            -1,
        )

    def chosen(first, second):
        return jnp.where(core == 0, first, second), jnp.where(core == 0, second, first)

    near = list(range(wide_bits))

    def partner(index, axis):
        line_at, here_at = divmod(index, blocks)
        if axis == "x":
            return line_at * blocks + (here_at ^ 2)
        return (line_at ^ (1 << axis)) * blocks + here_at

    def exchange(value, first, second=None):
        axes = (first, first if second is None else second)
        pairs = [(i, partner(i, axes[i % 2])) for i in range(wide_size * blocks)]
        return lax.ppermute(value, ("wide", "narrow"), pairs)

    def bit_of(axis):
        return chip if axis == "x" else (line >> axis) & 1

    class Scatter:
        def __init__(self, shape, one, two, dims):
            self.shape, self.axes, self.dims = shape, (one, two), dims
            self.kept, self.come = [], []

        def add(self, halves, *others):
            self.sent, kept = (half.reshape(self.shape) for half in halves)
            self.kept.append(kept)
            self.come.append(exchange(after(self.sent, *others), *self.axes))
            self.held = [tuple(self.kept), tuple(self.come)]

        def advance(self, bit, dim, *axes):
            count = len(self.kept)

            def pieces(term):
                if isinstance(term, tuple):
                    return term
                return tuple(jnp.split(term, count, 1)) if count > 1 else (term,)

            def take(value, which):
                size = value.shape[dim] // 2
                return lax.dynamic_slice_in_dim(value, which * size, size, dim)

            def choose(term, which):
                if dim == 1 and isinstance(term, tuple) and count > 1:
                    return (jnp.where(which == 0, term[0], term[1]),)
                if dim == 1:
                    whole = term[0] if isinstance(term, tuple) else term
                    return (take(whole, which),)
                return tuple(take(piece, which) for piece in pieces(term))

            away = [choose(term, 1 - bit) for term in self.held]
            sums = [sum(p.astype(F32) for p in part).astype(BF) for part in zip(*away)]
            self.sent = sums[0] if len(sums) == 1 else jnp.concatenate(sums, 1)
            self.held = [choose(term, bit) for term in self.held] + [exchange(self.sent, *axes)]
            if dim == 1:
                self.kept = self.kept[:1]

        def turn(self):
            one, two = self.axes
            self.advance(jnp.where(core == 0, bit_of(two), bit_of(one)), 0, two, one)

        def step(self, axis):
            self.advance(bit_of(axis), self.dims[axis], axis)

        def wait(self, *others):
            self.held = list(lax.optimization_barrier((tuple(self.held),) + others)[0])

        def total(self, *shape):
            terms = [t[0] if isinstance(t, tuple) else t for t in self.held]
            return sum(t.astype(F32) for t in terms).reshape(shape)

    def bit_dims(first, *left_out):
        bits = [b for b in reversed(near) if b not in left_out]
        return (2,) * len(bits), {b: first + n for n, b in enumerate(bits)}

    def places(one, two):
        return jnp.stack([here, core, bit_of(one), bit_of(two)]).astype(jnp.int32)

    def both(own_part, mate_part):
        return jnp.concatenate([own_part, mate_part], 0)

    def after(value, *others):
        return lax.optimization_barrier((value,) + others)[0]

    rows_wide = width // wide_size
    quarter = width // 4

    def home(own, far):
        far = far.astype(F32)
        return jnp.where((jnp.arange(2) == chip)[:, None, None], own[None], far[None])

    own = jnp.concatenate([item(image_tokens, chip), item(text_states, chip)], 0)
    far = to_chip(
        jnp.concatenate([item(image_tokens, 1 - chip), item(text_states, 1 - chip)], 0)
    )
    own_mate = to_mate(own)
    place = jnp.stack([here, core]).astype(jnp.int32)
    first = project(place, own, own_mate, self_qkv, norm_gains, norm_shifts, 0, block, None)
    far = after(far, first[0])
    far_mate = to_mate(far)
    a, q, k, v = project(
        place, far, far_mate, self_qkv, norm_gains, norm_shifts, 1, block, first
    )
    x = both(own[:block], far[:block])
    text_all = jnp.concatenate(
        chosen(both(own[block:], far[block:]), both(own_mate[block:], far_mate[block:])), 0
    )
    slot_block = text_states.shape[1]
    slots = slot_block * blocks
    slot_order = jnp.stack([(2 * chip) ^ k for k in (0, 2, 1, 3)])
    slot = (slot_order[:, None] * slot_block + jnp.arange(slot_block)[None, :]).reshape(slots)
    kept = item(text_mask, chip).reshape(blocks, slot_block)
    kept = jnp.concatenate([item(kept, (2 * chip) ^ k) for k in (0, 2, 1, 3)], 0)
    length = item(caption_lengths, chip)
    live = ((slot < length) & ((kept == 1) | (slot == 0))).astype(F32).reshape(slots, 1)

    tk = dot(text_all, cross_kv[0], 1, 0).astype(BF)
    tv = dot(text_all, cross_kv[1], 1, 0).astype(BF)

    rows = 2 * block
    cot_far = to_chip(after(item(cotangent, 1 - chip), q))
    q = after(q, tk, tv)
    o, log_self = self_forward(place, q, k, v, blocks)
    o = after(o, cot_far)
    o_other = to_mate(o[1])
    e3 = both(item(cotangent, chip), cot_far)
    os_rows, h1, c, qc, oc, log_cross, h2, m = middle_forward(
        place,
        live,
        x,
        o,
        o_other,
        self_out,
        norm_gains,
        norm_shifts,
        out_biases,
        cross_query,
        tk,
        tv,
        cross_out,
        block,
    )
    e3_mate, m_mate = to_mate(e3), to_mate(m)
    c_mate, oc_mate, os_mate = to_mate(c), to_mate(oc), to_mate(os_rows)
    bias_row = mlp_bias.reshape(1, -1)
    sums = (h2, out_biases)
    g, g_mate, kept, kept_mate, hidden_sums = [], [], [], [], []
    for part in range(2):
        units, sent, stay, hidden_sum, *sums = mlp_part(
            place, m, e3, mlp_in, mlp_out, bias_row, *sums, part, TILE
        )
        g.append(units)
        g_mate.append(to_mate(units))
        kept.append(stay)
        kept_mate.append(to_mate(sent))
        hidden_sums.append(hidden_sum)
        if part == 0:
            sums[1] = after(sums[1], e3_mate, m_mate, c_mate, oc_mate, os_mate)
    layer_out, dm = sums
    out_far = to_chip(layer_out[block:].astype(BF))
    up_bits = (near[1], near[0])
    shape, dims = bit_dims(2, near[0], near[-1])
    dims[near[-1]] = 1
    down = Scatter(
        (2, 1) + shape + (quarter, mlp_out.shape[0] // wide_size), near[0], "x", dims
    )
    shape, dims = bit_dims(2, *up_bits)
    dims["x"] = 1
    up = Scatter((2, 1) + shape + (rows_wide, mlp_in.shape[1] // 4), *up_bits, dims)
    for part in range(2):
        down.add(
            grad_down(
                places(near[0], "x"), g[part], g_mate[part], e3, e3_mate, wide_size // 4
            )
        )
        kept[part] = after(kept[part], down.sent)
        up.add(
            grad_up(
                places(*up_bits), m, m_mate, kept[part], kept_mate[part], up_bits, wide_size
            )
        )
        if part == 0:
            g[1] = after(g[1], up.sent, out_far)
    down.wait(up.sent)
    down.turn()
    dm = after(dm, up.sent, down.sent)

    f2, dqc, f1, e1, do_own, do_other, cols, dt, row_sums = middle_backward(
        place,
        live,
        dm,
        e3,
        h1,
        h2,
        qc,
        oc,
        log_cross,
        self_out,
        norm_gains,
        cross_query,
        tk,
        tv,
        cross_out,
        block,
    )
    up.wait(row_sums)
    up.turn()
    down.wait(row_sums)
    down.step(near[1])
    do_mate = to_mate(do_other)
    dt_mate, cols_mate = to_mate(dt), to_mate(cols)
    dt_mate = after(dt_mate, up.sent, down.sent)
    dt = (dt.astype(F32) + dt_mate.astype(F32)).astype(BF)
    outer_axes = (near[1], near[0])
    shape, dims = bit_dims(1, *outer_axes)
    shape = (2,) + shape + (5, rows_wide, 2 * quarter)
    dims["x"] = len(shape) - 1
    outer = Scatter(shape, *outer_axes, dims)
    outer.add(
        grad_square(
            places(*outer_axes),
            [
                [(oc, f2, (), True), (oc_mate, cols_mate, (0,), False)],
                [(text_all, dt, (0,), True)],
                [(text_all, dt, (1,), True)],
                [(c, dqc, (), True), (c_mate, cols_mate, (1,), False)],
                [(os_rows, f1, (), True), (os_mate, cols_mate, (2,), False)],
            ],
            wide_size,
            outer_axes,
        )
    )
    down.wait(outer.sent)
    up.wait(outer.sent)
    up.step("x")
    for axis in near[2:]:
        down.step(axis)
    do_mate = after(do_mate, down.sent, up.sent)
    d = self_backward(place, q, k, v, o, do_own, do_mate, log_self, blocks)
    for axis in near[2:]:
        up.wait(d)
        up.step(axis)
    d = after(d, up.sent)
    d_other = to_mate(d[1])
    shape, dims = bit_dims(1, near[0])
    inner = Scatter((2,) + shape + (3, rows_wide, quarter), near[0], "x", dims)
    inner.add(
        grad_square(
            places(near[0], "x"),
            [[(a, d, (side, j), False) for side in range(2)] for j in range(3)],
            wide_size,
        )
    )
    d_other = after(d_other, inner.sent)
    grad_own, grad_far, late = first_backward(
        place, d, d_other, self_qkv, norm_gains, x, e1, block
    )
    image_far = to_chip(grad_far)
    late = jnp.concatenate(
        [late, row_sums[:7], jnp.concatenate(hidden_sums, 1).reshape(-1, width)]
    )
    late = late + to_mate(late)
    late = late + to_chip(late)
    outer.wait(grad_far)
    outer.turn()
    inner.wait(outer.sent)
    inner.turn()
    late = after(late, inner.sent)
    late = late + exchange(late, near[0])
    outer.wait(inner.sent)
    outer.step("x")
    dt_own = lax.dynamic_slice_in_dim(dt, core * 2 * slot_block, 2 * slot_block, 1)
    dt_own = after(dt_own, outer.sent)
    grad_text = dot(dt_own[0], cross_kv[0], 1, 1) + dot(dt_own[1], cross_kv[1], 1, 1)
    inner.wait(outer.sent)
    inner.step(near[1])
    late = after(late, inner.sent)
    for axis in near[1:]:
        late = late + exchange(late, axis)
    for axis in near[2:]:
        outer.step(axis)
        inner.step(axis)

    outer_part = outer.total(5, rows_wide, quarter)
    inner_part = inner.total(3, rows_wide, quarter)
    down_part = transposed(place, down.total(quarter, mlp_out.shape[0] // wide_size))

    gains = jnp.stack([late[0], late[2], late[3]])
    shifts = jnp.stack([late[1], late[4], late[5]])
    return (
        home(layer_out[:block], out_far),
        home(grad_own, image_far),
        home(grad_text[:slot_block], to_chip(grad_text[slot_block:])),
        inner_part,
        outer_part[4],
        outer_part[3],
        outer_part[1:3],
        outer_part[0],
        up.total(rows_wide, mlp_in.shape[1] // 4),
        down_part,
        gains,
        shifts,
        late[6:9],
        late[9:].reshape(-1),
    )


def solution(mesh):
    rows = P("wide", "narrow", None)
    whole = P()
    return jax.shard_map(
        body,
        mesh=mesh,
        in_specs=(rows, rows, P("wide"), P("wide", None)) + (whole,) * 11 + (rows,),
        out_specs=(rows,) * 3
        + (
            P(None, "wide", "narrow"),
            P("wide", "narrow"),
            P("wide", "narrow"),
            P(None, "wide", "narrow"),
        )
        + (P("wide", "narrow"),) * 3
        + (whole,) * 4,
        check_vma=False,
    )
```

```python
import jax
import jax.numpy as jnp
from jax import lax
from jax.experimental import pallas as pl
from jax.experimental.pallas import tpu as pltpu
from jax.sharding import PartitionSpec as P

HEAD_DIM = 64
PAIR = 2 * HEAD_DIM
SCALE = HEAD_DIM**-0.5
NEG = -1e30
BF = jnp.bfloat16
F32 = jnp.float32
VMEM = 56 * 1024 * 1024
TILE = 1024


def dot(left, right, left_axis, right_axis):
    return lax.dot_general(
        left, right, (((left_axis,), (right_axis,)), ((), ())), preferred_element_type=F32
    )


def two_heads(rows):
    lane = lax.broadcasted_iota(jnp.int32, rows.shape, 1)
    zero = jnp.zeros_like(rows)
    return jnp.concatenate(
        [jnp.where(lane < HEAD_DIM, rows, zero), jnp.where(lane < HEAD_DIM, zero, rows)], 0
    )


def block_rows(here, block, size):
    slot = here ^ block
    return pl.ds(pl.multiple_of(((slot & 1) * 2 + slot // 2) * size, size), size)


def slot_place(here, block, size):
    slot = here ^ block
    return slot & 1, pl.ds(pl.multiple_of((slot // 2) * size, size), size)


def store_sides(here, block, size, even, odd, own_ref, mate_ref):
    _, half = slot_place(here, block, size)
    own_first = (here & 1) == 0
    own_ref[half, :] = jnp.where(own_first, even, odd)
    mate_ref[half, :] = jnp.where(own_first, odd, even)


def causal_mask(scores, size):
    key = lax.broadcasted_iota(jnp.int32, scores.shape, 0)
    query = lax.broadcasted_iota(jnp.int32, scores.shape, 1)
    return jnp.where(key <= lax.rem(query, size), scores, NEG)


def self_forward_kernel(here_ref, q_ref, k_ref, v_ref, own_ref, mate_ref, log_ref, *, blocks):
    here = here_ref[0]
    size = q_ref.shape[0] // blocks
    for p in range(blocks):
        rows = block_rows(here, p, size)
        queries = two_heads(q_ref[rows, :] * BF(SCALE))
        scores = []
        for j in range(p + 1):
            s = dot(k_ref[block_rows(here, j, size), :], queries, 1, 1)
            scores.append(causal_mask(s, size) if j == p else s)
        top = scores[0].max(0, keepdims=True)
        for s in scores[1:]:
            top = jnp.maximum(top, s.max(0, keepdims=True))
        total = jnp.zeros_like(top)
        mixed = [jnp.zeros((HEAD_DIM, size), F32)] * 2
        for j in range(p + 1):
            e = jnp.exp(scores[j] - top)
            total = total + e.sum(0, keepdims=True)
            low = e.astype(BF)
            values = v_ref[block_rows(here, j, size), :].T
            for h in range(2):
                mixed[h] = mixed[h] + dot(
                    values[h * HEAD_DIM : (h + 1) * HEAD_DIM],
                    low[:, h * size : (h + 1) * size],
                    1,
                    0,
                )
        inverse = 1.0 / total
        both = jnp.concatenate(
            [mixed[h] * inverse[:, h * size : (h + 1) * size] for h in range(2)], 0
        )
        low = both.T.astype(BF)
        if p % 2:
            store_sides(here, p - 1, size, before, low, own_ref, mate_ref)
        before = low
        log_ref[0, :, 2 * size * p : 2 * size * (p + 1)] = top + jnp.log(total)


def row_dots(left, right):
    product = left.astype(F32).T * right.astype(F32).T
    return jnp.concatenate(
        [product[:HEAD_DIM].sum(0, keepdims=True), product[HEAD_DIM:].sum(0, keepdims=True)], 1
    )


def self_backward_kernel(
    here_ref,
    q_ref,
    k_ref,
    v_ref,
    o_ref,
    o_mate_ref,
    do_ref,
    do_mate_ref,
    log_ref,
    own_ref,
    mate_ref,
    *,
    blocks,
):
    here = here_ref[0]
    size = q_ref.shape[0] // blocks
    queries, grads, inner, dq = [], [], [], []
    for p in range(blocks):
        rows = block_rows(here, p, size)
        queries.append(two_heads(q_ref[rows, :] * BF(SCALE)))
        side, half = slot_place(here, p, size)
        do = jnp.where(side == 0, do_ref[half, :], do_mate_ref[half, :])
        grads.append(two_heads(do))
        o = jnp.where(side == 0, o_ref[half, :], o_mate_ref[half, :])
        inner.append(row_dots(do, o))
        dq.append([jnp.zeros((HEAD_DIM, size), F32)] * 2)
    for j in range(blocks):
        rows = block_rows(here, j, size)
        keys, values = k_ref[rows, :], v_ref[rows, :]
        turned = keys.T
        dk = jnp.zeros(keys.shape, F32)
        dv = jnp.zeros(keys.shape, F32)
        for p in range(j, blocks):
            s = dot(keys, queries[p], 1, 1)
            if j == p:
                s = causal_mask(s, size)
            probs = jnp.exp(s - log_ref[0, :, 2 * size * p : 2 * size * (p + 1)])
            dprobs = dot(values, grads[p], 1, 1)
            ds = (probs * (dprobs - inner[p])).astype(BF)
            dv = dv + dot(probs.astype(BF), grads[p], 1, 0)
            dk = dk + dot(ds, queries[p], 1, 0)
            for h in range(2):
                dq[p][h] = dq[p][h] + dot(
                    turned[h * HEAD_DIM : (h + 1) * HEAD_DIM],
                    ds[:, h * size : (h + 1) * size],
                    1,
                    0,
                )
        low = dk.astype(BF), dv.astype(BF)
        if j % 2:
            for n in range(2):
                store_sides(
                    here, j - 1, size, before[n], low[n], own_ref.at[1 + n], mate_ref.at[1 + n]
                )
        before = low
    for p in range(blocks):
        both = jnp.concatenate(dq[p], 0) * SCALE
        low = both.T.astype(BF)
        if p % 2:
            store_sides(here, p - 1, size, before, low, own_ref.at[0], mate_ref.at[0])
        before = low


def pair_spec(rows):
    return pl.BlockSpec((rows, PAIR), lambda i, *_: (0, i))


def log_spec(width):
    return pl.BlockSpec((1, 1, width), lambda i, *_: (i, 0, 0))


def self_forward(here, q, k, v, blocks):
    rows, width = q.shape
    pairs = width // PAIR
    spec = pair_spec(rows)
    return pl.pallas_call(
        lambda *refs: self_forward_kernel(*refs, blocks=blocks),
        name="self_forward",
        out_shape=(
            jax.ShapeDtypeStruct((rows // 2, width), BF),
            jax.ShapeDtypeStruct((rows // 2, width), BF),
            jax.ShapeDtypeStruct((pairs, 1, 2 * rows), F32),
        ),
        grid_spec=pltpu.PrefetchScalarGridSpec(
            num_scalar_prefetch=1,
            grid=(pairs,),
            in_specs=[spec] * 3,
            out_specs=(pair_spec(rows // 2), pair_spec(rows // 2), log_spec(2 * rows)),
        ),
        compiler_params=pltpu.CompilerParams(vmem_limit_bytes=VMEM),
        cost_estimate=pl.CostEstimate(flops=10**6, bytes_accessed=10**5, transcendentals=0),
    )(here, q, k, v)


def self_backward(here, q, k, v, o, o_mate, do, do_mate, log_total, blocks):
    rows, width = q.shape
    pairs = width // PAIR
    spec = pair_spec(rows)
    return pl.pallas_call(
        lambda *refs: self_backward_kernel(*refs, blocks=blocks),
        name="self_backward",
        out_shape=(jax.ShapeDtypeStruct((3, rows // 2, width), BF),) * 2,
        grid_spec=pltpu.PrefetchScalarGridSpec(
            num_scalar_prefetch=1,
            grid=(pairs,),
            in_specs=[spec] * 3 + [pair_spec(rows // 2)] * 4 + [log_spec(2 * rows)],
            out_specs=(pl.BlockSpec((3, rows // 2, PAIR), lambda i, *_: (0, 0, i)),) * 2,
        ),
        compiler_params=pltpu.CompilerParams(vmem_limit_bytes=VMEM),
        cost_estimate=pl.CostEstimate(flops=10**6, bytes_accessed=10**5, transcendentals=0),
    )(here, q, k, v, o, o_mate, do, do_mate, log_total)


def standardize(rows):
    centered = rows - jnp.mean(rows, -1, keepdims=True)
    inverse = lax.rsqrt(jnp.mean(centered * centered, -1, keepdims=True) + 1e-05)
    return centered * inverse, inverse


def normed(rows, gain, shift):
    return (standardize(rows)[0] * gain + shift).astype(BF)


def norm_back(grad_out, gain, rows):
    unit, inverse = standardize(rows)
    grad_unit = grad_out * gain
    grad_in = inverse * (
        grad_unit
        - jnp.mean(grad_unit, -1, keepdims=True)
        - unit * jnp.mean(grad_unit * unit, -1, keepdims=True)
    )
    return grad_in, column_sum(grad_out * unit), column_sum(grad_out)


def column_sum(rows):
    return jnp.sum(rows.astype(F32), 0, keepdims=True)


def gelu_and_slope(pre):
    square = pre * pre
    bend = jnp.tanh(pre * (0.7978845608028654 + (0.7978845608028654 * 0.044715) * square))
    half = 0.5 + 0.5 * bend
    value = pre * half
    steep = 0.7978845608028654 + (3.0 * 0.7978845608028654 * 0.044715) * square
    return value, half + value * (1.0 - bend) * steep


def whole_spec(shape):
    return pl.BlockSpec(shape, lambda *_: (0,) * len(shape))


def row_spec(rows, cols, start=0):
    return pl.BlockSpec((rows, cols), lambda i, *_: (start + i, 0))


def call(kernel, name, out_shape, grid, in_specs, out_specs, scratch=(), aliases=None):
    return pl.pallas_call(
        kernel,
        name=name,
        out_shape=out_shape,
        grid_spec=pltpu.PrefetchScalarGridSpec(
            num_scalar_prefetch=1,
            grid=grid,
            in_specs=in_specs,
            out_specs=out_specs,
            scratch_shapes=scratch,
        ),
        input_output_aliases=aliases or {},
        compiler_params=pltpu.CompilerParams(vmem_limit_bytes=VMEM),
        cost_estimate=pl.CostEstimate(flops=10**6, bytes_accessed=10**5, transcendentals=0),
    )


def out_struct(rows, cols, kind=BF):
    return jax.ShapeDtypeStruct((rows, cols), kind)


def project(place, own, mate, qkv, gains, shifts, half, size, into):
    width = qkv.shape[1]
    quarter = width // 4

    def kernel(place_ref, own_ref, mate_ref, gain_ref, shift_ref, *refs):
        weights, outs = refs[:6], refs[-4:]
        rows = jnp.where(pl.program_id(0) == 0, own_ref[...], mate_ref[...]).astype(F32)
        a = normed(rows, gain_ref[0:1], shift_ref[0:1])
        outs[0][...] = a
        for j in range(3):
            pair = jnp.concatenate([weights[2 * j][0], weights[2 * j + 1][0]], 1)
            outs[1 + j][...] = dot(a, pair, 1, 0).astype(BF)

    def weight_spec(j, k):
        return pl.BlockSpec((1, width, quarter), lambda i, place: (j, 0, 2 * k + place[1]))

    def out_spec(cols):
        return pl.BlockSpec((size, cols), lambda i, place: (2 * i + half, 0))

    specs = [whole_spec((size, width))] * 2 + [whole_spec(gains.shape)] * 2
    specs += [weight_spec(j, k) for j in range(3) for k in range(2)]
    arrays = [own, mate, gains, shifts] + [qkv] * 6
    aliases = None
    if into is not None:
        aliases = {1 + len(arrays) + n: n for n in range(4)}
        arrays += list(into)
        specs += [pl.BlockSpec(memory_space=pl.ANY)] * 4
    rows = 4 * size
    return call(
        kernel,
        "project",
        (out_struct(rows, width),) + (out_struct(rows, width // 2),) * 3,
        (2,),
        specs,
        (out_spec(width),) + (out_spec(width // 2),) * 3,
        aliases=aliases,
    )(place, *arrays)


def head_row_specs(width):
    quarter = width // 4
    return [
        pl.BlockSpec((quarter, width), lambda i, place, k=k, flip=flip: (2 * k + (place[1] ^ flip), 0))
        for flip in range(2)
        for k in range(2)
    ]


def middle_forward(place, live, x, o, o_other, self_out, gains, shifts, biases, wq, tk, tv, wo, size):
    rows, width = x.shape
    quarter, slots, steps = width // 4, tk.shape[0], rows // size

    def kernel(
        place_ref,
        live_ref,
        x_ref,
        o_ref,
        other_ref,
        w0,
        w1,
        w2,
        w3,
        gain_ref,
        shift_ref,
        bias_ref,
        wq_ref,
        tk_ref,
        tv_ref,
        wo_ref,
        os_ref,
        h1_ref,
        c_ref,
        qc_ref,
        oc_ref,
        log_ref,
        h2_ref,
        m_ref,
    ):
        core = place_ref[1]
        h1 = x_ref[...].astype(F32) + bias_ref[0:1]
        for n, (ref, weight) in enumerate(
            ((o_ref, w0), (o_ref, w1), (other_ref, w2), (other_ref, w3))
        ):
            k, side = n % 2, core ^ (n // 2)
            part = ref[:, k * quarter : (k + 1) * quarter]
            at = pl.multiple_of((2 * k + side) * quarter, quarter)
            os_ref[:, pl.ds(at, quarter)] = part
            h1 = h1 + dot(part, weight[...], 1, 0)
        h1_ref[...] = h1
        c = normed(h1, gain_ref[1:2], shift_ref[1:2])
        c_ref[...] = c
        qc_ref[...] = dot(c, wq_ref[...], 1, 0).astype(BF)
        for pair in range(width // PAIR):
            lanes = slice(pair * PAIR, (pair + 1) * PAIR)
            queries = two_heads(qc_ref[:, lanes] * BF(SCALE))
            s = dot(tk_ref[:, lanes], queries, 1, 1)
            s = jnp.where(live_ref[...] > 0, s, NEG)
            top = s.max(0, keepdims=True)
            e = jnp.exp(s - top)
            total = e.sum(0, keepdims=True)
            low = e.astype(BF)
            values = tv_ref[:, lanes].T
            inverse = 1.0 / total
            both = jnp.concatenate(
                [
                    dot(
                        values[h * HEAD_DIM : (h + 1) * HEAD_DIM],
                        low[:, h * size : (h + 1) * size],
                        1,
                        0,
                    )
                    * inverse[:, h * size : (h + 1) * size]
                    for h in range(2)
                ],
                0,
            )
            oc_ref[:, lanes] = both.T.astype(BF)
            log_ref[0, pair : pair + 1] = top + jnp.log(total)
        h2 = h1 + dot(oc_ref[...], wo_ref[...], 1, 0) + bias_ref[1:2]
        h2_ref[...] = h2
        m_ref[...] = normed(h2, gain_ref[2:3], shift_ref[2:3])

    row = row_spec(size, width)
    square = whole_spec((width, width))
    low, high = out_struct(rows, width), out_struct(rows, width, F32)
    pairs = width // PAIR
    return call(
        kernel,
        "middle_forward",
        (low, high, low, low, low, jax.ShapeDtypeStruct((steps, pairs, 2 * size), F32), high, low),
        (steps,),
        [
            whole_spec((slots, 1)),
            row,
            row_spec(size, width // 2),
            row_spec(size, width // 2),
        ]
        + head_row_specs(width)
        + [whole_spec(gains.shape)] * 3
        + [square, whole_spec((slots, width)), whole_spec((slots, width)), square],
        (row,) * 5 + (pl.BlockSpec((1, pairs, 2 * size), lambda i, *_: (i, 0, 0)), row, row),
    )(place, live, x, o, o_other, *[self_out] * 4, gains, shifts, biases, wq, tk, tv, wo)


def middle_backward(
    place, live, dm, e3, h1, h2, qc, oc, logs, self_out, gains, wq, tk, tv, wo, size
):
    rows, width = h1.shape
    quarter, slots, steps = width // 4, tk.shape[0], rows // size

    def kernel(
        place_ref,
        live_ref,
        dm_ref,
        e3_ref,
        h1_ref,
        h2_ref,
        qc_ref,
        oc_ref,
        log_ref,
        w0,
        w1,
        w2,
        w3,
        gain_ref,
        wq_ref,
        tk_ref,
        tv_ref,
        wo_ref,
        f2_ref,
        dqc_ref,
        f1_ref,
        e1_ref,
        do_ref,
        other_ref,
        cols_ref,
        dt_ref,
        sum_ref,
        doc_ref,
        dtk_sum,
        dtv_sum,
    ):
        first = pl.program_id(0) == 0

        @pl.when(first)
        def _():
            dtk_sum[...] = jnp.zeros_like(dtk_sum)
            dtv_sum[...] = jnp.zeros_like(dtv_sum)

        e3 = e3_ref[...].astype(F32)
        grad, gain_three, shift_three = norm_back(dm_ref[...], gain_ref[2:3], h2_ref[...])
        e2 = e3 + grad
        f2 = e2.astype(BF)
        f2_ref[...] = f2
        doc_ref[...] = dot(f2, wo_ref[...], 1, 1).astype(BF)
        for pair in range(width // PAIR):
            lanes = slice(pair * PAIR, (pair + 1) * PAIR)
            queries = two_heads(qc_ref[:, lanes] * BF(SCALE))
            doc = doc_ref[:, lanes]
            grads = two_heads(doc)
            inner = row_dots(doc, oc_ref[:, lanes])
            keys = tk_ref[:, lanes]
            s = dot(keys, queries, 1, 1)
            s = jnp.where(live_ref[...] > 0, s, NEG)
            probs = jnp.exp(s - log_ref[0, pair : pair + 1])
            dprobs = dot(tv_ref[:, lanes], grads, 1, 1)
            ds = (probs * (dprobs - inner)).astype(BF)
            dtv_sum[:, lanes] += dot(probs.astype(BF), grads, 1, 0)
            dtk_sum[:, lanes] += dot(ds, queries, 1, 0)
            turned = keys.T
            both = jnp.concatenate(
                [
                    dot(
                        turned[h * HEAD_DIM : (h + 1) * HEAD_DIM],
                        ds[:, h * size : (h + 1) * size],
                        1,
                        0,
                    )
                    for h in range(2)
                ],
                0,
            )
            dqc_ref[:, lanes] = (both * SCALE).T.astype(BF)
        dc = dot(dqc_ref[...], wq_ref[...], 1, 1)
        grad, gain_two, shift_two = norm_back(dc, gain_ref[1:2], h1_ref[...])
        e1 = e2 + grad
        e1_ref[...] = e1
        f1 = e1.astype(BF)
        f1_ref[...] = f1
        for n, (ref, weight) in enumerate(
            ((do_ref, w0), (do_ref, w1), (other_ref, w2), (other_ref, w3))
        ):
            k = n % 2
            ref[:, k * quarter : (k + 1) * quarter] = dot(f1, weight[...], 1, 1).astype(BF)
        for n, ref in enumerate((f2_ref, dqc_ref, f1_ref)):
            for k in range(2):
                at = pl.multiple_of((2 * k + 1 - place_ref[1]) * quarter, quarter)
                cols_ref[n, :, k * quarter : (k + 1) * quarter] = ref[:, pl.ds(at, quarter)]
        sums = jnp.concatenate(
            [gain_two, gain_three, shift_two, shift_three]
            + [column_sum(v) for v in (f1, f2, e3)]
            + [jnp.zeros_like(gain_two)],
            0,
        )

        @pl.when(first)
        def _():
            sum_ref[...] = sums

        @pl.when(jnp.logical_not(first))
        def _():
            sum_ref[...] += sums

        @pl.when(pl.program_id(0) == steps - 1)
        def _():
            dt_ref[0] = dtk_sum[...].astype(BF)
            dt_ref[1] = dtv_sum[...].astype(BF)

    row, half = row_spec(size, width), row_spec(size, width // 2)
    square, text = whole_spec((width, width)), whole_spec((slots, width))
    low, narrow = out_struct(rows, width), out_struct(rows, width // 2)
    pairs = width // PAIR
    return call(
        kernel,
        "middle_backward",
        (low, low, low, out_struct(rows, width, F32), narrow, narrow)
        + (jax.ShapeDtypeStruct((3, rows, width // 2), BF),)
        + (jax.ShapeDtypeStruct((2, slots, width), BF),)
        + (out_struct(8, width, F32),),
        (steps,),
        [whole_spec((slots, 1))]
        + [row] * 6
        + [pl.BlockSpec((1, pairs, 2 * size), lambda i, *_: (i, 0, 0))]
        + head_row_specs(width)
        + [whole_spec(gains.shape), square, text, text, square],
        (row,) * 4
        + (half,) * 2
        + (pl.BlockSpec((3, size, width // 2), lambda i, *_: (0, i, 0)),)
        + (whole_spec((2, slots, width)),)
        + (whole_spec((8, width)),),
        scratch=[
            pltpu.VMEM((size, width), BF),
            pltpu.VMEM((slots, width), F32),
            pltpu.VMEM((slots, width), F32),
        ],
    )(place, live, dm, e3, h1, h2, qc, oc, logs, *[self_out] * 4, gains, wq, tk, tv, wo)


def mlp_part(place, m, e3, w_in, w_out, bias, start, dm_sum, part, tile):
    rows, width = m.shape
    hidden = w_in.shape[1] // 2
    steps = hidden // tile
    turn = steps // 2

    def column(t, place):
        ahead = t < turn
        side = jnp.where(ahead, 1 - place[1], place[1])
        return side * turn + jnp.where(ahead, t, t - turn)

    def kernel(place_ref, m_ref, e3_ref, in_ref, out_ref, bias_ref, *refs):
        starts, (g_ref, far_ref, near_ref, sum_ref, dm_ref, *outs, o_ref) = refs[:2], refs[2:]
        t = pl.program_id(0)

        @pl.when(t == 0)
        def _():
            o_ref[...] = starts[0][...] + starts[1][2:3] if part == 0 else starts[0][...]
            dm_ref[...] = jnp.zeros_like(dm_ref) if part == 0 else starts[1][...]

        g, slope = gelu_and_slope(dot(m_ref[...], in_ref[...], 1, 0) + bias_ref[...])
        g = g.astype(BF)
        g_ref[...] = g
        dg = dot(e3_ref[...], out_ref[...], 1, 1).astype(BF).astype(F32)
        d = (dg * slope).astype(BF)

        @pl.when(t < turn)
        def _():
            far_ref[...] = d

        @pl.when(t >= turn)
        def _():
            near_ref[...] = d

        sum_ref[...] = column_sum(d)
        o_ref[...] += dot(g, out_ref[...], 1, 0)
        dm_ref[...] += dot(d, in_ref[...], 1, 1)

        if part:

            @pl.when(t == steps - 1)
            def _():
                outs[0][...] = o_ref[: rows // 2]
                outs[1][...] = o_ref[rows // 2 :].astype(BF)

    full = whole_spec((rows, width))
    wide = pl.BlockSpec((rows, tile), lambda t, place: (0, column(t, place)))
    second = whole_spec(dm_sum.shape)
    return call(
        kernel,
        "mlp",
        (out_struct(rows, hidden), out_struct(rows, hidden // 2), out_struct(rows, hidden // 2))
        + (out_struct(1, hidden, F32), out_struct(rows, width, F32))
        + (
            (out_struct(rows // 2, width, F32), out_struct(rows // 2, width))
            if part
            else (out_struct(rows, width, F32),)
        ),
        (steps,),
        [
            full,
            full,
            pl.BlockSpec((width, tile), lambda t, place: (0, part * steps + column(t, place))),
            pl.BlockSpec((tile, width), lambda t, place: (part * steps + column(t, place), 0)),
            pl.BlockSpec((1, tile), lambda t, place: (0, part * steps + column(t, place))),
            full,
            second,
        ],
        (
            wide,
            pl.BlockSpec((rows, tile), lambda t, place: (0, jnp.minimum(t, turn - 1))),
            pl.BlockSpec((rows, tile), lambda t, place: (0, jnp.maximum(t - turn, 0))),
            pl.BlockSpec((1, tile), lambda t, place: (0, column(t, place))),
            full,
        )
        + ((whole_spec((rows // 2, width)),) * 2 if part else (full,)),
        scratch=[pltpu.VMEM((rows, width), F32)] if part else [],
    )(place, m, e3, w_in, w_out, bias, start, dm_sum)


def part_out(place_ref, write):
    core = place_ref[1]
    mine = jnp.where(core == 0, place_ref[2], place_ref[3])
    for ahead, output in ((1 - mine, 0), (mine, 1)):
        for behind in range(2):
            write(
                output,
                behind,
                jnp.where(core == 0, ahead, behind),
                jnp.where(core == 0, behind, ahead),
            )


def core_columns(rows, quarter):
    return [
        pl.BlockSpec((rows, quarter), lambda t, place, k=k: (0, 2 * k + place[1]))
        for k in range(2)
    ]


def pair_struct(shape):
    return (jax.ShapeDtypeStruct(shape, BF),) * 2


def grad_down(place, units, mate_units, e3, e3_mate, steps):
    rows, half = units.shape
    quarter = e3.shape[1] // 4
    tile = half // steps

    def kernel(place_ref, own, mate, *refs):
        sent, kept, turned, both = refs[-4:]

        @pl.when(pl.program_id(0) == 0)
        def _():
            for k in range(2):
                at = slice(k * quarter, (k + 1) * quarter)
                turned[at, :rows] = refs[k][...].T
                turned[at, rows:] = refs[2 + k][...].T

        total = dot(turned[:, :rows], own[...], 1, 0) + dot(turned[:, rows:], mate[...], 1, 0)
        for k in range(2):
            for y in range(2):
                both[y, k] = total[
                    k * quarter : (k + 1) * quarter, y * (tile // 2) : (y + 1) * (tile // 2)
                ].astype(BF)

        def write(output, behind, one, two):
            (sent, kept)[output][behind, 0] = both[one, two]

        part_out(place_ref, write)

    wide = pl.BlockSpec((rows, tile), lambda t, place: (0, t))
    out = pl.BlockSpec((2, 1, quarter, tile // 2), lambda t, place: (0, t, 0, 0))
    return call(
        kernel,
        "grad_down",
        pair_struct((2, steps, quarter, tile // 2)),
        (steps,),
        [wide, wide] + core_columns(rows, quarter) * 2,
        (out, out),
        scratch=[pltpu.VMEM((2 * quarter, 2 * rows), BF), pltpu.VMEM((2, 2, quarter, tile // 2), BF)],
    )(place, units, mate_units, e3, e3, e3_mate, e3_mate)


def transposed(place, array):
    def kernel(place_ref, from_ref, to_ref):
        to_ref[...] = from_ref[...].T

    rows, cols = array.shape
    return call(
        kernel,
        "transposed",
        jax.ShapeDtypeStruct((cols, rows), array.dtype),
        (1,),
        [whole_spec((rows, cols))],
        whole_spec((cols, rows)),
    )(place, array)


def row_blocks(one_bit, two_bit, count):
    at = []
    for rest in range(count // 4):
        low, high = min(one_bit, two_bit), max(one_bit, two_bit)
        rest = ((rest >> low) << (low + 1)) | (rest & ((1 << low) - 1))
        rest = ((rest >> high) << (high + 1)) | (rest & ((1 << high) - 1))
        at.append(rest)
    return at


def grad_up(place, m, m_mate, grads, mate_grads, bits, count):
    rows, depth = m.shape
    cols = grads.shape[1]
    size = depth // count
    others = row_blocks(*bits, count)

    def kernel(place_ref, m_ref, mate_ref, own, mate, *refs):
        sent, kept, both = refs[-3:]
        total = dot(m_ref[...].T, own[...], 1, 0) + dot(mate_ref[...].T, mate[...], 1, 0)
        for w in range(count):
            both[w] = total[w * size : (w + 1) * size].astype(BF)

        def write(output, behind, one, two):
            for n, rest in enumerate(others):
                (sent, kept)[output][behind, n] = both[
                    rest + (one << bits[0]) + (two << bits[1])
                ]

        part_out(place_ref, write)

    shape = (2, count // 4, size, cols)
    return call(
        kernel,
        "grad_up",
        pair_struct(shape),
        (1,),
        [whole_spec((rows, depth))] * 2 + [whole_spec((rows, cols))] * 2,
        (whole_spec(shape),) * 2,
        scratch=[pltpu.VMEM((count, size, cols), BF)],
    )(place, m, m_mate, grads, mate_grads)


def grad_square(place, members, count, bits=None):
    arrays, specs, plan = [], [], []
    known = {}
    for member in members:
        pieces = []
        for left, block, right, lead, whole in member:
            rows, depth = right.shape[-2], left.shape[1]
            quarter = right.shape[-1] // (4 if whole else 2)
            if (id(left), block) not in known:
                known[id(left), block] = len(arrays)
                arrays.append(left)
                specs.append(
                    pl.BlockSpec((rows, depth), lambda t, place, block=block: (block, 0))
                )
            pieces.append((known[id(left), block], len(arrays)))
            arrays += [right, right]
            for k in range(2):

                def column(t, place, k=k, lead=lead, whole=whole):
                    return (*lead, 0, 2 * k + place[1] if whole else k)

                specs.append(pl.BlockSpec((None,) * len(lead) + (rows, quarter), column))
        plan.append(pieces)
    size = depth // count
    others = row_blocks(*bits, count) if bits else range(count // 2)

    def kernel(place_ref, *refs):
        sent, kept, both = refs[-3:]
        turned = {}
        for n, pieces in enumerate(plan):
            total = 0.0
            for left, right in pieces:
                if left not in turned:
                    turned[left] = refs[left][...].T
                cols = jnp.concatenate([refs[right][...], refs[right + 1][...]], 1)
                total = total + dot(turned[left], cols, 1, 0)
            for w in range(count):
                rows = total[w * size : (w + 1) * size].astype(BF)
                if bits:
                    both[w] = rows
                else:
                    for k in range(2):
                        both[w, k] = rows[:, k * quarter : (k + 1) * quarter]

            def write(output, behind, one, two):
                for n_rest, rest in enumerate(others):
                    if bits:
                        found = both[rest + (one << bits[0]) + (two << bits[1])]
                    else:
                        found = both[2 * rest + one, two]
                    (sent, kept)[output][behind, n_rest, n] = found

            part_out(place_ref, write)

    tile = (size, 2 * quarter) if bits else (2, size, quarter)
    shape = (2, len(others), len(members)) + tile[-2:]
    return call(
        kernel,
        "grad_square",
        pair_struct(shape),
        (1,),
        specs,
        (whole_spec(shape),) * 2,
        scratch=[pltpu.VMEM((count,) + tile, BF)],
    )(place, *arrays)


def first_backward(place, d, d_other, qkv, gains, x, e1, size):
    rows, width = x.shape
    quarter, steps = width // 4, rows // size

    def kernel(place_ref, d_ref, other_ref, gain_ref, x_ref, e1_ref, *refs):
        weights, (own_ref, far_ref, sum_ref) = refs[:12], refs[12:]
        grad = jnp.zeros((size, width), F32)
        for j in range(3):
            for k in range(2):
                cols = slice(k * quarter, (k + 1) * quarter)
                grad = grad + dot(d_ref[j][:, cols], weights[4 * j + k][0], 1, 1)
                grad = grad + dot(other_ref[j][:, cols], weights[4 * j + 2 + k][0], 1, 1)
        grad, gain, shift = norm_back(grad, gain_ref[0:1], x_ref[...].astype(F32))
        total = e1_ref[...] + grad
        sums = jnp.concatenate([gain, shift], 0)

        @pl.when(pl.program_id(0) == 0)
        def _():
            own_ref[...] = total
            sum_ref[...] = sums

        @pl.when(pl.program_id(0) == 1)
        def _():
            far_ref[...] = total.astype(BF)
            sum_ref[...] += sums

    def weight_spec(j, flip, k):
        return pl.BlockSpec(
            (1, width, quarter), lambda i, place: (j, 0, 2 * k + (place[1] ^ flip))
        )

    return call(
        kernel,
        "first_backward",
        (out_struct(size, width, F32), out_struct(size, width), out_struct(2, width, F32)),
        (steps,),
        [
            pl.BlockSpec((3, size, width // 2), lambda i, *_: (0, i, 0)),
            pl.BlockSpec((3, size, width // 2), lambda i, *_: (0, i, 0)),
        ]
        + [whole_spec(gains.shape), row_spec(size, width), row_spec(size, width)]
        + [weight_spec(j, flip, k) for j in range(3) for flip in range(2) for k in range(2)],
        (whole_spec((size, width)), whole_spec((size, width)), whole_spec((2, width))),
    )(place, d, d_other, gains, x, e1, *[qkv] * 12)


def body(
    image_tokens,
    text_states,
    caption_lengths,
    text_mask,
    self_qkv,
    self_out,
    cross_query,
    cross_kv,
    cross_out,
    mlp_in,
    mlp_out,
    norm_gains,
    norm_shifts,
    out_biases,
    mlp_bias,
    cotangent,
):
    _, block, width = image_tokens.shape
    blocks = lax.axis_size("narrow")
    wide_size = lax.axis_size("wide")
    here = lax.axis_index("narrow")
    line = lax.axis_index("wide")
    chip, core = here // 2, here % 2
    wide_bits = wide_size.bit_length() - 1
    mates = [(i, i ^ 1) for i in range(blocks)]
    across = [(i, i ^ 2) for i in range(blocks)]

    def to_mate(value):
        return lax.ppermute(value, "narrow", mates)

    def to_chip(value):
        return lax.ppermute(value, "narrow", across)

    def item(array, index):
        return lax.dynamic_index_in_dim(array, index, 0, keepdims=False)

    def columns(array, side):
        quarter = array.shape[-1] // 4
        return jnp.concatenate(
            [
                lax.dynamic_slice_in_dim(array, (2 * k + side) * quarter, quarter, array.ndim - 1)
                for k in range(2)
            ],
            -1,
        )

    def chosen(first, second):
        return jnp.where(core == 0, first, second), jnp.where(core == 0, second, first)

    near = list(range(wide_bits))

    def partner(index, axis):
        line_at, here_at = divmod(index, blocks)
        if axis == "x":
            return line_at * blocks + (here_at ^ 2)
        return (line_at ^ (1 << axis)) * blocks + here_at

    def exchange(value, first, second=None):
        axes = (first, first if second is None else second)
        pairs = [(i, partner(i, axes[i % 2])) for i in range(wide_size * blocks)]
        return lax.ppermute(value, ("wide", "narrow"), pairs)

    def bit_of(axis):
        return chip if axis == "x" else (line >> axis) & 1

    class Scatter:
        def __init__(self, shape, one, two, dims):
            self.shape, self.axes, self.dims = shape, (one, two), dims
            self.kept, self.come = [], []

        def add(self, halves, *others):
            self.sent, kept = (half.reshape(self.shape) for half in halves)
            self.kept.append(kept)
            self.come.append(exchange(after(self.sent, *others), *self.axes))
            self.terms = [(tuple(self.kept), {}), (tuple(self.come), {})]
            self.count = len(self.kept)

        def values(self, extra):
            found = []
            for parts, taken in self.terms:
                taken = {**taken, **extra}
                split = len(parts) > 1
                which = taken.pop(1, None) if split else None
                pieces = []
                for array in parts:
                    at = [taken.get(d, 0) * (n // 2) for d, n in enumerate(array.shape)]
                    size = [n // 2 if d in taken else n for d, n in enumerate(array.shape)]
                    pieces.append(lax.dynamic_slice(array, at, size) if taken else array)
                if which is not None:
                    pieces = [jnp.where(which == 0, *pieces)]
                elif self.count > 1 and not split:
                    pieces = jnp.split(pieces[0], self.count, 1)
                found.append([piece.astype(F32) for piece in pieces])
            return [sum(pieces) for pieces in zip(*found)]

        def advance(self, bit, dim, *axes):
            if dim == 1:
                self.count = 1
            sums = [value.astype(BF) for value in self.values({dim: 1 - bit})]
            self.sent = sums[0] if len(sums) == 1 else jnp.concatenate(sums, 1)
            self.terms = [(parts, {**taken, dim: bit}) for parts, taken in self.terms]
            self.terms.append(((exchange(self.sent, *axes),), {}))

        def turn(self):
            one, two = self.axes
            self.advance(jnp.where(core == 0, bit_of(two), bit_of(one)), 0, two, one)

        def step(self, axis):
            self.advance(bit_of(axis), self.dims[axis], axis)

        def wait(self, *others):
            arrays = tuple(parts for parts, _ in self.terms)
            arrays = lax.optimization_barrier((arrays,) + others)[0]
            self.terms = [(a, taken) for a, (_, taken) in zip(arrays, self.terms)]

        def total(self, *shape):
            return self.values({})[0].reshape(shape)

    def bit_dims(first, *left_out):
        bits = [b for b in reversed(near) if b not in left_out]
        return (2,) * len(bits), {b: first + n for n, b in enumerate(bits)}

    def places(one, two):
        return jnp.stack([here, core, bit_of(one), bit_of(two)]).astype(jnp.int32)

    def both(own_part, mate_part):
        return jnp.concatenate([own_part, mate_part], 0)

    def after(value, *others):
        return lax.optimization_barrier((value,) + others)[0]

    rows_wide = width // wide_size
    quarter = width // 4

    def home(own, far):
        far = far.astype(F32)
        return jnp.where((jnp.arange(2) == chip)[:, None, None], own[None], far[None])

    own = jnp.concatenate([item(image_tokens, chip), item(text_states, chip)], 0)
    far = to_chip(
        jnp.concatenate([item(image_tokens, 1 - chip), item(text_states, 1 - chip)], 0)
    )
    own_mate = to_mate(own)
    place = jnp.stack([here, core]).astype(jnp.int32)
    first = project(place, own, own_mate, self_qkv, norm_gains, norm_shifts, 0, block, None)
    far = after(far, first[0])
    far_mate = to_mate(far)
    a, q, k, v = project(
        place, far, far_mate, self_qkv, norm_gains, norm_shifts, 1, block, first
    )
    x = both(own[:block], far[:block])
    text_all = jnp.concatenate(
        chosen(both(own[block:], far[block:]), both(own_mate[block:], far_mate[block:])), 0
    )
    slot_block = text_states.shape[1]
    slots = slot_block * blocks
    slot_order = jnp.stack([(2 * chip) ^ k for k in (0, 2, 1, 3)])
    slot = (slot_order[:, None] * slot_block + jnp.arange(slot_block)[None, :]).reshape(slots)
    kept = item(text_mask, chip).reshape(blocks, slot_block)
    kept = jnp.concatenate([item(kept, (2 * chip) ^ k) for k in (0, 2, 1, 3)], 0)
    length = item(caption_lengths, chip)
    live = ((slot < length) & ((kept == 1) | (slot == 0))).astype(F32).reshape(slots, 1)

    tk = dot(text_all, cross_kv[0], 1, 0).astype(BF)
    tv = dot(text_all, cross_kv[1], 1, 0).astype(BF)

    rows = 2 * block
    cot_far = to_chip(after(item(cotangent, 1 - chip), q))
    q = after(q, tk, tv)
    o, o_mate, log_self = self_forward(place, q, k, v, blocks)
    o_other = to_mate(after(o_mate, cot_far))
    e3 = both(item(cotangent, chip), cot_far)
    os_rows, h1, c, qc, oc, log_cross, h2, m = middle_forward(
        place,
        live,
        x,
        o,
        o_other,
        self_out,
        norm_gains,
        norm_shifts,
        out_biases,
        cross_query,
        tk,
        tv,
        cross_out,
        block,
    )
    e3_mate, m_mate = to_mate(e3), to_mate(m)
    c_mate, oc_mate, os_mate = to_mate(c), to_mate(oc), to_mate(os_rows)
    bias_row = mlp_bias.reshape(1, -1)
    sums = (h2, out_biases)
    g, g_mate, kept, kept_mate, hidden_sums = [], [], [], [], []
    for part in range(2):
        units, sent, stay, hidden_sum, dm, *outs = mlp_part(
            place, m, e3, mlp_in, mlp_out, bias_row, *sums, part, TILE
        )
        g.append(units)
        g_mate.append(to_mate(units))
        kept.append(stay)
        kept_mate.append(to_mate(sent))
        hidden_sums.append(hidden_sum)
        if part == 0:
            sums = (outs[0], after(dm, e3_mate, m_mate, c_mate, oc_mate, os_mate))
    layer_out, out_far = outs
    out_far = to_chip(out_far)
    up_bits = (near[1], near[0])
    shape, dims = bit_dims(2, near[0], near[-1])
    dims[near[-1]] = 1
    down = Scatter(
        (2, 1) + shape + (quarter, mlp_out.shape[0] // wide_size), near[0], "x", dims
    )
    shape, dims = bit_dims(2, *up_bits)
    dims["x"] = 1
    up = Scatter((2, 1) + shape + (rows_wide, mlp_in.shape[1] // 4), *up_bits, dims)
    for part in range(2):
        down.add(
            grad_down(
                places(near[0], "x"), g[part], g_mate[part], e3, e3_mate, wide_size // 4
            )
        )
        kept[part] = after(kept[part], down.sent)
        up.add(
            grad_up(
                places(*up_bits), m, m_mate, kept[part], kept_mate[part], up_bits, wide_size
            )
        )
        if part == 0:
            g[1] = after(g[1], up.sent, out_far)
    dm = after(dm, up.sent)

    f2, dqc, f1, e1, do_own, do_other, cols, dt, row_sums = middle_backward(
        place,
        live,
        dm,
        e3,
        h1,
        h2,
        qc,
        oc,
        log_cross,
        self_out,
        norm_gains,
        cross_query,
        tk,
        tv,
        cross_out,
        block,
    )
    dt_mate, cols_mate, do_mate = to_mate(dt), to_mate(cols), to_mate(do_other)
    down.wait(row_sums)
    down.turn()
    up.wait(row_sums, down.sent)
    up.turn()
    dt_mate = after(dt_mate, up.sent, down.sent)
    dt = (dt.astype(F32) + dt_mate.astype(F32)).astype(BF)
    outer_axes = (near[1], near[0])
    shape, dims = bit_dims(1, *outer_axes)
    shape = (2,) + shape + (5, rows_wide, 2 * quarter)
    dims["x"] = len(shape) - 1
    outer = Scatter(shape, *outer_axes, dims)
    outer_halves = (
        grad_square(
            places(*outer_axes),
            [
                [(oc, 0, f2, (), True), (oc_mate, 0, cols_mate, (0,), False)],
                [(text_all, 0, dt, (0,), True)],
                [(text_all, 0, dt, (1,), True)],
                [(c, 0, dqc, (), True), (c_mate, 0, cols_mate, (1,), False)],
                [(os_rows, 0, f1, (), True), (os_mate, 0, cols_mate, (2,), False)],
            ],
            wide_size,
            outer_axes,
        )
    )
    down.wait(outer_halves)
    down.step(near[1])
    up.wait(outer_halves, down.sent)
    up.step("x")
    outer.add(outer_halves, down.sent, up.sent)
    do_mate = after(do_mate, down.sent, up.sent)
    d, d_mate = self_backward(place, q, k, v, o, o_mate, do_own, do_mate, log_self, blocks)
    d_other = to_mate(d_mate)
    shape, dims = bit_dims(1, near[0])
    inner = Scatter((2,) + shape + (3, rows_wide, quarter), near[0], "x", dims)
    inner.add(
        grad_square(
            places(near[0], "x"),
            [[(a, 0, d, (j,), False), (a, 1, d_mate, (j,), False)] for j in range(3)],
            wide_size,
        )
    )
    d_other = after(d_other, inner.sent)
    grad_own, grad_far, late = first_backward(
        place, d, d_other, self_qkv, norm_gains, x, e1, block
    )
    image_far = to_chip(grad_far)
    late = jnp.concatenate(
        [late, row_sums[:7], jnp.concatenate(hidden_sums, 1).reshape(-1, width)]
    )
    late = late + to_mate(late)
    outer.wait(grad_far)
    outer.turn()
    for axis in near[2:]:
        down.wait(outer.sent)
        down.step(axis)
        up.wait(down.sent)
        up.step(axis)
    inner.wait(up.sent)
    inner.turn()
    for axis in near[1:]:
        late = late + exchange(late, axis)
    late_far = exchange(after(late, inner.sent), near[0])
    outer.wait(inner.sent)
    outer.step("x")
    late = late + after(late_far, outer.sent)
    late_far = to_chip(late)
    inner.wait(outer.sent)
    inner.step(near[1])
    dt_own = lax.dynamic_slice_in_dim(dt, core * 2 * slot_block, 2 * slot_block, 1)
    dt_own = after(dt_own, inner.sent)
    grad_text = dot(dt_own[0], cross_kv[0], 1, 1) + dot(dt_own[1], cross_kv[1], 1, 1)
    text_far = to_chip(grad_text[slot_block:])
    for axis in near[2:]:
        outer.wait(inner.sent)
        outer.step(axis)
        inner.wait(outer.sent)
        inner.step(axis)
    down.wait(inner.sent)
    up.wait(inner.sent)
    outer.wait(inner.sent)
    inner.wait(inner.sent)
    late = late + after(late_far, inner.sent)
    image_far, out_far, text_far = after((image_far, out_far, text_far), inner.sent)

    outer_part = outer.total(5, rows_wide, quarter)
    inner_part = inner.total(3, rows_wide, quarter)
    down_part = transposed(place, down.total(quarter, mlp_out.shape[0] // wide_size))

    gains = jnp.stack([late[0], late[2], late[3]])
    shifts = jnp.stack([late[1], late[4], late[5]])
    return (
        home(layer_out, out_far),
        home(grad_own, image_far),
        home(grad_text[:slot_block], text_far),
        inner_part,
        outer_part[4],
        outer_part[3],
        outer_part[1:3],
        outer_part[0],
        up.total(rows_wide, mlp_in.shape[1] // 4),
        down_part,
        gains,
        shifts,
        late[6:9],
        late[9:].reshape(-1),
    )


def solution(mesh):
    rows = P("wide", "narrow", None)
    whole = P()
    return jax.shard_map(
        body,
        mesh=mesh,
        in_specs=(rows, rows, P("wide"), P("wide", None)) + (whole,) * 11 + (rows,),
        out_specs=(rows,) * 3
        + (
            P(None, "wide", "narrow"),
            P("wide", "narrow"),
            P("wide", "narrow"),
            P(None, "wide", "narrow"),
        )
        + (P("wide", "narrow"),) * 3
        + (whole,) * 4,
        check_vma=False,
    )
```

```python
import jax
import jax.numpy as jnp
from jax import lax
from jax.experimental import pallas as pl
from jax.experimental.pallas import tpu as pltpu
from jax.sharding import PartitionSpec as P

HEAD_DIM = 64
PAIR = 2 * HEAD_DIM
SCALE = HEAD_DIM**-0.5
NEG = -1e30
BF = jnp.bfloat16
F32 = jnp.float32
VMEM = 56 * 1024 * 1024
TILE = 1024


def dot(left, right, left_axis, right_axis):
    return lax.dot_general(
        left, right, (((left_axis,), (right_axis,)), ((), ())), preferred_element_type=F32
    )


def two_heads(rows):
    lane = lax.broadcasted_iota(jnp.int32, rows.shape, 1)
    zero = jnp.zeros_like(rows)
    return jnp.concatenate(
        [jnp.where(lane < HEAD_DIM, rows, zero), jnp.where(lane < HEAD_DIM, zero, rows)], 0
    )


def block_rows(here, block, size):
    slot = here ^ block
    return pl.ds(pl.multiple_of(((slot & 1) * 2 + slot // 2) * size, size), size)


def slot_place(here, block, size):
    slot = here ^ block
    return slot & 1, pl.ds(pl.multiple_of((slot // 2) * size, size), size)


def store_sides(here, block, size, even, odd, own_ref, mate_ref):
    _, half = slot_place(here, block, size)
    own_first = (here & 1) == 0
    own_ref[half, :] = jnp.where(own_first, even, odd)
    mate_ref[half, :] = jnp.where(own_first, odd, even)


def causal_mask(scores, size):
    key = lax.broadcasted_iota(jnp.int32, scores.shape, 0)
    query = lax.broadcasted_iota(jnp.int32, scores.shape, 1)
    return jnp.where(key <= lax.rem(query, size), scores, NEG)


def self_forward_kernel(here_ref, q_ref, k_ref, v_ref, own_ref, mate_ref, log_ref, *, blocks):
    here = here_ref[0]
    size = q_ref.shape[0] // blocks
    for p in range(blocks):
        rows = block_rows(here, p, size)
        queries = two_heads(q_ref[rows, :] * BF(SCALE))
        scores = []
        for j in range(p + 1):
            s = dot(k_ref[block_rows(here, j, size), :], queries, 1, 1)
            scores.append(causal_mask(s, size) if j == p else s)
        top = scores[0].max(0, keepdims=True)
        for s in scores[1:]:
            top = jnp.maximum(top, s.max(0, keepdims=True))
        total = jnp.zeros_like(top)
        mixed = [jnp.zeros((HEAD_DIM, size), F32)] * 2
        for j in range(p + 1):
            e = jnp.exp(scores[j] - top)
            total = total + e.sum(0, keepdims=True)
            low = e.astype(BF)
            values = v_ref[block_rows(here, j, size), :].T
            for h in range(2):
                mixed[h] = mixed[h] + dot(
                    values[h * HEAD_DIM : (h + 1) * HEAD_DIM],
                    low[:, h * size : (h + 1) * size],
                    1,
                    0,
                )
        inverse = 1.0 / total
        both = jnp.concatenate(
            [mixed[h] * inverse[:, h * size : (h + 1) * size] for h in range(2)], 0
        )
        low = both.T.astype(BF)
        if p % 2:
            store_sides(here, p - 1, size, before, low, own_ref, mate_ref)
        before = low
        log_ref[0, :, 2 * size * p : 2 * size * (p + 1)] = top + jnp.log(total)


def row_dots(left, right):
    product = left.astype(F32).T * right.astype(F32).T
    return jnp.concatenate(
        [product[:HEAD_DIM].sum(0, keepdims=True), product[HEAD_DIM:].sum(0, keepdims=True)], 1
    )


def self_backward_kernel(
    here_ref,
    q_ref,
    k_ref,
    v_ref,
    o_ref,
    o_mate_ref,
    do_ref,
    do_mate_ref,
    log_ref,
    *sides,
    blocks,
):
    here = here_ref[0]
    size = q_ref.shape[0] // blocks
    queries, grads, inner, dq = [], [], [], []
    for p in range(blocks):
        rows = block_rows(here, p, size)
        queries.append(two_heads(q_ref[rows, :] * BF(SCALE)))
        side, half = slot_place(here, p, size)
        do = jnp.where(side == 0, do_ref[half, :], do_mate_ref[half, :])
        grads.append(two_heads(do))
        o = jnp.where(side == 0, o_ref[half, :], o_mate_ref[half, :])
        inner.append(row_dots(do, o))
        dq.append([jnp.zeros((HEAD_DIM, size), F32)] * 2)
    for j in range(blocks):
        rows = block_rows(here, j, size)
        keys, values = k_ref[rows, :], v_ref[rows, :]
        turned = keys.T
        dk = jnp.zeros(keys.shape, F32)
        dv = jnp.zeros(keys.shape, F32)
        for p in range(j, blocks):
            s = dot(keys, queries[p], 1, 1)
            if j == p:
                s = causal_mask(s, size)
            probs = jnp.exp(s - log_ref[0, :, 2 * size * p : 2 * size * (p + 1)])
            dprobs = dot(values, grads[p], 1, 1)
            ds = (probs * (dprobs - inner[p])).astype(BF)
            dv = dv + dot(probs.astype(BF), grads[p], 1, 0)
            dk = dk + dot(ds, queries[p], 1, 0)
            for h in range(2):
                dq[p][h] = dq[p][h] + dot(
                    turned[h * HEAD_DIM : (h + 1) * HEAD_DIM],
                    ds[:, h * size : (h + 1) * size],
                    1,
                    0,
                )
        low = dk.astype(BF), dv.astype(BF)
        if j % 2:
            for n in range(2):
                store_sides(here, j - 1, size, before[n], low[n], sides[1 + n], sides[4 + n])
        before = low
    for p in range(blocks):
        both = jnp.concatenate(dq[p], 0) * SCALE
        low = both.T.astype(BF)
        if p % 2:
            store_sides(here, p - 1, size, before, low, sides[0], sides[3])
        before = low


def pair_spec(rows):
    return pl.BlockSpec((rows, PAIR), lambda i, *_: (0, i))


def log_spec(width):
    return pl.BlockSpec((1, 1, width), lambda i, *_: (i, 0, 0))


def self_forward(here, q, k, v, blocks):
    rows, width = q.shape
    pairs = width // PAIR
    spec = pair_spec(rows)
    return pl.pallas_call(
        lambda *refs: self_forward_kernel(*refs, blocks=blocks),
        name="self_forward",
        out_shape=(
            jax.ShapeDtypeStruct((rows // 2, width), BF),
            jax.ShapeDtypeStruct((rows // 2, width), BF),
            jax.ShapeDtypeStruct((pairs, 1, 2 * rows), F32),
        ),
        grid_spec=pltpu.PrefetchScalarGridSpec(
            num_scalar_prefetch=1,
            grid=(pairs,),
            in_specs=[spec] * 3,
            out_specs=(pair_spec(rows // 2), pair_spec(rows // 2), log_spec(2 * rows)),
        ),
        compiler_params=pltpu.CompilerParams(vmem_limit_bytes=VMEM),
        cost_estimate=pl.CostEstimate(flops=10**6, bytes_accessed=10**5, transcendentals=0),
    )(here, q, k, v)


def self_backward(here, q, k, v, o, o_mate, do, do_mate, log_total, blocks):
    rows, width = q.shape
    pairs = width // PAIR
    spec = pair_spec(rows)
    return pl.pallas_call(
        lambda *refs: self_backward_kernel(*refs, blocks=blocks),
        name="self_backward",
        out_shape=(jax.ShapeDtypeStruct((rows // 2, width), BF),) * 6,
        grid_spec=pltpu.PrefetchScalarGridSpec(
            num_scalar_prefetch=1,
            grid=(pairs,),
            in_specs=[spec] * 3 + [pair_spec(rows // 2)] * 4 + [log_spec(2 * rows)],
            out_specs=(pair_spec(rows // 2),) * 6,
        ),
        compiler_params=pltpu.CompilerParams(vmem_limit_bytes=VMEM),
        cost_estimate=pl.CostEstimate(flops=10**6, bytes_accessed=10**5, transcendentals=0),
    )(here, q, k, v, o, o_mate, do, do_mate, log_total)


def standardize(rows):
    centered = rows - jnp.mean(rows, -1, keepdims=True)
    inverse = lax.rsqrt(jnp.mean(centered * centered, -1, keepdims=True) + 1e-05)
    return centered * inverse, inverse


def normed(rows, gain, shift):
    return (standardize(rows)[0] * gain + shift).astype(BF)


def norm_back(grad_out, gain, rows):
    unit, inverse = standardize(rows)
    grad_unit = grad_out * gain
    grad_in = inverse * (
        grad_unit
        - jnp.mean(grad_unit, -1, keepdims=True)
        - unit * jnp.mean(grad_unit * unit, -1, keepdims=True)
    )
    return grad_in, column_sum(grad_out * unit), column_sum(grad_out)


def column_sum(rows):
    return jnp.sum(rows.astype(F32), 0, keepdims=True)


def gelu_and_slope(pre):
    square = pre * pre
    bend = jnp.tanh(pre * (0.7978845608028654 + (0.7978845608028654 * 0.044715) * square))
    half = 0.5 + 0.5 * bend
    value = pre * half
    steep = 0.7978845608028654 + (3.0 * 0.7978845608028654 * 0.044715) * square
    return value, half + value * (1.0 - bend) * steep


def whole_spec(shape):
    return pl.BlockSpec(shape, lambda *_: (0,) * len(shape))


def row_spec(rows, cols, start=0):
    return pl.BlockSpec((rows, cols), lambda i, *_: (start + i, 0))


def call(kernel, name, out_shape, grid, in_specs, out_specs, scratch=(), aliases=None):
    return pl.pallas_call(
        kernel,
        name=name,
        out_shape=out_shape,
        grid_spec=pltpu.PrefetchScalarGridSpec(
            num_scalar_prefetch=1,
            grid=grid,
            in_specs=in_specs,
            out_specs=out_specs,
            scratch_shapes=scratch,
        ),
        input_output_aliases=aliases or {},
        compiler_params=pltpu.CompilerParams(vmem_limit_bytes=VMEM),
        cost_estimate=pl.CostEstimate(flops=10**6, bytes_accessed=10**5, transcendentals=0),
    )


def out_struct(rows, cols, kind=BF):
    return jax.ShapeDtypeStruct((rows, cols), kind)


def project(place, own, mate, qkv, gains, shifts, half, size, into):
    width = qkv.shape[1]
    quarter = width // 4

    def kernel(place_ref, own_ref, mate_ref, gain_ref, shift_ref, *refs):
        weights, outs = refs[:6], refs[-4:]
        rows = jnp.where(pl.program_id(0) == 0, own_ref[...], mate_ref[...]).astype(F32)
        a = normed(rows, gain_ref[0:1], shift_ref[0:1])
        outs[0][...] = a
        for j in range(3):
            pair = jnp.concatenate([weights[2 * j][0], weights[2 * j + 1][0]], 1)
            outs[1 + j][...] = dot(a, pair, 1, 0).astype(BF)

    def weight_spec(j, k):
        return pl.BlockSpec((1, width, quarter), lambda i, place: (j, 0, 2 * k + place[1]))

    def out_spec(cols):
        return pl.BlockSpec((size, cols), lambda i, place: (2 * i + half, 0))

    specs = [whole_spec((size, width))] * 2 + [whole_spec(gains.shape)] * 2
    specs += [weight_spec(j, k) for j in range(3) for k in range(2)]
    arrays = [own, mate, gains, shifts] + [qkv] * 6
    aliases = None
    if into is not None:
        aliases = {1 + len(arrays) + n: n for n in range(4)}
        arrays += list(into)
        specs += [pl.BlockSpec(memory_space=pl.ANY)] * 4
    rows = 4 * size
    return call(
        kernel,
        "project",
        (out_struct(rows, width),) + (out_struct(rows, width // 2),) * 3,
        (2,),
        specs,
        (out_spec(width),) + (out_spec(width // 2),) * 3,
        aliases=aliases,
    )(place, *arrays)


def head_row_specs(width):
    quarter = width // 4
    return [
        pl.BlockSpec((quarter, width), lambda i, place, k=k, flip=flip: (2 * k + (place[1] ^ flip), 0))
        for flip in range(2)
        for k in range(2)
    ]


def middle_forward(place, live, x, o, o_other, self_out, gains, shifts, biases, wq, tk, tv, wo, size):
    rows, width = x.shape
    quarter, slots, steps = width // 4, tk.shape[0], rows // size

    def kernel(
        place_ref,
        live_ref,
        x_ref,
        o_ref,
        other_ref,
        w0,
        w1,
        w2,
        w3,
        gain_ref,
        shift_ref,
        bias_ref,
        wq_ref,
        tk_ref,
        tv_ref,
        wo_ref,
        os_ref,
        h1_ref,
        c_ref,
        qc_ref,
        oc_ref,
        log_ref,
        h2_ref,
        m_ref,
    ):
        core = place_ref[1]
        h1 = x_ref[...].astype(F32) + bias_ref[0:1]
        for n, (ref, weight) in enumerate(
            ((o_ref, w0), (o_ref, w1), (other_ref, w2), (other_ref, w3))
        ):
            k, side = n % 2, core ^ (n // 2)
            part = ref[:, k * quarter : (k + 1) * quarter]
            at = pl.multiple_of((2 * k + side) * quarter, quarter)
            os_ref[:, pl.ds(at, quarter)] = part
            h1 = h1 + dot(part, weight[...], 1, 0)
        h1_ref[...] = h1
        c = normed(h1, gain_ref[1:2], shift_ref[1:2])
        c_ref[...] = c
        qc_ref[...] = dot(c, wq_ref[...], 1, 0).astype(BF)
        for pair in range(width // PAIR):
            lanes = slice(pair * PAIR, (pair + 1) * PAIR)
            queries = two_heads(qc_ref[:, lanes] * BF(SCALE))
            s = dot(tk_ref[:, lanes], queries, 1, 1)
            s = jnp.where(live_ref[...] > 0, s, NEG)
            top = s.max(0, keepdims=True)
            e = jnp.exp(s - top)
            total = e.sum(0, keepdims=True)
            low = e.astype(BF)
            values = tv_ref[:, lanes].T
            inverse = 1.0 / total
            both = jnp.concatenate(
                [
                    dot(
                        values[h * HEAD_DIM : (h + 1) * HEAD_DIM],
                        low[:, h * size : (h + 1) * size],
                        1,
                        0,
                    )
                    * inverse[:, h * size : (h + 1) * size]
                    for h in range(2)
                ],
                0,
            )
            oc_ref[:, lanes] = both.T.astype(BF)
            log_ref[0, pair : pair + 1] = top + jnp.log(total)
        h2 = h1 + dot(oc_ref[...], wo_ref[...], 1, 0) + bias_ref[1:2]
        h2_ref[...] = h2
        m_ref[...] = normed(h2, gain_ref[2:3], shift_ref[2:3])

    row = row_spec(size, width)
    square = whole_spec((width, width))
    low, high = out_struct(rows, width), out_struct(rows, width, F32)
    pairs = width // PAIR
    return call(
        kernel,
        "middle_forward",
        (low, high, low, low, low, jax.ShapeDtypeStruct((steps, pairs, 2 * size), F32), high, low),
        (steps,),
        [
            whole_spec((slots, 1)),
            row,
            row_spec(size, width // 2),
            row_spec(size, width // 2),
        ]
        + head_row_specs(width)
        + [whole_spec(gains.shape)] * 3
        + [square, whole_spec((slots, width)), whole_spec((slots, width)), square],
        (row,) * 5 + (pl.BlockSpec((1, pairs, 2 * size), lambda i, *_: (i, 0, 0)), row, row),
    )(place, live, x, o, o_other, *[self_out] * 4, gains, shifts, biases, wq, tk, tv, wo)


def middle_backward(
    place, live, dm, e3, h1, h2, qc, oc, logs, self_out, gains, wq, tk, tv, wo, size
):
    rows, width = h1.shape
    quarter, slots, steps = width // 4, tk.shape[0], rows // size

    def kernel(
        place_ref,
        live_ref,
        dm_ref,
        e3_ref,
        h1_ref,
        h2_ref,
        qc_ref,
        oc_ref,
        log_ref,
        w0,
        w1,
        w2,
        w3,
        gain_ref,
        wq_ref,
        tk_ref,
        tv_ref,
        wo_ref,
        f2_ref,
        dqc_ref,
        f1_ref,
        e1_ref,
        do_ref,
        other_ref,
        cols_f2,
        cols_dqc,
        cols_f1,
        dt_ref,
        sum_ref,
        doc_ref,
        dtk_sum,
        dtv_sum,
    ):
        first = pl.program_id(0) == 0

        @pl.when(first)
        def _():
            dtk_sum[...] = jnp.zeros_like(dtk_sum)
            dtv_sum[...] = jnp.zeros_like(dtv_sum)

        e3 = e3_ref[...].astype(F32)
        grad, gain_three, shift_three = norm_back(dm_ref[...], gain_ref[2:3], h2_ref[...])
        e2 = e3 + grad
        f2 = e2.astype(BF)
        f2_ref[...] = f2
        doc_ref[...] = dot(f2, wo_ref[...], 1, 1).astype(BF)
        for pair in range(width // PAIR):
            lanes = slice(pair * PAIR, (pair + 1) * PAIR)
            queries = two_heads(qc_ref[:, lanes] * BF(SCALE))
            doc = doc_ref[:, lanes]
            grads = two_heads(doc)
            inner = row_dots(doc, oc_ref[:, lanes])
            keys = tk_ref[:, lanes]
            s = dot(keys, queries, 1, 1)
            s = jnp.where(live_ref[...] > 0, s, NEG)
            probs = jnp.exp(s - log_ref[0, pair : pair + 1])
            dprobs = dot(tv_ref[:, lanes], grads, 1, 1)
            ds = (probs * (dprobs - inner)).astype(BF)
            dtv_sum[:, lanes] += dot(probs.astype(BF), grads, 1, 0)
            dtk_sum[:, lanes] += dot(ds, queries, 1, 0)
            turned = keys.T
            both = jnp.concatenate(
                [
                    dot(
                        turned[h * HEAD_DIM : (h + 1) * HEAD_DIM],
                        ds[:, h * size : (h + 1) * size],
                        1,
                        0,
                    )
                    for h in range(2)
                ],
                0,
            )
            dqc_ref[:, lanes] = (both * SCALE).T.astype(BF)
        dc = dot(dqc_ref[...], wq_ref[...], 1, 1)
        grad, gain_two, shift_two = norm_back(dc, gain_ref[1:2], h1_ref[...])
        e1 = e2 + grad
        e1_ref[...] = e1
        f1 = e1.astype(BF)
        f1_ref[...] = f1
        for n, (ref, weight) in enumerate(
            ((do_ref, w0), (do_ref, w1), (other_ref, w2), (other_ref, w3))
        ):
            k = n % 2
            ref[:, k * quarter : (k + 1) * quarter] = dot(f1, weight[...], 1, 1).astype(BF)
        for ref, cols_ref in ((f2_ref, cols_f2), (dqc_ref, cols_dqc), (f1_ref, cols_f1)):
            for k in range(2):
                at = pl.multiple_of((2 * k + 1 - place_ref[1]) * quarter, quarter)
                cols_ref[:, k * quarter : (k + 1) * quarter] = ref[:, pl.ds(at, quarter)]
        sums = jnp.concatenate(
            [gain_two, gain_three, shift_two, shift_three]
            + [column_sum(v) for v in (f1, f2, e3)]
            + [jnp.zeros_like(gain_two)],
            0,
        )

        @pl.when(first)
        def _():
            sum_ref[...] = sums

        @pl.when(jnp.logical_not(first))
        def _():
            sum_ref[...] += sums

        @pl.when(pl.program_id(0) == steps - 1)
        def _():
            dt_ref[0] = dtk_sum[...].astype(BF)
            dt_ref[1] = dtv_sum[...].astype(BF)

    row, half = row_spec(size, width), row_spec(size, width // 2)
    square, text = whole_spec((width, width)), whole_spec((slots, width))
    low, narrow = out_struct(rows, width), out_struct(rows, width // 2)
    pairs = width // PAIR
    return call(
        kernel,
        "middle_backward",
        (low, low, low, out_struct(rows, width, F32), narrow, narrow)
        + (narrow,) * 3
        + (jax.ShapeDtypeStruct((2, slots, width), BF),)
        + (out_struct(8, width, F32),),
        (steps,),
        [whole_spec((slots, 1))]
        + [row] * 6
        + [pl.BlockSpec((1, pairs, 2 * size), lambda i, *_: (i, 0, 0))]
        + head_row_specs(width)
        + [whole_spec(gains.shape), square, text, text, square],
        (row,) * 4
        + (half,) * 5
        + (whole_spec((2, slots, width)),)
        + (whole_spec((8, width)),),
        scratch=[
            pltpu.VMEM((size, width), BF),
            pltpu.VMEM((slots, width), F32),
            pltpu.VMEM((slots, width), F32),
        ],
    )(place, live, dm, e3, h1, h2, qc, oc, logs, *[self_out] * 4, gains, wq, tk, tv, wo)


def mlp_part(place, m, e3, w_in, w_out, bias, start, dm_sum, part, tile):
    rows, width = m.shape
    hidden = w_in.shape[1] // 2
    steps = hidden // tile
    turn = steps // 2

    def column(t, place):
        ahead = t < turn
        side = jnp.where(ahead, 1 - place[1], place[1])
        return side * turn + jnp.where(ahead, t, t - turn)

    def kernel(place_ref, m_ref, e3_ref, in_ref, out_ref, bias_ref, *refs):
        starts, (g_ref, far_ref, near_ref, sum_ref, dm_ref, *outs, o_ref) = refs[:2], refs[2:]
        t = pl.program_id(0)

        @pl.when(t == 0)
        def _():
            o_ref[...] = starts[0][...] + starts[1][2:3] if part == 0 else starts[0][...]
            dm_ref[...] = jnp.zeros_like(dm_ref) if part == 0 else starts[1][...]

        g, slope = gelu_and_slope(dot(m_ref[...], in_ref[...], 1, 0) + bias_ref[...])
        g = g.astype(BF)
        g_ref[...] = g
        dg = dot(e3_ref[...], out_ref[...], 1, 1).astype(BF).astype(F32)
        d = (dg * slope).astype(BF)

        @pl.when(t < turn)
        def _():
            far_ref[...] = d

        @pl.when(t >= turn)
        def _():
            near_ref[...] = d

        sum_ref[...] = column_sum(d)
        o_ref[...] += dot(g, out_ref[...], 1, 0)
        dm_ref[...] += dot(d, in_ref[...], 1, 1)

        if part:

            @pl.when(t == steps - 1)
            def _():
                outs[0][...] = o_ref[: rows // 2]
                outs[1][...] = o_ref[rows // 2 :].astype(BF)

    full = whole_spec((rows, width))
    wide = pl.BlockSpec((rows, tile), lambda t, place: (0, column(t, place)))
    second = whole_spec(dm_sum.shape)
    return call(
        kernel,
        "mlp",
        (out_struct(rows, hidden), out_struct(rows, hidden // 2), out_struct(rows, hidden // 2))
        + (out_struct(1, hidden, F32), out_struct(rows, width, F32))
        + (
            (out_struct(rows // 2, width, F32), out_struct(rows // 2, width))
            if part
            else (out_struct(rows, width, F32),)
        ),
        (steps,),
        [
            full,
            full,
            pl.BlockSpec((width, tile), lambda t, place: (0, part * steps + column(t, place))),
            pl.BlockSpec((tile, width), lambda t, place: (part * steps + column(t, place), 0)),
            pl.BlockSpec((1, tile), lambda t, place: (0, part * steps + column(t, place))),
            full,
            second,
        ],
        (
            wide,
            pl.BlockSpec((rows, tile), lambda t, place: (0, jnp.minimum(t, turn - 1))),
            pl.BlockSpec((rows, tile), lambda t, place: (0, jnp.maximum(t - turn, 0))),
            pl.BlockSpec((1, tile), lambda t, place: (0, column(t, place))),
            full,
        )
        + ((whole_spec((rows // 2, width)),) * 2 if part else (full,)),
        scratch=[pltpu.VMEM((rows, width), F32)] if part else [],
    )(place, m, e3, w_in, w_out, bias, start, dm_sum)


def part_out(place_ref, write):
    core = place_ref[1]
    mine = jnp.where(core == 0, place_ref[2], place_ref[3])
    for ahead, output in ((1 - mine, 0), (mine, 1)):
        for behind in range(2):
            write(
                output,
                behind,
                jnp.where(core == 0, ahead, behind),
                jnp.where(core == 0, behind, ahead),
            )


def core_columns(rows, quarter):
    return [
        pl.BlockSpec((rows, quarter), lambda t, place, k=k: (0, 2 * k + place[1]))
        for k in range(2)
    ]


def pair_struct(shape):
    return (jax.ShapeDtypeStruct(shape, BF),) * 2


def grad_down(place, units, mate_units, e3, e3_mate, steps):
    rows, half = units.shape
    quarter = e3.shape[1] // 4
    tile = half // steps

    def kernel(place_ref, own, mate, *refs):
        sent, kept, turned, both = refs[-4:]

        @pl.when(pl.program_id(0) == 0)
        def _():
            for k in range(2):
                at = slice(k * quarter, (k + 1) * quarter)
                turned[at, :rows] = refs[k][...].T
                turned[at, rows:] = refs[2 + k][...].T

        total = dot(turned[:, :rows], own[...], 1, 0) + dot(turned[:, rows:], mate[...], 1, 0)
        for k in range(2):
            for y in range(2):
                both[y, k] = total[
                    k * quarter : (k + 1) * quarter, y * (tile // 2) : (y + 1) * (tile // 2)
                ].astype(BF)

        def write(output, behind, one, two):
            (sent, kept)[output][behind, 0] = both[one, two]

        part_out(place_ref, write)

    wide = pl.BlockSpec((rows, tile), lambda t, place: (0, t))
    out = pl.BlockSpec((2, 1, quarter, tile // 2), lambda t, place: (0, t, 0, 0))
    return call(
        kernel,
        "grad_down",
        pair_struct((2, steps, quarter, tile // 2)),
        (steps,),
        [wide, wide] + core_columns(rows, quarter) * 2,
        (out, out),
        scratch=[pltpu.VMEM((2 * quarter, 2 * rows), BF), pltpu.VMEM((2, 2, quarter, tile // 2), BF)],
    )(place, units, mate_units, e3, e3, e3_mate, e3_mate)


def transposed(place, array):
    def kernel(place_ref, from_ref, to_ref):
        to_ref[...] = from_ref[...].T

    rows, cols = array.shape
    return call(
        kernel,
        "transposed",
        jax.ShapeDtypeStruct((cols, rows), array.dtype),
        (1,),
        [whole_spec((rows, cols))],
        whole_spec((cols, rows)),
    )(place, array)


def row_blocks(one_bit, two_bit, count):
    at = []
    for rest in range(count // 4):
        low, high = min(one_bit, two_bit), max(one_bit, two_bit)
        rest = ((rest >> low) << (low + 1)) | (rest & ((1 << low) - 1))
        rest = ((rest >> high) << (high + 1)) | (rest & ((1 << high) - 1))
        at.append(rest)
    return at


def grad_up(place, m, m_mate, grads, mate_grads, bits, count):
    rows, depth = m.shape
    cols = grads.shape[1]
    size = depth // count
    others = row_blocks(*bits, count)

    def kernel(place_ref, m_ref, mate_ref, own, mate, *refs):
        sent, kept, both = refs[-3:]
        total = dot(m_ref[...].T, own[...], 1, 0) + dot(mate_ref[...].T, mate[...], 1, 0)
        for w in range(count):
            both[w] = total[w * size : (w + 1) * size].astype(BF)

        def write(output, behind, one, two):
            for n, rest in enumerate(others):
                (sent, kept)[output][behind, n] = both[
                    rest + (one << bits[0]) + (two << bits[1])
                ]

        part_out(place_ref, write)

    shape = (2, count // 4, size, cols)
    return call(
        kernel,
        "grad_up",
        pair_struct(shape),
        (1,),
        [whole_spec((rows, depth))] * 2 + [whole_spec((rows, cols))] * 2,
        (whole_spec(shape),) * 2,
        scratch=[pltpu.VMEM((count, size, cols), BF)],
    )(place, m, m_mate, grads, mate_grads)


def grad_square(place, members, count, bits=None):
    arrays, specs, plan = [], [], []
    known = {}
    for member in members:
        pieces = []
        for left, block, right, lead, whole in member:
            rows, depth = right.shape[-2], left.shape[1]
            quarter = right.shape[-1] // (4 if whole else 2)
            if (id(left), block) not in known:
                known[id(left), block] = len(arrays)
                arrays.append(left)
                specs.append(
                    pl.BlockSpec((rows, depth), lambda t, place, block=block: (block, 0))
                )
            pieces.append((known[id(left), block], len(arrays)))
            arrays += [right, right]
            for k in range(2):

                def column(t, place, k=k, lead=lead, whole=whole):
                    return (*lead, 0, 2 * k + place[1] if whole else k)

                specs.append(pl.BlockSpec((None,) * len(lead) + (rows, quarter), column))
        plan.append(pieces)
    size = depth // count
    others = row_blocks(*bits, count) if bits else range(count // 2)

    def kernel(place_ref, *refs):
        sent, kept, both = refs[-3:]
        turned = {}
        for n, pieces in enumerate(plan):
            total = 0.0
            for left, right in pieces:
                if left not in turned:
                    turned[left] = refs[left][...].T
                cols = jnp.concatenate([refs[right][...], refs[right + 1][...]], 1)
                total = total + dot(turned[left], cols, 1, 0)
            for w in range(count):
                rows = total[w * size : (w + 1) * size].astype(BF)
                if bits:
                    both[w] = rows
                else:
                    for k in range(2):
                        both[w, k] = rows[:, k * quarter : (k + 1) * quarter]

            def write(output, behind, one, two):
                for n_rest, rest in enumerate(others):
                    if bits:
                        found = both[rest + (one << bits[0]) + (two << bits[1])]
                    else:
                        found = both[2 * rest + one, two]
                    (sent, kept)[output][behind, n_rest, n] = found

            part_out(place_ref, write)

    tile = (size, 2 * quarter) if bits else (2, size, quarter)
    shape = (2, len(others), len(members)) + tile[-2:]
    return call(
        kernel,
        "grad_square",
        pair_struct(shape),
        (1,),
        specs,
        (whole_spec(shape),) * 2,
        scratch=[pltpu.VMEM((count,) + tile, BF)],
    )(place, *arrays)


def first_backward(place, d, d_other, qkv, gains, x, e1, size):
    rows, width = x.shape
    quarter, steps = width // 4, rows // size

    def kernel(place_ref, d0, d1, d2, other0, other1, other2, gain_ref, x_ref, e1_ref, *refs):
        weights, (own_ref, far_ref, sum_ref) = refs[:12], refs[12:]
        grad = jnp.zeros((size, width), F32)
        for j, (d_ref, other_ref) in enumerate(((d0, other0), (d1, other1), (d2, other2))):
            for k in range(2):
                cols = slice(k * quarter, (k + 1) * quarter)
                grad = grad + dot(d_ref[:, cols], weights[4 * j + k][0], 1, 1)
                grad = grad + dot(other_ref[:, cols], weights[4 * j + 2 + k][0], 1, 1)
        grad, gain, shift = norm_back(grad, gain_ref[0:1], x_ref[...].astype(F32))
        total = e1_ref[...] + grad
        sums = jnp.concatenate([gain, shift], 0)

        @pl.when(pl.program_id(0) == 0)
        def _():
            own_ref[...] = total
            sum_ref[...] = sums

        @pl.when(pl.program_id(0) == 1)
        def _():
            far_ref[...] = total.astype(BF)
            sum_ref[...] += sums

    def weight_spec(j, flip, k):
        return pl.BlockSpec(
            (1, width, quarter), lambda i, place: (j, 0, 2 * k + (place[1] ^ flip))
        )

    return call(
        kernel,
        "first_backward",
        (out_struct(size, width, F32), out_struct(size, width), out_struct(2, width, F32)),
        (steps,),
        [row_spec(size, width // 2)] * 6
        + [whole_spec(gains.shape), row_spec(size, width), row_spec(size, width)]
        + [weight_spec(j, flip, k) for j in range(3) for flip in range(2) for k in range(2)],
        (whole_spec((size, width)), whole_spec((size, width)), whole_spec((2, width))),
    )(place, *d, *d_other, gains, x, e1, *[qkv] * 12)


def body(
    image_tokens,
    text_states,
    caption_lengths,
    text_mask,
    self_qkv,
    self_out,
    cross_query,
    cross_kv,
    cross_out,
    mlp_in,
    mlp_out,
    norm_gains,
    norm_shifts,
    out_biases,
    mlp_bias,
    cotangent,
):
    _, block, width = image_tokens.shape
    blocks = lax.axis_size("narrow")
    wide_size = lax.axis_size("wide")
    here = lax.axis_index("narrow")
    line = lax.axis_index("wide")
    chip, core = here // 2, here % 2
    wide_bits = wide_size.bit_length() - 1
    mates = [(i, i ^ 1) for i in range(blocks)]
    across = [(i, i ^ 2) for i in range(blocks)]

    def to_mate(value):
        return lax.ppermute(value, "narrow", mates)

    def to_chip(value):
        return lax.ppermute(value, "narrow", across)

    def item(array, index):
        return lax.dynamic_index_in_dim(array, index, 0, keepdims=False)

    def columns(array, side):
        quarter = array.shape[-1] // 4
        return jnp.concatenate(
            [
                lax.dynamic_slice_in_dim(array, (2 * k + side) * quarter, quarter, array.ndim - 1)
                for k in range(2)
            ],
            -1,
        )

    def chosen(first, second):
        return jnp.where(core == 0, first, second), jnp.where(core == 0, second, first)

    near = list(range(wide_bits))

    def partner(index, axis):
        line_at, here_at = divmod(index, blocks)
        if axis == "x":
            return line_at * blocks + (here_at ^ 2)
        return (line_at ^ (1 << axis)) * blocks + here_at

    def exchange(value, first, second=None):
        axes = (first, first if second is None else second)
        pairs = [(i, partner(i, axes[i % 2])) for i in range(wide_size * blocks)]
        return lax.ppermute(value, ("wide", "narrow"), pairs)

    def bit_of(axis):
        return chip if axis == "x" else (line >> axis) & 1

    class Scatter:
        def __init__(self, shape, one, two, dims):
            self.shape, self.axes, self.dims = shape, (one, two), dims
            self.kept, self.come = [], []

        def add(self, halves, *others):
            self.sent, kept = (half.reshape(self.shape) for half in halves)
            self.kept.append(kept)
            self.come.append(exchange(after(self.sent, *others), *self.axes))
            self.terms = [(tuple(self.kept), {}), (tuple(self.come), {})]
            self.count = len(self.kept)

        def values(self, extra):
            found = []
            for parts, taken in self.terms:
                taken = {**taken, **extra}
                split = len(parts) > 1
                which = taken.pop(1, None) if split else None
                pieces = []
                for array in parts:
                    at = [taken.get(d, 0) * (n // 2) for d, n in enumerate(array.shape)]
                    size = [n // 2 if d in taken else n for d, n in enumerate(array.shape)]
                    pieces.append(lax.dynamic_slice(array, at, size) if taken else array)
                if which is not None:
                    pieces = [jnp.where(which == 0, *pieces)]
                elif self.count > 1 and not split:
                    pieces = jnp.split(pieces[0], self.count, 1)
                found.append([piece.astype(F32) for piece in pieces])
            return [sum(pieces) for pieces in zip(*found)]

        def advance(self, bit, dim, *axes):
            if dim == 1:
                self.count = 1
            sums = [value.astype(BF) for value in self.values({dim: 1 - bit})]
            self.sent = sums[0] if len(sums) == 1 else jnp.concatenate(sums, 1)
            self.terms = [(parts, {**taken, dim: bit}) for parts, taken in self.terms]
            self.terms.append(((exchange(self.sent, *axes),), {}))

        def turn(self):
            one, two = self.axes
            self.advance(jnp.where(core == 0, bit_of(two), bit_of(one)), 0, two, one)

        def step(self, axis):
            self.advance(bit_of(axis), self.dims[axis], axis)

        def wait(self, *others):
            arrays = tuple(parts for parts, _ in self.terms)
            arrays = lax.optimization_barrier((arrays,) + others)[0]
            self.terms = [(a, taken) for a, (_, taken) in zip(arrays, self.terms)]

        def total(self, *shape):
            return self.values({})[0].reshape(shape)

    def bit_dims(first, *left_out):
        bits = [b for b in reversed(near) if b not in left_out]
        return (2,) * len(bits), {b: first + n for n, b in enumerate(bits)}

    def places(one, two):
        return jnp.stack([here, core, bit_of(one), bit_of(two)]).astype(jnp.int32)

    def both(own_part, mate_part):
        return jnp.concatenate([own_part, mate_part], 0)

    def after(value, *others):
        return lax.optimization_barrier((value,) + others)[0]

    rows_wide = width // wide_size
    quarter = width // 4

    def home(own, far):
        far = far.astype(F32)
        return jnp.where((jnp.arange(2) == chip)[:, None, None], own[None], far[None])

    own = jnp.concatenate([item(image_tokens, chip), item(text_states, chip)], 0)
    far = to_chip(
        jnp.concatenate([item(image_tokens, 1 - chip), item(text_states, 1 - chip)], 0)
    )
    own_mate = to_mate(own)
    place = jnp.stack([here, core]).astype(jnp.int32)
    first = project(place, own, own_mate, self_qkv, norm_gains, norm_shifts, 0, block, None)
    far = after(far, first[0])
    far_mate = to_mate(far)
    a, q, k, v = project(
        place, far, far_mate, self_qkv, norm_gains, norm_shifts, 1, block, first
    )
    x = both(own[:block], far[:block])
    text_all = jnp.concatenate(
        chosen(both(own[block:], far[block:]), both(own_mate[block:], far_mate[block:])), 0
    )
    slot_block = text_states.shape[1]
    slots = slot_block * blocks
    slot_order = jnp.stack([(2 * chip) ^ k for k in (0, 2, 1, 3)])
    slot = (slot_order[:, None] * slot_block + jnp.arange(slot_block)[None, :]).reshape(slots)
    kept = item(text_mask, chip).reshape(blocks, slot_block)
    kept = jnp.concatenate([item(kept, (2 * chip) ^ k) for k in (0, 2, 1, 3)], 0)
    length = item(caption_lengths, chip)
    live = ((slot < length) & ((kept == 1) | (slot == 0))).astype(F32).reshape(slots, 1)

    tk = dot(text_all, cross_kv[0], 1, 0).astype(BF)
    tv = dot(text_all, cross_kv[1], 1, 0).astype(BF)

    rows = 2 * block
    cot_far = to_chip(after(item(cotangent, 1 - chip), q))
    q = after(q, tk, tv)
    o, o_mate, log_self = self_forward(place, q, k, v, blocks)
    o_other = to_mate(after(o_mate, cot_far))
    e3 = both(item(cotangent, chip), cot_far)
    os_rows, h1, c, qc, oc, log_cross, h2, m = middle_forward(
        place,
        live,
        x,
        o,
        o_other,
        self_out,
        norm_gains,
        norm_shifts,
        out_biases,
        cross_query,
        tk,
        tv,
        cross_out,
        block,
    )
    e3_mate, m_mate = to_mate(e3), to_mate(m)
    c_mate, oc_mate, os_mate = to_mate(c), to_mate(oc), to_mate(os_rows)
    bias_row = mlp_bias.reshape(1, -1)
    sums = (h2, out_biases)
    g, g_mate, kept, kept_mate, hidden_sums = [], [], [], [], []
    for part in range(2):
        units, sent, stay, hidden_sum, dm, *outs = mlp_part(
            place, m, e3, mlp_in, mlp_out, bias_row, *sums, part, TILE
        )
        g.append(units)
        g_mate.append(to_mate(units))
        kept.append(stay)
        kept_mate.append(to_mate(sent))
        hidden_sums.append(hidden_sum)
        if part == 0:
            sums = (outs[0], after(dm, e3_mate, m_mate, c_mate, oc_mate, os_mate))
    layer_out, out_far = outs
    out_far = to_chip(out_far)
    up_bits = (near[1], near[0])
    shape, dims = bit_dims(2, near[0], near[-1])
    dims[near[-1]] = 1
    down = Scatter(
        (2, 1) + shape + (quarter, mlp_out.shape[0] // wide_size), near[0], "x", dims
    )
    shape, dims = bit_dims(2, *up_bits)
    dims["x"] = 1
    up = Scatter((2, 1) + shape + (rows_wide, mlp_in.shape[1] // 4), *up_bits, dims)
    for part in range(2):
        down.add(
            grad_down(
                places(near[0], "x"), g[part], g_mate[part], e3, e3_mate, wide_size // 4
            )
        )
        kept[part] = after(kept[part], down.sent)
        up.add(
            grad_up(
                places(*up_bits), m, m_mate, kept[part], kept_mate[part], up_bits, wide_size
            )
        )
        if part == 0:
            g[1] = after(g[1], up.sent, out_far)
    dm = after(dm, up.sent)

    f2, dqc, f1, e1, do_own, do_other, *cols, dt, row_sums = middle_backward(
        place,
        live,
        dm,
        e3,
        h1,
        h2,
        qc,
        oc,
        log_cross,
        self_out,
        norm_gains,
        cross_query,
        tk,
        tv,
        cross_out,
        block,
    )
    dt_mate, do_mate = to_mate(dt), to_mate(do_other)
    cols_mate = [to_mate(part) for part in cols]
    down.wait(row_sums)
    down.turn()
    up.wait(row_sums, down.sent)
    up.turn()
    dt_mate = after(dt_mate, up.sent, down.sent)
    dt = (dt.astype(F32) + dt_mate.astype(F32)).astype(BF)
    shape, dims = bit_dims(1, near[0])
    outer = Scatter((2,) + shape + (5, rows_wide, quarter), near[0], "x", dims)
    outer_halves = (
        grad_square(
            places(near[0], "x"),
            [
                [(oc, 0, f2, (), True), (oc_mate, 0, cols_mate[0], (), False)],
                [(text_all, 0, dt, (0,), True)],
                [(text_all, 0, dt, (1,), True)],
                [(c, 0, dqc, (), True), (c_mate, 0, cols_mate[1], (), False)],
                [(os_rows, 0, f1, (), True), (os_mate, 0, cols_mate[2], (), False)],
            ],
            wide_size,
        )
    )
    down.wait(outer_halves)
    down.step(near[1])
    up.wait(outer_halves, down.sent)
    for axis in near[2:]:
        up.step(axis)
    outer.add(outer_halves, down.sent, up.sent)
    do_mate = after(do_mate, down.sent, up.sent)
    d = self_backward(place, q, k, v, o, o_mate, do_own, do_mate, log_self, blocks)
    d, d_mate = d[:3], d[3:]
    d_other = [to_mate(part) for part in d_mate]
    for axis in near[2:]:
        down.wait(d)
        down.step(axis)
    d = after(d, down.sent)
    shape, dims = bit_dims(1, near[0])
    inner = Scatter((2,) + shape + (3, rows_wide, quarter), near[0], "x", dims)
    inner.add(
        grad_square(
            places(near[0], "x"),
            [[(a, 0, d[j], (), False), (a, 1, d_mate[j], (), False)] for j in range(3)],
            wide_size,
        )
    )
    up.wait(inner.sent)
    up.step("x")
    d_other = after(d_other, inner.sent, up.sent)
    grad_own, grad_far, late = first_backward(
        place, d, d_other, self_qkv, norm_gains, x, e1, block
    )
    image_far = to_chip(grad_far)
    late = jnp.concatenate(
        [late, row_sums[:7], jnp.concatenate(hidden_sums, 1).reshape(-1, width)]
    )
    late = late + to_mate(late)
    outer.wait(grad_far)
    outer.turn()
    inner.wait(outer.sent)
    inner.turn()
    late = after(late, inner.sent)
    for axis in near[1:]:
        late = late + exchange(late, axis)
    late_far = exchange(after(late, inner.sent), near[0])
    outer.wait(inner.sent)
    outer.step(near[1])
    late = late + after(late_far, outer.sent)
    late_far = to_chip(late)
    inner.wait(outer.sent)
    inner.step(near[1])
    dt_own = lax.dynamic_slice_in_dim(dt, core * 2 * slot_block, 2 * slot_block, 1)
    dt_own = after(dt_own, inner.sent)
    grad_text = dot(dt_own[0], cross_kv[0], 1, 1) + dot(dt_own[1], cross_kv[1], 1, 1)
    text_far = to_chip(grad_text[slot_block:])
    for axis in near[2:]:
        outer.wait(inner.sent)
        outer.step(axis)
        inner.wait(outer.sent)
        inner.step(axis)
    down.wait(inner.sent)
    up.wait(inner.sent)
    outer.wait(inner.sent)
    inner.wait(inner.sent)
    late = late + after(late_far, inner.sent)
    image_far, out_far, text_far = after((image_far, out_far, text_far), inner.sent)

    outer_part = outer.total(5, rows_wide, quarter)
    inner_part = inner.total(3, rows_wide, quarter)
    down_part = transposed(place, down.total(quarter, mlp_out.shape[0] // wide_size))

    gains = jnp.stack([late[0], late[2], late[3]])
    shifts = jnp.stack([late[1], late[4], late[5]])
    return (
        home(layer_out, out_far),
        home(grad_own, image_far),
        home(grad_text[:slot_block], text_far),
        inner_part,
        outer_part[4],
        outer_part[3],
        outer_part[1:3],
        outer_part[0],
        up.total(rows_wide, mlp_in.shape[1] // 4),
        down_part,
        gains,
        shifts,
        late[6:9],
        late[9:].reshape(-1),
    )


def solution(mesh):
    rows = P("wide", "narrow", None)
    whole = P()
    return jax.shard_map(
        body,
        mesh=mesh,
        in_specs=(rows, rows, P("wide"), P("wide", None)) + (whole,) * 11 + (rows,),
        out_specs=(rows,) * 3
        + (
            P(None, "wide", "narrow"),
            P("wide", "narrow"),
            P("wide", "narrow"),
            P(None, "wide", "narrow"),
        )
        + (P("wide", "narrow"),) * 3
        + (whole,) * 4,
        check_vma=False,
    )
```

```python
import jax
import jax.numpy as jnp
from jax import lax
from jax.experimental import pallas as pl
from jax.experimental.pallas import tpu as pltpu
from jax.sharding import PartitionSpec as P

HEAD_DIM = 64
PAIR = 2 * HEAD_DIM
SCALE = HEAD_DIM**-0.5
NEG = -1e30
BF = jnp.bfloat16
F32 = jnp.float32
VMEM = 56 * 1024 * 1024
TILE = 1024


def dot(left, right, left_axis, right_axis):
    return lax.dot_general(
        left, right, (((left_axis,), (right_axis,)), ((), ())), preferred_element_type=F32
    )


def two_heads(rows):
    lane = lax.broadcasted_iota(jnp.int32, rows.shape, 1)
    zero = jnp.zeros_like(rows)
    return jnp.concatenate(
        [jnp.where(lane < HEAD_DIM, rows, zero), jnp.where(lane < HEAD_DIM, zero, rows)], 0
    )


def block_rows(here, block, size):
    slot = here ^ block
    return pl.ds(pl.multiple_of(((slot & 1) * 2 + slot // 2) * size, size), size)


def slot_place(here, block, size):
    slot = here ^ block
    return slot & 1, pl.ds(pl.multiple_of((slot // 2) * size, size), size)


def store_sides(here, block, size, even, odd, own_ref, mate_ref):
    _, half = slot_place(here, block, size)
    own_first = (here & 1) == 0
    own_ref[half, :] = jnp.where(own_first, even, odd)
    mate_ref[half, :] = jnp.where(own_first, odd, even)


def causal_mask(scores, size):
    key = lax.broadcasted_iota(jnp.int32, scores.shape, 0)
    query = lax.broadcasted_iota(jnp.int32, scores.shape, 1)
    return jnp.where(key <= lax.rem(query, size), scores, NEG)


def self_forward_kernel(here_ref, q_ref, k_ref, v_ref, own_ref, mate_ref, log_ref, *, blocks):
    here = here_ref[0]
    size = q_ref.shape[0] // blocks
    for p in range(blocks):
        rows = block_rows(here, p, size)
        queries = two_heads(q_ref[rows, :] * BF(SCALE))
        scores = []
        for j in range(p + 1):
            s = dot(k_ref[block_rows(here, j, size), :], queries, 1, 1)
            scores.append(causal_mask(s, size) if j == p else s)
        top = scores[0].max(0, keepdims=True)
        for s in scores[1:]:
            top = jnp.maximum(top, s.max(0, keepdims=True))
        total = jnp.zeros_like(top)
        mixed = [jnp.zeros((HEAD_DIM, size), F32)] * 2
        for j in range(p + 1):
            e = jnp.exp(scores[j] - top)
            total = total + e.sum(0, keepdims=True)
            low = e.astype(BF)
            values = v_ref[block_rows(here, j, size), :].T
            for h in range(2):
                mixed[h] = mixed[h] + dot(
                    values[h * HEAD_DIM : (h + 1) * HEAD_DIM],
                    low[:, h * size : (h + 1) * size],
                    1,
                    0,
                )
        inverse = 1.0 / total
        both = jnp.concatenate(
            [mixed[h] * inverse[:, h * size : (h + 1) * size] for h in range(2)], 0
        )
        low = both.T.astype(BF)
        if p % 2:
            store_sides(here, p - 1, size, before, low, own_ref, mate_ref)
        before = low
        log_ref[0, :, 2 * size * p : 2 * size * (p + 1)] = top + jnp.log(total)


def row_dots(left, right):
    product = left.astype(F32).T * right.astype(F32).T
    return jnp.concatenate(
        [product[:HEAD_DIM].sum(0, keepdims=True), product[HEAD_DIM:].sum(0, keepdims=True)], 1
    )


def self_backward_kernel(
    here_ref,
    q_ref,
    k_ref,
    v_ref,
    o_ref,
    o_mate_ref,
    do_ref,
    do_mate_ref,
    log_ref,
    *sides,
    blocks,
):
    here = here_ref[0]
    size = q_ref.shape[0] // blocks
    queries, grads, inner, dq = [], [], [], []
    for p in range(blocks):
        rows = block_rows(here, p, size)
        queries.append(two_heads(q_ref[rows, :] * BF(SCALE)))
        side, half = slot_place(here, p, size)
        do = jnp.where(side == 0, do_ref[half, :], do_mate_ref[half, :])
        grads.append(two_heads(do))
        o = jnp.where(side == 0, o_ref[half, :], o_mate_ref[half, :])
        inner.append(row_dots(do, o))
        dq.append([jnp.zeros((HEAD_DIM, size), F32)] * 2)
    for j in range(blocks):
        rows = block_rows(here, j, size)
        keys, values = k_ref[rows, :], v_ref[rows, :]
        turned = keys.T
        dk = jnp.zeros(keys.shape, F32)
        dv = jnp.zeros(keys.shape, F32)
        for p in range(j, blocks):
            s = dot(keys, queries[p], 1, 1)
            if j == p:
                s = causal_mask(s, size)
            probs = jnp.exp(s - log_ref[0, :, 2 * size * p : 2 * size * (p + 1)])
            dprobs = dot(values, grads[p], 1, 1)
            ds = (probs * (dprobs - inner[p])).astype(BF)
            dv = dv + dot(probs.astype(BF), grads[p], 1, 0)
            dk = dk + dot(ds, queries[p], 1, 0)
            for h in range(2):
                dq[p][h] = dq[p][h] + dot(
                    turned[h * HEAD_DIM : (h + 1) * HEAD_DIM],
                    ds[:, h * size : (h + 1) * size],
                    1,
                    0,
                )
        low = dk.astype(BF), dv.astype(BF)
        if j % 2:
            for n in range(2):
                store_sides(here, j - 1, size, before[n], low[n], sides[1 + n], sides[4 + n])
        before = low
    for p in range(blocks):
        both = jnp.concatenate(dq[p], 0) * SCALE
        low = both.T.astype(BF)
        if p % 2:
            store_sides(here, p - 1, size, before, low, sides[0], sides[3])
        before = low


def pair_spec(rows):
    return pl.BlockSpec((rows, PAIR), lambda i, *_: (0, i))


def log_spec(width):
    return pl.BlockSpec((1, 1, width), lambda i, *_: (i, 0, 0))


def self_forward(here, q, k, v, blocks):
    rows, width = q.shape
    pairs = width // PAIR
    spec = pair_spec(rows)
    return pl.pallas_call(
        lambda *refs: self_forward_kernel(*refs, blocks=blocks),
        name="self_forward",
        out_shape=(
            jax.ShapeDtypeStruct((rows // 2, width), BF),
            jax.ShapeDtypeStruct((rows // 2, width), BF),
            jax.ShapeDtypeStruct((pairs, 1, 2 * rows), F32),
        ),
        grid_spec=pltpu.PrefetchScalarGridSpec(
            num_scalar_prefetch=1,
            grid=(pairs,),
            in_specs=[spec] * 3,
            out_specs=(pair_spec(rows // 2), pair_spec(rows // 2), log_spec(2 * rows)),
        ),
        compiler_params=pltpu.CompilerParams(vmem_limit_bytes=VMEM),
        cost_estimate=pl.CostEstimate(flops=10**6, bytes_accessed=10**5, transcendentals=0),
    )(here, q, k, v)


def self_backward(here, q, k, v, o, o_mate, do, do_mate, log_total, blocks):
    rows, width = q.shape
    pairs = width // PAIR
    spec = pair_spec(rows)
    return pl.pallas_call(
        lambda *refs: self_backward_kernel(*refs, blocks=blocks),
        name="self_backward",
        out_shape=(jax.ShapeDtypeStruct((rows // 2, width), BF),) * 6,
        grid_spec=pltpu.PrefetchScalarGridSpec(
            num_scalar_prefetch=1,
            grid=(pairs,),
            in_specs=[spec] * 3 + [pair_spec(rows // 2)] * 4 + [log_spec(2 * rows)],
            out_specs=(pair_spec(rows // 2),) * 6,
        ),
        compiler_params=pltpu.CompilerParams(vmem_limit_bytes=VMEM),
        cost_estimate=pl.CostEstimate(flops=10**6, bytes_accessed=10**5, transcendentals=0),
    )(here, q, k, v, o, o_mate, do, do_mate, log_total)


def standardize(rows):
    centered = rows - jnp.mean(rows, -1, keepdims=True)
    inverse = lax.rsqrt(jnp.mean(centered * centered, -1, keepdims=True) + 1e-05)
    return centered * inverse, inverse


def normed(rows, gain, shift):
    return (standardize(rows)[0] * gain + shift).astype(BF)


def norm_back(grad_out, gain, rows):
    unit, inverse = standardize(rows)
    grad_unit = grad_out * gain
    grad_in = inverse * (
        grad_unit
        - jnp.mean(grad_unit, -1, keepdims=True)
        - unit * jnp.mean(grad_unit * unit, -1, keepdims=True)
    )
    return grad_in, column_sum(grad_out * unit), column_sum(grad_out)


def column_sum(rows):
    return jnp.sum(rows.astype(F32), 0, keepdims=True)


def gelu_and_slope(pre):
    square = pre * pre
    bend = jnp.tanh(pre * (0.7978845608028654 + (0.7978845608028654 * 0.044715) * square))
    half = 0.5 + 0.5 * bend
    value = pre * half
    steep = 0.7978845608028654 + (3.0 * 0.7978845608028654 * 0.044715) * square
    return value, half + value * (1.0 - bend) * steep


def whole_spec(shape):
    return pl.BlockSpec(shape, lambda *_: (0,) * len(shape))


def row_spec(rows, cols, start=0):
    return pl.BlockSpec((rows, cols), lambda i, *_: (start + i, 0))


def call(kernel, name, out_shape, grid, in_specs, out_specs, scratch=(), aliases=None):
    return pl.pallas_call(
        kernel,
        name=name,
        out_shape=out_shape,
        grid_spec=pltpu.PrefetchScalarGridSpec(
            num_scalar_prefetch=1,
            grid=grid,
            in_specs=in_specs,
            out_specs=out_specs,
            scratch_shapes=scratch,
        ),
        input_output_aliases=aliases or {},
        compiler_params=pltpu.CompilerParams(vmem_limit_bytes=VMEM),
        cost_estimate=pl.CostEstimate(flops=10**6, bytes_accessed=10**5, transcendentals=0),
    )


def out_struct(rows, cols, kind=BF):
    return jax.ShapeDtypeStruct((rows, cols), kind)


def project(place, own, mate, qkv, gains, shifts, half, size, into):
    width = qkv.shape[1]
    quarter = width // 4

    def kernel(place_ref, own_ref, mate_ref, gain_ref, shift_ref, *refs):
        weights, outs = refs[:6], refs[-4:]
        rows = jnp.where(pl.program_id(0) == 0, own_ref[...], mate_ref[...]).astype(F32)
        a = normed(rows, gain_ref[0:1], shift_ref[0:1])
        outs[0][...] = a
        for j in range(3):
            pair = jnp.concatenate([weights[2 * j][0], weights[2 * j + 1][0]], 1)
            outs[1 + j][...] = dot(a, pair, 1, 0).astype(BF)

    def weight_spec(j, k):
        return pl.BlockSpec((1, width, quarter), lambda i, place: (j, 0, 2 * k + place[1]))

    def out_spec(cols):
        return pl.BlockSpec((size, cols), lambda i, place: (2 * i + half, 0))

    specs = [whole_spec((size, width))] * 2 + [whole_spec(gains.shape)] * 2
    specs += [weight_spec(j, k) for j in range(3) for k in range(2)]
    arrays = [own, mate, gains, shifts] + [qkv] * 6
    aliases = None
    if into is not None:
        aliases = {1 + len(arrays) + n: n for n in range(4)}
        arrays += list(into)
        specs += [pl.BlockSpec(memory_space=pl.ANY)] * 4
    rows = 4 * size
    return call(
        kernel,
        "project",
        (out_struct(rows, width),) + (out_struct(rows, width // 2),) * 3,
        (2,),
        specs,
        (out_spec(width),) + (out_spec(width // 2),) * 3,
        aliases=aliases,
    )(place, *arrays)


def head_row_specs(width):
    quarter = width // 4
    return [
        pl.BlockSpec((quarter, width), lambda i, place, k=k, flip=flip: (2 * k + (place[1] ^ flip), 0))
        for flip in range(2)
        for k in range(2)
    ]


def middle_forward(place, live, own, far, o, o_other, self_out, gains, shifts, biases, wq, tk, tv, wo, size):
    rows, width = 2 * size, own.shape[1]
    quarter, slots, steps = width // 4, tk.shape[0], rows // size

    def kernel(
        place_ref,
        live_ref,
        own_ref,
        far_ref,
        o_ref,
        other_ref,
        w0,
        w1,
        w2,
        w3,
        gain_ref,
        shift_ref,
        bias_ref,
        wq_ref,
        tk_ref,
        tv_ref,
        wo_ref,
        os_ref,
        h1_ref,
        c_ref,
        qc_ref,
        oc_ref,
        log_ref,
        h2_ref,
        m_ref,
    ):
        core = place_ref[1]
        x = jnp.where(pl.program_id(0) == 0, own_ref[...], far_ref[...])
        h1 = x.astype(F32) + bias_ref[0:1]
        for n, (ref, weight) in enumerate(
            ((o_ref, w0), (o_ref, w1), (other_ref, w2), (other_ref, w3))
        ):
            k, side = n % 2, core ^ (n // 2)
            part = ref[:, k * quarter : (k + 1) * quarter]
            at = pl.multiple_of((2 * k + side) * quarter, quarter)
            os_ref[:, pl.ds(at, quarter)] = part
            h1 = h1 + dot(part, weight[...], 1, 0)
        h1_ref[...] = h1
        c = normed(h1, gain_ref[1:2], shift_ref[1:2])
        c_ref[...] = c
        qc_ref[...] = dot(c, wq_ref[...], 1, 0).astype(BF)
        for pair in range(width // PAIR):
            lanes = slice(pair * PAIR, (pair + 1) * PAIR)
            queries = two_heads(qc_ref[:, lanes] * BF(SCALE))
            s = dot(tk_ref[:, lanes], queries, 1, 1)
            s = jnp.where(live_ref[...] > 0, s, NEG)
            top = s.max(0, keepdims=True)
            e = jnp.exp(s - top)
            total = e.sum(0, keepdims=True)
            low = e.astype(BF)
            values = tv_ref[:, lanes].T
            inverse = 1.0 / total
            both = jnp.concatenate(
                [
                    dot(
                        values[h * HEAD_DIM : (h + 1) * HEAD_DIM],
                        low[:, h * size : (h + 1) * size],
                        1,
                        0,
                    )
                    * inverse[:, h * size : (h + 1) * size]
                    for h in range(2)
                ],
                0,
            )
            oc_ref[:, lanes] = both.T.astype(BF)
            log_ref[0, pair : pair + 1] = top + jnp.log(total)
        h2 = h1 + dot(oc_ref[...], wo_ref[...], 1, 0) + bias_ref[1:2]
        h2_ref[...] = h2
        m_ref[...] = normed(h2, gain_ref[2:3], shift_ref[2:3])

    row = row_spec(size, width)
    square = whole_spec((width, width))
    low, high = out_struct(rows, width), out_struct(rows, width, F32)
    pairs = width // PAIR
    return call(
        kernel,
        "middle_forward",
        (low, high, low, low, low, jax.ShapeDtypeStruct((steps, pairs, 2 * size), F32), high, low),
        (steps,),
        [
            whole_spec((slots, 1)),
            whole_spec((size, width)),
            whole_spec((size, width)),
            row_spec(size, width // 2),
            row_spec(size, width // 2),
        ]
        + head_row_specs(width)
        + [whole_spec(gains.shape)] * 3
        + [square, whole_spec((slots, width)), whole_spec((slots, width)), square],
        (row,) * 5 + (pl.BlockSpec((1, pairs, 2 * size), lambda i, *_: (i, 0, 0)), row, row),
    )(place, live, own, far, o, o_other, *[self_out] * 4, gains, shifts, biases, wq, tk, tv, wo)


def middle_backward(
    place, live, dm, e3, h1, h2, qc, oc, logs, self_out, gains, wq, tk, tv, wo, size
):
    rows, width = h1.shape
    quarter, slots, steps = width // 4, tk.shape[0], rows // size

    def kernel(
        place_ref,
        live_ref,
        dm_ref,
        e3_ref,
        h1_ref,
        h2_ref,
        qc_ref,
        oc_ref,
        log_ref,
        w0,
        w1,
        w2,
        w3,
        gain_ref,
        wq_ref,
        tk_ref,
        tv_ref,
        wo_ref,
        f2_ref,
        dqc_ref,
        f1_ref,
        e1_ref,
        do_ref,
        other_ref,
        cols_f2,
        cols_dqc,
        cols_f1,
        dt_ref,
        sum_ref,
        doc_ref,
        dtk_sum,
        dtv_sum,
    ):
        first = pl.program_id(0) == 0

        @pl.when(first)
        def _():
            dtk_sum[...] = jnp.zeros_like(dtk_sum)
            dtv_sum[...] = jnp.zeros_like(dtv_sum)

        e3 = e3_ref[...].astype(F32)
        grad, gain_three, shift_three = norm_back(dm_ref[...], gain_ref[2:3], h2_ref[...])
        e2 = e3 + grad
        f2 = e2.astype(BF)
        f2_ref[...] = f2
        doc_ref[...] = dot(f2, wo_ref[...], 1, 1).astype(BF)
        for pair in range(width // PAIR):
            lanes = slice(pair * PAIR, (pair + 1) * PAIR)
            queries = two_heads(qc_ref[:, lanes] * BF(SCALE))
            doc = doc_ref[:, lanes]
            grads = two_heads(doc)
            inner = row_dots(doc, oc_ref[:, lanes])
            keys = tk_ref[:, lanes]
            s = dot(keys, queries, 1, 1)
            s = jnp.where(live_ref[...] > 0, s, NEG)
            probs = jnp.exp(s - log_ref[0, pair : pair + 1])
            dprobs = dot(tv_ref[:, lanes], grads, 1, 1)
            ds = (probs * (dprobs - inner)).astype(BF)
            dtv_sum[:, lanes] += dot(probs.astype(BF), grads, 1, 0)
            dtk_sum[:, lanes] += dot(ds, queries, 1, 0)
            turned = keys.T
            both = jnp.concatenate(
                [
                    dot(
                        turned[h * HEAD_DIM : (h + 1) * HEAD_DIM],
                        ds[:, h * size : (h + 1) * size],
                        1,
                        0,
                    )
                    for h in range(2)
                ],
                0,
            )
            dqc_ref[:, lanes] = (both * SCALE).T.astype(BF)
        dc = dot(dqc_ref[...], wq_ref[...], 1, 1)
        grad, gain_two, shift_two = norm_back(dc, gain_ref[1:2], h1_ref[...])
        e1 = e2 + grad
        e1_ref[...] = e1
        f1 = e1.astype(BF)
        f1_ref[...] = f1
        for n, (ref, weight) in enumerate(
            ((do_ref, w0), (do_ref, w1), (other_ref, w2), (other_ref, w3))
        ):
            k = n % 2
            ref[:, k * quarter : (k + 1) * quarter] = dot(f1, weight[...], 1, 1).astype(BF)
        for ref, cols_ref in ((f2_ref, cols_f2), (dqc_ref, cols_dqc), (f1_ref, cols_f1)):
            for k in range(2):
                at = pl.multiple_of((2 * k + 1 - place_ref[1]) * quarter, quarter)
                cols_ref[:, k * quarter : (k + 1) * quarter] = ref[:, pl.ds(at, quarter)]
        sums = jnp.concatenate(
            [gain_two, gain_three, shift_two, shift_three]
            + [column_sum(v) for v in (f1, f2, e3)]
            + [jnp.zeros_like(gain_two)],
            0,
        )

        @pl.when(first)
        def _():
            sum_ref[...] = sums

        @pl.when(jnp.logical_not(first))
        def _():
            sum_ref[...] += sums

        @pl.when(pl.program_id(0) == steps - 1)
        def _():
            dt_ref[0] = dtk_sum[...].astype(BF)
            dt_ref[1] = dtv_sum[...].astype(BF)

    row, half = row_spec(size, width), row_spec(size, width // 2)
    square, text = whole_spec((width, width)), whole_spec((slots, width))
    low, narrow = out_struct(rows, width), out_struct(rows, width // 2)
    pairs = width // PAIR
    return call(
        kernel,
        "middle_backward",
        (low, low, low, out_struct(rows, width, F32), narrow, narrow)
        + (narrow,) * 3
        + (jax.ShapeDtypeStruct((2, slots, width), BF),)
        + (out_struct(8, width, F32),),
        (steps,),
        [whole_spec((slots, 1))]
        + [row] * 6
        + [pl.BlockSpec((1, pairs, 2 * size), lambda i, *_: (i, 0, 0))]
        + head_row_specs(width)
        + [whole_spec(gains.shape), square, text, text, square],
        (row,) * 4
        + (half,) * 5
        + (whole_spec((2, slots, width)),)
        + (whole_spec((8, width)),),
        scratch=[
            pltpu.VMEM((size, width), BF),
            pltpu.VMEM((slots, width), F32),
            pltpu.VMEM((slots, width), F32),
        ],
    )(place, live, dm, e3, h1, h2, qc, oc, logs, *[self_out] * 4, gains, wq, tk, tv, wo)


def mlp_part(place, m, e3, w_in, w_out, bias, start, dm_sum, part, tile):
    rows, width = m.shape
    hidden = w_in.shape[1] // 2
    steps = hidden // tile
    turn = steps // 2

    def column(t, place):
        ahead = t < turn
        side = jnp.where(ahead, 1 - place[1], place[1])
        return side * turn + jnp.where(ahead, t, t - turn)

    def kernel(place_ref, m_ref, e3_ref, in_ref, out_ref, bias_ref, *refs):
        starts, (g_ref, far_ref, near_ref, sum_ref, dm_ref, *outs, o_ref) = refs[:2], refs[2:]
        t = pl.program_id(0)

        @pl.when(t == 0)
        def _():
            o_ref[...] = starts[0][...] + starts[1][2:3] if part == 0 else starts[0][...]
            dm_ref[...] = jnp.zeros_like(dm_ref) if part == 0 else starts[1][...]

        g, slope = gelu_and_slope(dot(m_ref[...], in_ref[...], 1, 0) + bias_ref[...])
        g = g.astype(BF)
        g_ref[...] = g
        dg = dot(e3_ref[...], out_ref[...], 1, 1).astype(BF).astype(F32)
        d = (dg * slope).astype(BF)

        @pl.when(t < turn)
        def _():
            far_ref[...] = d

        @pl.when(t >= turn)
        def _():
            near_ref[...] = d

        sum_ref[...] = column_sum(d)
        o_ref[...] += dot(g, out_ref[...], 1, 0)
        dm_ref[...] += dot(d, in_ref[...], 1, 1)

        if part:

            @pl.when(t == steps - 1)
            def _():
                outs[0][...] = o_ref[: rows // 2]
                outs[1][...] = o_ref[rows // 2 :].astype(BF)

    full = whole_spec((rows, width))
    wide = pl.BlockSpec((rows, tile), lambda t, place: (0, column(t, place)))
    second = whole_spec(dm_sum.shape)
    return call(
        kernel,
        "mlp",
        (out_struct(rows, hidden), out_struct(rows, hidden // 2), out_struct(rows, hidden // 2))
        + (out_struct(1, hidden, F32), out_struct(rows, width, F32))
        + (
            (out_struct(rows // 2, width, F32), out_struct(rows // 2, width))
            if part
            else (out_struct(rows, width, F32),)
        ),
        (steps,),
        [
            full,
            full,
            pl.BlockSpec((width, tile), lambda t, place: (0, part * steps + column(t, place))),
            pl.BlockSpec((tile, width), lambda t, place: (part * steps + column(t, place), 0)),
            pl.BlockSpec((1, tile), lambda t, place: (0, part * steps + column(t, place))),
            full,
            second,
        ],
        (
            wide,
            pl.BlockSpec((rows, tile), lambda t, place: (0, jnp.minimum(t, turn - 1))),
            pl.BlockSpec((rows, tile), lambda t, place: (0, jnp.maximum(t - turn, 0))),
            pl.BlockSpec((1, tile), lambda t, place: (0, column(t, place))),
            full,
        )
        + ((whole_spec((rows // 2, width)),) * 2 if part else (full,)),
        scratch=[pltpu.VMEM((rows, width), F32)] if part else [],
    )(place, m, e3, w_in, w_out, bias, start, dm_sum)


def part_out(place_ref, axes, write):
    core = place_ref[1]
    mine = jnp.where(core == 0, place_ref[axes[0]], place_ref[axes[1]])
    for ahead, output in ((1 - mine, 0), (mine, 1)):
        for behind in range(2):
            write(
                output,
                behind,
                jnp.where(core == 0, ahead, behind),
                jnp.where(core == 0, behind, ahead),
            )


def core_columns(rows, quarter):
    return [
        pl.BlockSpec((rows, quarter), lambda t, place, k=k: (0, 2 * k + place[1]))
        for k in range(2)
    ]


def pair_struct(shape):
    return (jax.ShapeDtypeStruct(shape, BF),) * 2


def grad_down(place, axes, units, mate_units, e3, e3_mate, steps):
    rows, half = units.shape
    quarter = e3.shape[1] // 4
    tile = half // steps

    def kernel(place_ref, own, mate, *refs):
        sent, kept, turned, both = refs[-4:]

        @pl.when(pl.program_id(0) == 0)
        def _():
            for k in range(2):
                at = slice(k * quarter, (k + 1) * quarter)
                turned[at, :rows] = refs[k][...].T
                turned[at, rows:] = refs[2 + k][...].T

        total = dot(turned[:, :rows], own[...], 1, 0) + dot(turned[:, rows:], mate[...], 1, 0)
        for k in range(2):
            for y in range(2):
                both[y, k] = total[
                    k * quarter : (k + 1) * quarter, y * (tile // 2) : (y + 1) * (tile // 2)
                ].astype(BF)

        def write(output, behind, one, two):
            (sent, kept)[output][behind, 0] = both[one, two]

        part_out(place_ref, axes, write)

    wide = pl.BlockSpec((rows, tile), lambda t, place: (0, t))
    out = pl.BlockSpec((2, 1, quarter, tile // 2), lambda t, place: (0, t, 0, 0))
    return call(
        kernel,
        "grad_down",
        pair_struct((2, steps, quarter, tile // 2)),
        (steps,),
        [wide, wide] + core_columns(rows, quarter) * 2,
        (out, out),
        scratch=[pltpu.VMEM((2 * quarter, 2 * rows), BF), pltpu.VMEM((2, 2, quarter, tile // 2), BF)],
    )(place, units, mate_units, e3, e3, e3_mate, e3_mate)


def transposed(place, array):
    def kernel(place_ref, from_ref, to_ref):
        to_ref[...] = from_ref[...].T

    rows, cols = array.shape
    return call(
        kernel,
        "transposed",
        jax.ShapeDtypeStruct((cols, rows), array.dtype),
        (1,),
        [whole_spec((rows, cols))],
        whole_spec((cols, rows)),
    )(place, array)


def row_blocks(one_bit, two_bit, count):
    at = []
    for rest in range(count // 4):
        low, high = min(one_bit, two_bit), max(one_bit, two_bit)
        rest = ((rest >> low) << (low + 1)) | (rest & ((1 << low) - 1))
        rest = ((rest >> high) << (high + 1)) | (rest & ((1 << high) - 1))
        at.append(rest)
    return at


def grad_up(place, axes, m, m_mate, grads, mate_grads, bits, count):
    rows, depth = m.shape
    cols = grads.shape[1]
    size = depth // count
    others = row_blocks(*bits, count)

    def kernel(place_ref, m_ref, mate_ref, own, mate, *refs):
        sent, kept, both = refs[-3:]
        total = dot(m_ref[...].T, own[...], 1, 0) + dot(mate_ref[...].T, mate[...], 1, 0)
        for w in range(count):
            both[w] = total[w * size : (w + 1) * size].astype(BF)

        def write(output, behind, one, two):
            for n, rest in enumerate(others):
                (sent, kept)[output][behind, n] = both[
                    rest + (one << bits[0]) + (two << bits[1])
                ]

        part_out(place_ref, axes, write)

    shape = (2, count // 4, size, cols)
    return call(
        kernel,
        "grad_up",
        pair_struct(shape),
        (1,),
        [whole_spec((rows, depth))] * 2 + [whole_spec((rows, cols))] * 2,
        (whole_spec(shape),) * 2,
        scratch=[pltpu.VMEM((count, size, cols), BF)],
    )(place, m, m_mate, grads, mate_grads)


def grad_square(place, axes, members, count, bits=None):
    arrays, specs, plan = [], [], []
    known = {}
    for member in members:
        pieces = []
        for left, block, right, lead, whole in member:
            rows, depth = right.shape[-2], left.shape[1]
            quarter = right.shape[-1] // (4 if whole else 2)
            if (id(left), block) not in known:
                known[id(left), block] = len(arrays)
                arrays.append(left)
                specs.append(
                    pl.BlockSpec((rows, depth), lambda t, place, block=block: (block, 0))
                )
            pieces.append((known[id(left), block], len(arrays)))
            arrays += [right, right]
            for k in range(2):

                def column(t, place, k=k, lead=lead, whole=whole):
                    return (*lead, 0, 2 * k + place[1] if whole else k)

                specs.append(pl.BlockSpec((None,) * len(lead) + (rows, quarter), column))
        plan.append(pieces)
    size = depth // count
    others = row_blocks(*bits, count) if bits else range(count // 2)

    def kernel(place_ref, *refs):
        sent, kept, both = refs[-3:]
        turned = {}
        for n, pieces in enumerate(plan):
            total = 0.0
            for left, right in pieces:
                if left not in turned:
                    turned[left] = refs[left][...].T
                cols = jnp.concatenate([refs[right][...], refs[right + 1][...]], 1)
                total = total + dot(turned[left], cols, 1, 0)
            for w in range(count):
                rows = total[w * size : (w + 1) * size].astype(BF)
                if bits:
                    both[w] = rows
                else:
                    for k in range(2):
                        both[w, k] = rows[:, k * quarter : (k + 1) * quarter]

            def write(output, behind, one, two):
                for n_rest, rest in enumerate(others):
                    if bits:
                        found = both[rest + (one << bits[0]) + (two << bits[1])]
                    else:
                        found = both[2 * rest + one, two]
                    (sent, kept)[output][behind, n_rest, n] = found

            part_out(place_ref, axes, write)

    tile = (size, 2 * quarter) if bits else (2, size, quarter)
    shape = (2, len(others), len(members)) + tile[-2:]
    return call(
        kernel,
        "grad_square",
        pair_struct(shape),
        (1,),
        specs,
        (whole_spec(shape),) * 2,
        scratch=[pltpu.VMEM((count,) + tile, BF)],
    )(place, *arrays)


def first_backward(place, d, d_other, qkv, gains, own, far, e1, size):
    rows, width = e1.shape
    quarter, steps = width // 4, rows // size

    def kernel(place_ref, d0, d1, d2, other0, other1, other2, gain_ref, x_own, x_far, e1_ref, *refs):
        weights, (own_ref, far_ref, sum_ref) = refs[:12], refs[12:]
        grad = jnp.zeros((size, width), F32)
        for j, (d_ref, other_ref) in enumerate(((d0, other0), (d1, other1), (d2, other2))):
            for k in range(2):
                cols = slice(k * quarter, (k + 1) * quarter)
                grad = grad + dot(d_ref[:, cols], weights[4 * j + k][0], 1, 1)
                grad = grad + dot(other_ref[:, cols], weights[4 * j + 2 + k][0], 1, 1)
        x = jnp.where(pl.program_id(0) == 0, x_own[...], x_far[...])
        grad, gain, shift = norm_back(grad, gain_ref[0:1], x.astype(F32))
        total = e1_ref[...] + grad
        sums = jnp.concatenate([gain, shift], 0)

        @pl.when(pl.program_id(0) == 0)
        def _():
            own_ref[...] = total
            sum_ref[...] = sums

        @pl.when(pl.program_id(0) == 1)
        def _():
            far_ref[...] = total.astype(BF)
            sum_ref[...] += sums

    def weight_spec(j, flip, k):
        return pl.BlockSpec(
            (1, width, quarter), lambda i, place: (j, 0, 2 * k + (place[1] ^ flip))
        )

    return call(
        kernel,
        "first_backward",
        (out_struct(size, width, F32), out_struct(size, width), out_struct(2, width, F32)),
        (steps,),
        [row_spec(size, width // 2)] * 6
        + [whole_spec(gains.shape)]
        + [whole_spec((size, width))] * 2
        + [row_spec(size, width)]
        + [weight_spec(j, flip, k) for j in range(3) for flip in range(2) for k in range(2)],
        (whole_spec((size, width)), whole_spec((size, width)), whole_spec((2, width))),
    )(place, *d, *d_other, gains, own, far, e1, *[qkv] * 12)


def body(
    image_tokens,
    text_states,
    caption_lengths,
    text_mask,
    self_qkv,
    self_out,
    cross_query,
    cross_kv,
    cross_out,
    mlp_in,
    mlp_out,
    norm_gains,
    norm_shifts,
    out_biases,
    mlp_bias,
    cotangent,
):
    _, block, width = image_tokens.shape
    blocks = lax.axis_size("narrow")
    wide_size = lax.axis_size("wide")
    here = lax.axis_index("narrow")
    line = lax.axis_index("wide")
    chip, core = here // 2, here % 2
    wide_bits = wide_size.bit_length() - 1
    mates = [(i, i ^ 1) for i in range(blocks)]
    across = [(i, i ^ 2) for i in range(blocks)]

    def to_mate(value):
        return lax.ppermute(value, "narrow", mates)

    def to_chip(value):
        return lax.ppermute(value, "narrow", across)

    def item(array, index):
        return lax.dynamic_index_in_dim(array, index, 0, keepdims=False)

    def columns(array, side):
        quarter = array.shape[-1] // 4
        return jnp.concatenate(
            [
                lax.dynamic_slice_in_dim(array, (2 * k + side) * quarter, quarter, array.ndim - 1)
                for k in range(2)
            ],
            -1,
        )

    def chosen(first, second):
        return jnp.where(core == 0, first, second), jnp.where(core == 0, second, first)

    near = list(range(wide_bits))

    def partner(index, axis):
        line_at, here_at = divmod(index, blocks)
        if axis == "x":
            return line_at * blocks + (here_at ^ 2)
        return (line_at ^ (1 << axis)) * blocks + here_at

    def exchange(value, first, second=None):
        axes = (first, first if second is None else second)
        pairs = [(i, partner(i, axes[i % 2])) for i in range(wide_size * blocks)]
        return lax.ppermute(value, ("wide", "narrow"), pairs)

    def bit_of(axis):
        return chip if axis == "x" else (line >> axis) & 1

    class Scatter:
        def __init__(self, shape, one, two, dims):
            self.shape, self.axes, self.dims = shape, (one, two), dims
            self.kept, self.come = [], []

        def add(self, halves, *others):
            self.sent, kept = (half.reshape(self.shape) for half in halves)
            self.kept.append(kept)
            self.come.append(exchange(after(self.sent, *others), *self.axes))
            self.terms = [(tuple(self.kept), {}), (tuple(self.come), {})]
            self.count = len(self.kept)

        def values(self, extra):
            found = []
            for parts, taken in self.terms:
                taken = {**taken, **extra}
                split = len(parts) > 1
                which = taken.pop(1, None) if split else None
                pieces = []
                for array in parts:
                    at = [taken.get(d, 0) * (n // 2) for d, n in enumerate(array.shape)]
                    size = [n // 2 if d in taken else n for d, n in enumerate(array.shape)]
                    pieces.append(lax.dynamic_slice(array, at, size) if taken else array)
                if which is not None:
                    pieces = [jnp.where(which == 0, *pieces)]
                elif self.count > 1 and not split:
                    pieces = jnp.split(pieces[0], self.count, 1)
                found.append([piece.astype(F32) for piece in pieces])
            return [sum(pieces) for pieces in zip(*found)]

        def advance(self, bit, dim, *axes):
            if dim == 1:
                self.count = 1
            sums = [value.astype(BF) for value in self.values({dim: 1 - bit})]
            self.sent = sums[0] if len(sums) == 1 else jnp.concatenate(sums, 1)
            self.terms = [(parts, {**taken, dim: bit}) for parts, taken in self.terms]
            self.terms.append(((exchange(self.sent, *axes),), {}))

        def turn(self):
            one, two = self.axes
            self.advance(jnp.where(core == 0, bit_of(two), bit_of(one)), 0, two, one)

        def step(self, axis):
            self.advance(bit_of(axis), self.dims[axis], axis)

        def wait(self, *others):
            arrays = tuple(parts for parts, _ in self.terms)
            arrays = lax.optimization_barrier((arrays,) + others)[0]
            self.terms = [(a, taken) for a, (_, taken) in zip(arrays, self.terms)]

        def total(self, *shape):
            return self.values({})[0].reshape(shape)

    def bit_dims(first, *left_out):
        bits = [b for b in reversed(near) if b not in left_out]
        return (2,) * len(bits), {b: first + n for n, b in enumerate(bits)}

    def places(*axes):
        return tuple(2 if axis == "x" else 3 + axis for axis in axes)

    def both(own_part, mate_part):
        return jnp.concatenate([own_part, mate_part], 0)

    def after(value, *others):
        return lax.optimization_barrier((value,) + others)[0]

    rows_wide = width // wide_size
    quarter = width // 4

    def home(own, far):
        far = far.astype(F32)
        return jnp.where((jnp.arange(2) == chip)[:, None, None], own[None], far[None])

    own = jnp.concatenate([item(image_tokens, chip), item(text_states, chip)], 0)
    far = to_chip(
        jnp.concatenate([item(image_tokens, 1 - chip), item(text_states, 1 - chip)], 0)
    )
    own_mate = to_mate(own)
    place = jnp.stack([here, core, chip] + [(line >> b) & 1 for b in near]).astype(jnp.int32)
    first = project(place, own, own_mate, self_qkv, norm_gains, norm_shifts, 0, block, None)
    far = after(far, first[0])
    far_mate = to_mate(far)
    a, q, k, v = project(
        place, far, far_mate, self_qkv, norm_gains, norm_shifts, 1, block, first
    )
    text_all = jnp.concatenate(
        chosen(both(own[block:], far[block:]), both(own_mate[block:], far_mate[block:])), 0
    )
    slot_block = text_states.shape[1]
    slots = slot_block * blocks
    slot_order = jnp.stack([(2 * chip) ^ k for k in (0, 2, 1, 3)])
    slot = (slot_order[:, None] * slot_block + jnp.arange(slot_block)[None, :]).reshape(slots)
    kept = item(text_mask, chip).reshape(blocks, slot_block)
    kept = jnp.concatenate([item(kept, (2 * chip) ^ k) for k in (0, 2, 1, 3)], 0)
    length = item(caption_lengths, chip)
    live = ((slot < length) & ((kept == 1) | (slot == 0))).astype(F32).reshape(slots, 1)


    rows = 2 * block
    cot_far = to_chip(after(item(cotangent, 1 - chip), q))
    o, o_mate, log_self = self_forward(place, q, k, v, blocks)
    o_other = to_mate(after(o_mate, cot_far))
    text_all = after(text_all, o_mate)
    tk = dot(text_all, cross_kv[0], 1, 0).astype(BF)
    tv = dot(text_all, cross_kv[1], 1, 0).astype(BF)
    e3 = both(item(cotangent, chip), cot_far)
    os_rows, h1, c, qc, oc, log_cross, h2, m = middle_forward(
        place,
        live,
        own,
        far,
        o,
        o_other,
        self_out,
        norm_gains,
        norm_shifts,
        out_biases,
        cross_query,
        tk,
        tv,
        cross_out,
        block,
    )
    e3_mate, m_mate = to_mate(e3), to_mate(m)
    c_mate, oc_mate, os_mate = to_mate(c), to_mate(oc), to_mate(os_rows)
    bias_row = mlp_bias.reshape(1, -1)
    sums = (h2, out_biases)
    g, g_mate, kept, kept_mate, hidden_sums = [], [], [], [], []
    for part in range(2):
        units, sent, stay, hidden_sum, dm, *outs = mlp_part(
            place, m, e3, mlp_in, mlp_out, bias_row, *sums, part, TILE
        )
        g.append(units)
        g_mate.append(to_mate(units))
        kept.append(stay)
        kept_mate.append(to_mate(sent))
        hidden_sums.append(hidden_sum)
        if part == 0:
            sums = (outs[0], after(dm, e3_mate, m_mate, c_mate, oc_mate, os_mate))
    layer_out, out_far = outs
    out_far = to_chip(out_far)
    up_bits = (near[1], near[0])
    shape, dims = bit_dims(2, near[0], near[-1])
    dims[near[-1]] = 1
    down = Scatter(
        (2, 1) + shape + (quarter, mlp_out.shape[0] // wide_size), near[0], "x", dims
    )
    shape, dims = bit_dims(2, *up_bits)
    dims["x"] = 1
    up = Scatter((2, 1) + shape + (rows_wide, mlp_in.shape[1] // 4), *up_bits, dims)
    for part in range(2):
        down.add(
            grad_down(
                place, places(near[0], "x"), g[part], g_mate[part], e3, e3_mate, wide_size // 4
            )
        )
        kept[part] = after(kept[part], down.sent)
        up.add(
            grad_up(
                place, places(*up_bits), m, m_mate, kept[part], kept_mate[part], up_bits, wide_size
            )
        )
        if part == 0:
            g[1] = after(g[1], up.sent, out_far)
    dm = after(dm, up.sent)

    f2, dqc, f1, e1, do_own, do_other, *cols, dt, row_sums = middle_backward(
        place,
        live,
        dm,
        e3,
        h1,
        h2,
        qc,
        oc,
        log_cross,
        self_out,
        norm_gains,
        cross_query,
        tk,
        tv,
        cross_out,
        block,
    )
    dt_mate, do_mate = to_mate(dt), to_mate(do_other)
    cols_mate = [to_mate(part) for part in cols]
    down.wait(row_sums)
    down.turn()
    up.wait(row_sums, down.sent)
    up.turn()
    dt = after(dt, up.sent, down.sent)
    shape, dims = bit_dims(1, near[0])
    outer = Scatter((2,) + shape + (5, rows_wide, quarter), near[0], "x", dims)
    outer_halves = (
        grad_square(
            place,
            places(near[0], "x"),
            [
                [(oc, 0, f2, (), True), (oc_mate, 0, cols_mate[0], (), False)],
                [(text_all, 0, dt, (0,), True), (text_all, 0, dt_mate, (0,), True)],
                [(text_all, 0, dt, (1,), True), (text_all, 0, dt_mate, (1,), True)],
                [(c, 0, dqc, (), True), (c_mate, 0, cols_mate[1], (), False)],
                [(os_rows, 0, f1, (), True), (os_mate, 0, cols_mate[2], (), False)],
            ],
            wide_size,
        )
    )
    down.wait(outer_halves)
    down.step(near[1])
    up.wait(outer_halves, down.sent)
    for axis in near[2:]:
        up.step(axis)
    outer.add(outer_halves, down.sent, up.sent)
    do_mate = after(do_mate, down.sent, up.sent)
    d = self_backward(place, q, k, v, o, o_mate, do_own, do_mate, log_self, blocks)
    d, d_mate = d[:3], d[3:]
    d_other = [to_mate(part) for part in d_mate]
    for axis in near[2:]:
        down.wait(d)
        down.step(axis)
    d = after(d, down.sent)
    shape, dims = bit_dims(1, near[0])
    inner_shape, inner_dims = bit_dims(1, *up_bits)
    inner_shape = (2,) + inner_shape + (3, rows_wide, 2 * quarter)
    inner_dims["x"] = len(inner_shape) - 1
    inner = Scatter(inner_shape, *up_bits, inner_dims)
    inner.add(
        grad_square(
            place,
            places(*up_bits),
            [[(a, 0, d[j], (), False), (a, 1, d_mate[j], (), False)] for j in range(3)],
            wide_size,
            up_bits,
        )
    )
    up.wait(inner.sent)
    up.step("x")
    d_other = after(d_other, inner.sent, up.sent)
    grad_own, grad_far, late = first_backward(
        place, d, d_other, self_qkv, norm_gains, own, far, e1, block
    )
    image_far = to_chip(grad_far)
    late = jnp.concatenate(
        [late, row_sums[:7], jnp.concatenate(hidden_sums, 1).reshape(-1, width)]
    )
    late = late + to_mate(late)
    outer.wait(grad_far)
    outer.turn()
    inner.wait(outer.sent)
    inner.turn()
    late = after(late, inner.sent)
    for axis in near[1:]:
        late = late + exchange(late, axis)
    late_far = exchange(after(late, inner.sent), near[0])
    outer.wait(inner.sent)
    outer.step(near[1])
    late = late + after(late_far, outer.sent)
    late_far = to_chip(late)
    inner.wait(outer.sent)
    inner.step("x")
    dt = (dt.astype(F32) + dt_mate.astype(F32)).astype(BF)
    dt_own = lax.dynamic_slice_in_dim(dt, core * 2 * slot_block, 2 * slot_block, 1)
    dt_own = after(dt_own, inner.sent)
    grad_text = dot(dt_own[0], cross_kv[0], 1, 1) + dot(dt_own[1], cross_kv[1], 1, 1)
    text_far = to_chip(grad_text[slot_block:])
    for axis in near[2:]:
        outer.wait(inner.sent)
        outer.step(axis)
        inner.wait(outer.sent)
        inner.step(axis)
    down.wait(inner.sent)
    up.wait(inner.sent)
    outer.wait(inner.sent)
    inner.wait(inner.sent)
    late = late + after(late_far, inner.sent)
    image_far, out_far, text_far = after((image_far, out_far, text_far), inner.sent)

    outer_part = outer.total(5, rows_wide, quarter)
    inner_part = inner.total(3, rows_wide, quarter)
    down_part = transposed(place, down.total(quarter, mlp_out.shape[0] // wide_size))

    gains = jnp.stack([late[0], late[2], late[3]])
    shifts = jnp.stack([late[1], late[4], late[5]])
    return (
        home(layer_out, out_far),
        home(grad_own, image_far),
        home(grad_text[:slot_block], text_far),
        inner_part,
        outer_part[4],
        outer_part[3],
        outer_part[1:3],
        outer_part[0],
        up.total(rows_wide, mlp_in.shape[1] // 4),
        down_part,
        gains,
        shifts,
        late[6:9],
        late[9:].reshape(-1),
    )


def solution(mesh):
    rows = P("wide", "narrow", None)
    whole = P()
    return jax.shard_map(
        body,
        mesh=mesh,
        in_specs=(rows, rows, P("wide"), P("wide", None)) + (whole,) * 11 + (rows,),
        out_specs=(rows,) * 3
        + (
            P(None, "wide", "narrow"),
            P("wide", "narrow"),
            P("wide", "narrow"),
            P(None, "wide", "narrow"),
        )
        + (P("wide", "narrow"),) * 3
        + (whole,) * 4,
        check_vma=False,
    )
```

```python
import jax
import jax.numpy as jnp
from jax import lax
from jax.experimental import pallas as pl
from jax.experimental.pallas import tpu as pltpu
from jax.sharding import PartitionSpec as P

HEAD_DIM = 64
PAIR = 2 * HEAD_DIM
SCALE = HEAD_DIM**-0.5
NEG = -1e30
BF = jnp.bfloat16
F32 = jnp.float32
MIB = 1024 * 1024
VMEM = {
    "project": 16 * MIB,
    "self_forward": 16 * MIB,
    "self_backward": 24 * MIB,
    "middle_forward": 32 * MIB,
    "mlp": 40 * MIB,
    "grad_down": 20 * MIB,
    "grad_up": 20 * MIB,
    "middle_backward": 36 * MIB,
    "grad_square": 48 * MIB,
    "first_backward": 32 * MIB,
    "transposed": 8 * MIB,
}
TILE = 1024


def dot(left, right, left_axis, right_axis):
    return lax.dot_general(
        left, right, (((left_axis,), (right_axis,)), ((), ())), preferred_element_type=F32
    )


def two_heads(rows):
    lane = lax.broadcasted_iota(jnp.int32, rows.shape, 1)
    zero = jnp.zeros_like(rows)
    return jnp.concatenate(
        [jnp.where(lane < HEAD_DIM, rows, zero), jnp.where(lane < HEAD_DIM, zero, rows)], 0
    )


def block_rows(here, block, size):
    slot = here ^ block
    return pl.ds(pl.multiple_of(((slot & 1) * 2 + slot // 2) * size, size), size)


def slot_place(here, block, size):
    slot = here ^ block
    return slot & 1, pl.ds(pl.multiple_of((slot // 2) * size, size), size)


def store_sides(here, block, size, even, odd, own_ref, mate_ref):
    _, half = slot_place(here, block, size)
    own_first = (here & 1) == 0
    own_ref[half, :] = jnp.where(own_first, even, odd)
    mate_ref[half, :] = jnp.where(own_first, odd, even)


def causal_mask(scores, size):
    key = lax.broadcasted_iota(jnp.int32, scores.shape, 0)
    query = lax.broadcasted_iota(jnp.int32, scores.shape, 1)
    return jnp.where(key <= lax.rem(query, size), scores, NEG)


def self_forward_kernel(here_ref, q_ref, k_ref, v_ref, own_ref, mate_ref, log_ref, *, blocks):
    here = here_ref[0]
    size = q_ref.shape[0] // blocks
    for p in range(blocks):
        rows = block_rows(here, p, size)
        queries = two_heads(q_ref[rows, :] * BF(SCALE))
        scores = []
        for j in range(p + 1):
            s = dot(k_ref[block_rows(here, j, size), :], queries, 1, 1)
            scores.append(causal_mask(s, size) if j == p else s)
        top = scores[0].max(0, keepdims=True)
        for s in scores[1:]:
            top = jnp.maximum(top, s.max(0, keepdims=True))
        total = jnp.zeros_like(top)
        mixed = [jnp.zeros((HEAD_DIM, size), F32)] * 2
        for j in range(p + 1):
            e = jnp.exp(scores[j] - top)
            total = total + e.sum(0, keepdims=True)
            low = e.astype(BF)
            values = v_ref[block_rows(here, j, size), :].T
            for h in range(2):
                mixed[h] = mixed[h] + dot(
                    values[h * HEAD_DIM : (h + 1) * HEAD_DIM],
                    low[:, h * size : (h + 1) * size],
                    1,
                    0,
                )
        inverse = 1.0 / total
        both = jnp.concatenate(
            [mixed[h] * inverse[:, h * size : (h + 1) * size] for h in range(2)], 0
        )
        low = both.T.astype(BF)
        if p % 2:
            store_sides(here, p - 1, size, before, low, own_ref, mate_ref)
        before = low
        log_ref[0, :, 2 * size * p : 2 * size * (p + 1)] = top + jnp.log(total)


def row_dots(left, right):
    product = left.astype(F32).T * right.astype(F32).T
    return jnp.concatenate(
        [product[:HEAD_DIM].sum(0, keepdims=True), product[HEAD_DIM:].sum(0, keepdims=True)], 1
    )


def self_backward_kernel(
    here_ref,
    q_ref,
    k_ref,
    v_ref,
    o_ref,
    o_mate_ref,
    do_ref,
    do_mate_ref,
    log_ref,
    *sides,
    blocks,
):
    here = here_ref[0]
    size = q_ref.shape[0] // blocks
    queries, grads, inner, dq = [], [], [], []
    for p in range(blocks):
        rows = block_rows(here, p, size)
        queries.append(two_heads(q_ref[rows, :] * BF(SCALE)))
        side, half = slot_place(here, p, size)
        do = jnp.where(side == 0, do_ref[half, :], do_mate_ref[half, :])
        grads.append(two_heads(do))
        o = jnp.where(side == 0, o_ref[half, :], o_mate_ref[half, :])
        inner.append(row_dots(do, o))
        dq.append([jnp.zeros((HEAD_DIM, size), F32)] * 2)
    for j in range(blocks):
        rows = block_rows(here, j, size)
        keys, values = k_ref[rows, :], v_ref[rows, :]
        turned = keys.T
        dk = jnp.zeros(keys.shape, F32)
        dv = jnp.zeros(keys.shape, F32)
        for p in range(j, blocks):
            s = dot(keys, queries[p], 1, 1)
            if j == p:
                s = causal_mask(s, size)
            probs = jnp.exp(s - log_ref[0, :, 2 * size * p : 2 * size * (p + 1)])
            dprobs = dot(values, grads[p], 1, 1)
            ds = (probs * (dprobs - inner[p])).astype(BF)
            dv = dv + dot(probs.astype(BF), grads[p], 1, 0)
            dk = dk + dot(ds, queries[p], 1, 0)
            for h in range(2):
                dq[p][h] = dq[p][h] + dot(
                    turned[h * HEAD_DIM : (h + 1) * HEAD_DIM],
                    ds[:, h * size : (h + 1) * size],
                    1,
                    0,
                )
        low = dk.astype(BF), dv.astype(BF)
        if j % 2:
            for n in range(2):
                store_sides(here, j - 1, size, before[n], low[n], sides[1 + n], sides[4 + n])
        before = low
    for p in range(blocks):
        both = jnp.concatenate(dq[p], 0) * SCALE
        low = both.T.astype(BF)
        if p % 2:
            store_sides(here, p - 1, size, before, low, sides[0], sides[3])
        before = low


def pair_spec(rows):
    return pl.BlockSpec((rows, PAIR), lambda i, *_: (0, i))


def log_spec(width):
    return pl.BlockSpec((1, 1, width), lambda i, *_: (i, 0, 0))


def self_forward(here, q, k, v, blocks):
    rows, width = q.shape
    pairs = width // PAIR
    spec = pair_spec(rows)
    return pl.pallas_call(
        lambda *refs: self_forward_kernel(*refs, blocks=blocks),
        name="self_forward",
        out_shape=(
            jax.ShapeDtypeStruct((rows // 2, width), BF),
            jax.ShapeDtypeStruct((rows // 2, width), BF),
            jax.ShapeDtypeStruct((pairs, 1, 2 * rows), F32),
        ),
        grid_spec=pltpu.PrefetchScalarGridSpec(
            num_scalar_prefetch=1,
            grid=(pairs,),
            in_specs=[spec] * 3,
            out_specs=(pair_spec(rows // 2), pair_spec(rows // 2), log_spec(2 * rows)),
        ),
        compiler_params=pltpu.CompilerParams(vmem_limit_bytes=VMEM["self_forward"]),
        cost_estimate=cost("self_forward"),
    )(here, q, k, v)


def self_backward(here, q, k, v, o, o_mate, do, do_mate, log_total, blocks):
    rows, width = q.shape
    pairs = width // PAIR
    spec = pair_spec(rows)
    return pl.pallas_call(
        lambda *refs: self_backward_kernel(*refs, blocks=blocks),
        name="self_backward",
        out_shape=(jax.ShapeDtypeStruct((rows // 2, width), BF),) * 6,
        grid_spec=pltpu.PrefetchScalarGridSpec(
            num_scalar_prefetch=1,
            grid=(pairs,),
            in_specs=[spec] * 3 + [pair_spec(rows // 2)] * 4 + [log_spec(2 * rows)],
            out_specs=(pair_spec(rows // 2),) * 6,
        ),
        compiler_params=pltpu.CompilerParams(vmem_limit_bytes=VMEM["self_backward"]),
        cost_estimate=cost("self_backward"),
    )(here, q, k, v, o, o_mate, do, do_mate, log_total)


def standardize(rows):
    centered = rows - jnp.mean(rows, -1, keepdims=True)
    inverse = lax.rsqrt(jnp.mean(centered * centered, -1, keepdims=True) + 1e-05)
    return centered * inverse, inverse


def normed(rows, gain, shift):
    return (standardize(rows)[0] * gain + shift).astype(BF)


def norm_back(grad_out, gain, rows):
    unit, inverse = standardize(rows)
    grad_unit = grad_out * gain
    grad_in = inverse * (
        grad_unit
        - jnp.mean(grad_unit, -1, keepdims=True)
        - unit * jnp.mean(grad_unit * unit, -1, keepdims=True)
    )
    return grad_in, column_sum(grad_out * unit), column_sum(grad_out)


def column_sum(rows):
    return jnp.sum(rows.astype(F32), 0, keepdims=True)


def gelu_and_slope(pre):
    square = pre * pre
    bend = jnp.tanh(pre * (0.7978845608028654 + (0.7978845608028654 * 0.044715) * square))
    half = 0.5 + 0.5 * bend
    value = pre * half
    steep = 0.7978845608028654 + (3.0 * 0.7978845608028654 * 0.044715) * square
    return value, half + value * (1.0 - bend) * steep


def whole_spec(shape):
    return pl.BlockSpec(shape, lambda *_: (0,) * len(shape))


def row_spec(rows, cols, start=0):
    return pl.BlockSpec((rows, cols), lambda i, *_: (start + i, 0))


MICROSECONDS = {
    "self_forward": 13.0,
    "self_backward": 19.0,
    "project": 4.0,
    "middle_forward": 11.0,
    "mlp": 13.5,
    "grad_down": 5.0,
    "grad_up": 4.0,
    "middle_backward": 15.0,
    "grad_square": 8.0,
    "first_backward": 7.0,
    "transposed": 2.5,
}
SHARE = 1.0


def cost(name):
    flops = int(1.15e9 * SHARE * MICROSECONDS[name])
    return pl.CostEstimate(flops=flops, bytes_accessed=10**5, transcendentals=0)


def call(kernel, name, out_shape, grid, in_specs, out_specs, scratch=(), aliases=None):
    return pl.pallas_call(
        kernel,
        name=name,
        out_shape=out_shape,
        grid_spec=pltpu.PrefetchScalarGridSpec(
            num_scalar_prefetch=1,
            grid=grid,
            in_specs=in_specs,
            out_specs=out_specs,
            scratch_shapes=scratch,
        ),
        input_output_aliases=aliases or {},
        compiler_params=pltpu.CompilerParams(vmem_limit_bytes=VMEM[name]),
        cost_estimate=cost(name),
    )


def out_struct(rows, cols, kind=BF):
    return jax.ShapeDtypeStruct((rows, cols), kind)


def project(place, own, mate, qkv, gains, shifts, half, size, into):
    width = qkv.shape[1]
    quarter = width // 4

    def kernel(place_ref, own_ref, mate_ref, gain_ref, shift_ref, *refs):
        weights, outs = refs[:6], refs[-4:]
        rows = jnp.where(pl.program_id(0) == 0, own_ref[...], mate_ref[...]).astype(F32)
        a = normed(rows, gain_ref[0:1], shift_ref[0:1])
        outs[0][...] = a
        for j in range(3):
            pair = jnp.concatenate([weights[2 * j][0], weights[2 * j + 1][0]], 1)
            outs[1 + j][...] = dot(a, pair, 1, 0).astype(BF)

    def weight_spec(j, k):
        return pl.BlockSpec((1, width, quarter), lambda i, place: (j, 0, 2 * k + place[1]))

    def out_spec(cols):
        return pl.BlockSpec((size, cols), lambda i, place: (2 * i + half, 0))

    specs = [whole_spec((size, width))] * 2 + [whole_spec(gains.shape)] * 2
    specs += [weight_spec(j, k) for j in range(3) for k in range(2)]
    arrays = [own, mate, gains, shifts] + [qkv] * 6
    aliases = None
    if into is not None:
        aliases = {1 + len(arrays) + n: n for n in range(4)}
        arrays += list(into)
        specs += [pl.BlockSpec(memory_space=pl.ANY)] * 4
    rows = 4 * size
    return call(
        kernel,
        "project",
        (out_struct(rows, width),) + (out_struct(rows, width // 2),) * 3,
        (2,),
        specs,
        (out_spec(width),) + (out_spec(width // 2),) * 3,
        aliases=aliases,
    )(place, *arrays)


def head_row_specs(width):
    quarter = width // 4
    return [
        pl.BlockSpec((quarter, width), lambda i, place, k=k, flip=flip: (2 * k + (place[1] ^ flip), 0))
        for flip in range(2)
        for k in range(2)
    ]


def middle_forward(place, live, own, far, o, o_other, self_out, gains, shifts, biases, wq, tk, tv, wo, size):
    rows, width = 2 * size, own.shape[1]
    quarter, slots, steps = width // 4, tk.shape[0], rows // size

    def kernel(
        place_ref,
        live_ref,
        own_ref,
        far_ref,
        o_ref,
        other_ref,
        w0,
        w1,
        w2,
        w3,
        gain_ref,
        shift_ref,
        bias_ref,
        wq_ref,
        tk_ref,
        tv_ref,
        wo_ref,
        os_ref,
        h1_ref,
        c_ref,
        qc_ref,
        oc_ref,
        log_ref,
        h2_ref,
        m_ref,
    ):
        core = place_ref[1]
        x = jnp.where(pl.program_id(0) == 0, own_ref[...], far_ref[...])
        h1 = x.astype(F32) + bias_ref[0:1]
        for n, (ref, weight) in enumerate(
            ((o_ref, w0), (o_ref, w1), (other_ref, w2), (other_ref, w3))
        ):
            k, side = n % 2, core ^ (n // 2)
            part = ref[:, k * quarter : (k + 1) * quarter]
            at = pl.multiple_of((2 * k + side) * quarter, quarter)
            os_ref[:, pl.ds(at, quarter)] = part
            h1 = h1 + dot(part, weight[...], 1, 0)
        h1_ref[...] = h1
        c = normed(h1, gain_ref[1:2], shift_ref[1:2])
        c_ref[...] = c
        qc_ref[...] = dot(c, wq_ref[...], 1, 0).astype(BF)
        for pair in range(width // PAIR):
            lanes = slice(pair * PAIR, (pair + 1) * PAIR)
            queries = two_heads(qc_ref[:, lanes] * BF(SCALE))
            s = dot(tk_ref[:, lanes], queries, 1, 1)
            s = jnp.where(live_ref[...] > 0, s, NEG)
            top = s.max(0, keepdims=True)
            e = jnp.exp(s - top)
            total = e.sum(0, keepdims=True)
            low = e.astype(BF)
            values = tv_ref[:, lanes].T
            inverse = 1.0 / total
            both = jnp.concatenate(
                [
                    dot(
                        values[h * HEAD_DIM : (h + 1) * HEAD_DIM],
                        low[:, h * size : (h + 1) * size],
                        1,
                        0,
                    )
                    * inverse[:, h * size : (h + 1) * size]
                    for h in range(2)
                ],
                0,
            )
            oc_ref[:, lanes] = both.T.astype(BF)
            log_ref[0, pair : pair + 1] = top + jnp.log(total)
        h2 = h1 + dot(oc_ref[...], wo_ref[...], 1, 0) + bias_ref[1:2]
        h2_ref[...] = h2
        m_ref[...] = normed(h2, gain_ref[2:3], shift_ref[2:3])

    row = row_spec(size, width)
    square = whole_spec((width, width))
    low, high = out_struct(rows, width), out_struct(rows, width, F32)
    pairs = width // PAIR
    return call(
        kernel,
        "middle_forward",
        (low, high, low, low, low, jax.ShapeDtypeStruct((steps, pairs, 2 * size), F32), high, low),
        (steps,),
        [
            whole_spec((slots, 1)),
            whole_spec((size, width)),
            whole_spec((size, width)),
            row_spec(size, width // 2),
            row_spec(size, width // 2),
        ]
        + head_row_specs(width)
        + [whole_spec(gains.shape)] * 3
        + [square, whole_spec((slots, width)), whole_spec((slots, width)), square],
        (row,) * 5 + (pl.BlockSpec((1, pairs, 2 * size), lambda i, *_: (i, 0, 0)), row, row),
    )(place, live, own, far, o, o_other, *[self_out] * 4, gains, shifts, biases, wq, tk, tv, wo)


def middle_backward(
    place, live, dm, e3, h1, h2, qc, oc, logs, self_out, gains, wq, tk, tv, wo, size
):
    rows, width = h1.shape
    quarter, slots, steps = width // 4, tk.shape[0], rows // size

    def kernel(
        place_ref,
        live_ref,
        dm_ref,
        e3_ref,
        h1_ref,
        h2_ref,
        qc_ref,
        oc_ref,
        log_ref,
        w0,
        w1,
        w2,
        w3,
        gain_ref,
        wq_ref,
        tk_ref,
        tv_ref,
        wo_ref,
        f2_ref,
        dqc_ref,
        f1_ref,
        e1_ref,
        do_ref,
        other_ref,
        cols_f2,
        cols_dqc,
        cols_f1,
        dt_ref,
        sum_ref,
        doc_ref,
        dtk_sum,
        dtv_sum,
    ):
        first = pl.program_id(0) == 0

        @pl.when(first)
        def _():
            dtk_sum[...] = jnp.zeros_like(dtk_sum)
            dtv_sum[...] = jnp.zeros_like(dtv_sum)

        e3 = e3_ref[...].astype(F32)
        grad, gain_three, shift_three = norm_back(dm_ref[...], gain_ref[2:3], h2_ref[...])
        e2 = e3 + grad
        f2 = e2.astype(BF)
        f2_ref[...] = f2
        doc_ref[...] = dot(f2, wo_ref[...], 1, 1).astype(BF)
        for pair in range(width // PAIR):
            lanes = slice(pair * PAIR, (pair + 1) * PAIR)
            queries = two_heads(qc_ref[:, lanes] * BF(SCALE))
            doc = doc_ref[:, lanes]
            grads = two_heads(doc)
            inner = row_dots(doc, oc_ref[:, lanes])
            keys = tk_ref[:, lanes]
            s = dot(keys, queries, 1, 1)
            s = jnp.where(live_ref[...] > 0, s, NEG)
            probs = jnp.exp(s - log_ref[0, pair : pair + 1])
            dprobs = dot(tv_ref[:, lanes], grads, 1, 1)
            ds = (probs * (dprobs - inner)).astype(BF)
            dtv_sum[:, lanes] += dot(probs.astype(BF), grads, 1, 0)
            dtk_sum[:, lanes] += dot(ds, queries, 1, 0)
            turned = keys.T
            both = jnp.concatenate(
                [
                    dot(
                        turned[h * HEAD_DIM : (h + 1) * HEAD_DIM],
                        ds[:, h * size : (h + 1) * size],
                        1,
                        0,
                    )
                    for h in range(2)
                ],
                0,
            )
            dqc_ref[:, lanes] = (both * SCALE).T.astype(BF)
        dc = dot(dqc_ref[...], wq_ref[...], 1, 1)
        grad, gain_two, shift_two = norm_back(dc, gain_ref[1:2], h1_ref[...])
        e1 = e2 + grad
        e1_ref[...] = e1
        f1 = e1.astype(BF)
        f1_ref[...] = f1
        for n, (ref, weight) in enumerate(
            ((do_ref, w0), (do_ref, w1), (other_ref, w2), (other_ref, w3))
        ):
            k = n % 2
            ref[:, k * quarter : (k + 1) * quarter] = dot(f1, weight[...], 1, 1).astype(BF)
        for ref, cols_ref in ((f2_ref, cols_f2), (dqc_ref, cols_dqc), (f1_ref, cols_f1)):
            for k in range(2):
                at = pl.multiple_of((2 * k + 1 - place_ref[1]) * quarter, quarter)
                cols_ref[:, k * quarter : (k + 1) * quarter] = ref[:, pl.ds(at, quarter)]
        sums = jnp.concatenate(
            [gain_two, gain_three, shift_two, shift_three]
            + [column_sum(v) for v in (f1, f2, e3)]
            + [jnp.zeros_like(gain_two)],
            0,
        )

        @pl.when(first)
        def _():
            sum_ref[...] = sums

        @pl.when(jnp.logical_not(first))
        def _():
            sum_ref[...] += sums

        @pl.when(pl.program_id(0) == steps - 1)
        def _():
            dt_ref[0] = dtk_sum[...].astype(BF)
            dt_ref[1] = dtv_sum[...].astype(BF)

    row, half = row_spec(size, width), row_spec(size, width // 2)
    square, text = whole_spec((width, width)), whole_spec((slots, width))
    low, narrow = out_struct(rows, width), out_struct(rows, width // 2)
    pairs = width // PAIR
    return call(
        kernel,
        "middle_backward",
        (low, low, low, out_struct(rows, width, F32), narrow, narrow)
        + (narrow,) * 3
        + (jax.ShapeDtypeStruct((2, slots, width), BF),)
        + (out_struct(8, width, F32),),
        (steps,),
        [whole_spec((slots, 1))]
        + [row] * 6
        + [pl.BlockSpec((1, pairs, 2 * size), lambda i, *_: (i, 0, 0))]
        + head_row_specs(width)
        + [whole_spec(gains.shape), square, text, text, square],
        (row,) * 4
        + (half,) * 5
        + (whole_spec((2, slots, width)),)
        + (whole_spec((8, width)),),
        scratch=[
            pltpu.VMEM((size, width), BF),
            pltpu.VMEM((slots, width), F32),
            pltpu.VMEM((slots, width), F32),
        ],
    )(place, live, dm, e3, h1, h2, qc, oc, logs, *[self_out] * 4, gains, wq, tk, tv, wo)


def mlp_part(place, m, e3, w_in, w_out, bias, start, dm_sum, part, tile):
    rows, width = m.shape
    hidden = w_in.shape[1] // 2
    steps = hidden // tile
    turn = steps // 2

    def column(t, place):
        ahead = t < turn
        side = jnp.where(ahead, 1 - place[1], place[1])
        return side * turn + jnp.where(ahead, t, t - turn)

    def kernel(place_ref, m_ref, e3_ref, in_ref, out_ref, bias_ref, *refs):
        starts, (g_ref, far_ref, near_ref, sum_ref, dm_ref, *outs, o_ref) = refs[:2], refs[2:]
        t = pl.program_id(0)

        @pl.when(t == 0)
        def _():
            o_ref[...] = starts[0][...] + starts[1][2:3] if part == 0 else starts[0][...]
            dm_ref[...] = jnp.zeros_like(dm_ref) if part == 0 else starts[1][...]

        g, slope = gelu_and_slope(dot(m_ref[...], in_ref[...], 1, 0) + bias_ref[...])
        g = g.astype(BF)
        g_ref[...] = g
        dg = dot(e3_ref[...], out_ref[...], 1, 1).astype(BF).astype(F32)
        d = (dg * slope).astype(BF)

        @pl.when(t < turn)
        def _():
            far_ref[...] = d

        @pl.when(t >= turn)
        def _():
            near_ref[...] = d

        sum_ref[...] = column_sum(d)
        o_ref[...] += dot(g, out_ref[...], 1, 0)
        dm_ref[...] += dot(d, in_ref[...], 1, 1)

        if part:

            @pl.when(t == steps - 1)
            def _():
                outs[0][...] = o_ref[: rows // 2]
                outs[1][...] = o_ref[rows // 2 :].astype(BF)

    full = whole_spec((rows, width))
    wide = pl.BlockSpec((rows, tile), lambda t, place: (0, column(t, place)))
    second = whole_spec(dm_sum.shape)
    return call(
        kernel,
        "mlp",
        (out_struct(rows, hidden), out_struct(rows, hidden // 2), out_struct(rows, hidden // 2))
        + (out_struct(1, hidden, F32), out_struct(rows, width, F32))
        + (
            (out_struct(rows // 2, width, F32), out_struct(rows // 2, width))
            if part
            else (out_struct(rows, width, F32),)
        ),
        (steps,),
        [
            full,
            full,
            pl.BlockSpec((width, tile), lambda t, place: (0, part * steps + column(t, place))),
            pl.BlockSpec((tile, width), lambda t, place: (part * steps + column(t, place), 0)),
            pl.BlockSpec((1, tile), lambda t, place: (0, part * steps + column(t, place))),
            full,
            second,
        ],
        (
            wide,
            pl.BlockSpec((rows, tile), lambda t, place: (0, jnp.minimum(t, turn - 1))),
            pl.BlockSpec((rows, tile), lambda t, place: (0, jnp.maximum(t - turn, 0))),
            pl.BlockSpec((1, tile), lambda t, place: (0, column(t, place))),
            full,
        )
        + ((whole_spec((rows // 2, width)),) * 2 if part else (full,)),
        scratch=[pltpu.VMEM((rows, width), F32)] if part else [],
    )(place, m, e3, w_in, w_out, bias, start, dm_sum)


def part_out(place_ref, axes, write):
    core = place_ref[1]
    mine = jnp.where(core == 0, place_ref[axes[0]], place_ref[axes[1]])
    for ahead, output in ((1 - mine, 0), (mine, 1)):
        for behind in range(2):
            write(
                output,
                behind,
                jnp.where(core == 0, ahead, behind),
                jnp.where(core == 0, behind, ahead),
            )


def core_columns(rows, quarter):
    return [
        pl.BlockSpec((rows, quarter), lambda t, place, k=k: (0, 2 * k + place[1]))
        for k in range(2)
    ]


def pair_struct(shape):
    return (jax.ShapeDtypeStruct(shape, BF),) * 2


def grad_down(place, axes, units, mate_units, e3, e3_mate, steps):
    rows, half = units.shape
    quarter = e3.shape[1] // 4
    tile = half // steps

    def kernel(place_ref, own, mate, *refs):
        sent, kept, turned, both = refs[-4:]

        @pl.when(pl.program_id(0) == 0)
        def _():
            for k in range(2):
                at = slice(k * quarter, (k + 1) * quarter)
                turned[at, :rows] = refs[k][...].T
                turned[at, rows:] = refs[2 + k][...].T

        total = dot(turned[:, :rows], own[...], 1, 0) + dot(turned[:, rows:], mate[...], 1, 0)
        for k in range(2):
            for y in range(2):
                both[y, k] = total[
                    k * quarter : (k + 1) * quarter, y * (tile // 2) : (y + 1) * (tile // 2)
                ].astype(BF)

        def write(output, behind, one, two):
            (sent, kept)[output][behind, 0] = both[one, two]

        part_out(place_ref, axes, write)

    wide = pl.BlockSpec((rows, tile), lambda t, place: (0, t))
    out = pl.BlockSpec((2, 1, quarter, tile // 2), lambda t, place: (0, t, 0, 0))
    return call(
        kernel,
        "grad_down",
        pair_struct((2, steps, quarter, tile // 2)),
        (steps,),
        [wide, wide] + core_columns(rows, quarter) * 2,
        (out, out),
        scratch=[pltpu.VMEM((2 * quarter, 2 * rows), BF), pltpu.VMEM((2, 2, quarter, tile // 2), BF)],
    )(place, units, mate_units, e3, e3, e3_mate, e3_mate)


def transposed(place, array):
    def kernel(place_ref, from_ref, to_ref):
        to_ref[...] = from_ref[...].T

    rows, cols = array.shape
    return call(
        kernel,
        "transposed",
        jax.ShapeDtypeStruct((cols, rows), array.dtype),
        (1,),
        [whole_spec((rows, cols))],
        whole_spec((cols, rows)),
    )(place, array)


def row_blocks(one_bit, two_bit, count):
    at = []
    for rest in range(count // 4):
        low, high = min(one_bit, two_bit), max(one_bit, two_bit)
        rest = ((rest >> low) << (low + 1)) | (rest & ((1 << low) - 1))
        rest = ((rest >> high) << (high + 1)) | (rest & ((1 << high) - 1))
        at.append(rest)
    return at


def grad_up(place, axes, m, m_mate, grads, mate_grads, bits, count):
    rows, depth = m.shape
    cols = grads.shape[1]
    size = depth // count
    others = row_blocks(*bits, count)

    def kernel(place_ref, m_ref, mate_ref, own, mate, *refs):
        sent, kept, both = refs[-3:]
        total = dot(m_ref[...].T, own[...], 1, 0) + dot(mate_ref[...].T, mate[...], 1, 0)
        for w in range(count):
            both[w] = total[w * size : (w + 1) * size].astype(BF)

        def write(output, behind, one, two):
            for n, rest in enumerate(others):
                (sent, kept)[output][behind, n] = both[
                    rest + (one << bits[0]) + (two << bits[1])
                ]

        part_out(place_ref, axes, write)

    shape = (2, count // 4, size, cols)
    return call(
        kernel,
        "grad_up",
        pair_struct(shape),
        (1,),
        [whole_spec((rows, depth))] * 2 + [whole_spec((rows, cols))] * 2,
        (whole_spec(shape),) * 2,
        scratch=[pltpu.VMEM((count, size, cols), BF)],
    )(place, m, m_mate, grads, mate_grads)


def grad_square(place, axes, members, count, bits=None):
    arrays, specs, plan = [], [], []
    known = {}
    for member in members:
        pieces = []
        for left, block, right, lead, whole in member:
            rows, depth = right.shape[-2], left.shape[1]
            quarter = right.shape[-1] // (4 if whole else 2)
            if (id(left), block) not in known:
                known[id(left), block] = len(arrays)
                arrays.append(left)
                specs.append(
                    pl.BlockSpec((rows, depth), lambda t, place, block=block: (block, 0))
                )
            pieces.append((known[id(left), block], len(arrays)))
            arrays += [right, right]
            for k in range(2):

                def column(t, place, k=k, lead=lead, whole=whole):
                    return (*lead, 0, 2 * k + place[1] if whole else k)

                specs.append(pl.BlockSpec((None,) * len(lead) + (rows, quarter), column))
        plan.append(pieces)
    size = depth // count
    others = row_blocks(*bits, count) if bits else range(count // 2)

    def kernel(place_ref, *refs):
        sent, kept, both = refs[-3:]
        turned = {}
        for n, pieces in enumerate(plan):
            total = 0.0
            for left, right in pieces:
                if left not in turned:
                    turned[left] = refs[left][...].T
                cols = jnp.concatenate([refs[right][...], refs[right + 1][...]], 1)
                total = total + dot(turned[left], cols, 1, 0)
            for w in range(count):
                rows = total[w * size : (w + 1) * size].astype(BF)
                if bits:
                    both[w] = rows
                else:
                    for k in range(2):
                        both[w, k] = rows[:, k * quarter : (k + 1) * quarter]

            def write(output, behind, one, two):
                for n_rest, rest in enumerate(others):
                    if bits:
                        found = both[rest + (one << bits[0]) + (two << bits[1])]
                    else:
                        found = both[2 * rest + one, two]
                    (sent, kept)[output][behind, n_rest, n] = found

            part_out(place_ref, axes, write)

    tile = (size, 2 * quarter) if bits else (2, size, quarter)
    shape = (2, len(others), len(members)) + tile[-2:]
    return call(
        kernel,
        "grad_square",
        pair_struct(shape),
        (1,),
        specs,
        (whole_spec(shape),) * 2,
        scratch=[pltpu.VMEM((count,) + tile, BF)],
    )(place, *arrays)


def first_backward(place, d, d_other, qkv, gains, own, far, e1, size):
    rows, width = e1.shape
    quarter, steps = width // 4, rows // size

    def kernel(place_ref, d0, d1, d2, other0, other1, other2, gain_ref, x_own, x_far, e1_ref, *refs):
        weights, (own_ref, far_ref, sum_ref) = refs[:12], refs[12:]
        grad = jnp.zeros((size, width), F32)
        for j, (d_ref, other_ref) in enumerate(((d0, other0), (d1, other1), (d2, other2))):
            for k in range(2):
                cols = slice(k * quarter, (k + 1) * quarter)
                grad = grad + dot(d_ref[:, cols], weights[4 * j + k][0], 1, 1)
                grad = grad + dot(other_ref[:, cols], weights[4 * j + 2 + k][0], 1, 1)
        x = jnp.where(pl.program_id(0) == 0, x_own[...], x_far[...])
        grad, gain, shift = norm_back(grad, gain_ref[0:1], x.astype(F32))
        total = e1_ref[...] + grad
        sums = jnp.concatenate([gain, shift], 0)

        @pl.when(pl.program_id(0) == 0)
        def _():
            own_ref[...] = total
            sum_ref[...] = sums

        @pl.when(pl.program_id(0) == 1)
        def _():
            far_ref[...] = total.astype(BF)
            sum_ref[...] += sums

    def weight_spec(j, flip, k):
        return pl.BlockSpec(
            (1, width, quarter), lambda i, place: (j, 0, 2 * k + (place[1] ^ flip))
        )

    return call(
        kernel,
        "first_backward",
        (out_struct(size, width, F32), out_struct(size, width), out_struct(2, width, F32)),
        (steps,),
        [row_spec(size, width // 2)] * 6
        + [whole_spec(gains.shape)]
        + [whole_spec((size, width))] * 2
        + [row_spec(size, width)]
        + [weight_spec(j, flip, k) for j in range(3) for flip in range(2) for k in range(2)],
        (whole_spec((size, width)), whole_spec((size, width)), whole_spec((2, width))),
    )(place, *d, *d_other, gains, own, far, e1, *[qkv] * 12)


def body(
    image_tokens,
    text_states,
    caption_lengths,
    text_mask,
    self_qkv,
    self_out,
    cross_query,
    cross_kv,
    cross_out,
    mlp_in,
    mlp_out,
    norm_gains,
    norm_shifts,
    out_biases,
    mlp_bias,
    cotangent,
):
    _, block, width = image_tokens.shape
    blocks = lax.axis_size("narrow")
    wide_size = lax.axis_size("wide")
    here = lax.axis_index("narrow")
    line = lax.axis_index("wide")
    chip, core = here // 2, here % 2
    wide_bits = wide_size.bit_length() - 1
    mates = [(i, i ^ 1) for i in range(blocks)]
    across = [(i, i ^ 2) for i in range(blocks)]

    def to_mate(value):
        return lax.ppermute(value, "narrow", mates)

    def to_chip(value):
        return lax.ppermute(value, "narrow", across)

    def item(array, index):
        return lax.dynamic_index_in_dim(array, index, 0, keepdims=False)

    def columns(array, side):
        quarter = array.shape[-1] // 4
        return jnp.concatenate(
            [
                lax.dynamic_slice_in_dim(array, (2 * k + side) * quarter, quarter, array.ndim - 1)
                for k in range(2)
            ],
            -1,
        )

    def chosen(first, second):
        return jnp.where(core == 0, first, second), jnp.where(core == 0, second, first)

    near = list(range(wide_bits))

    def partner(index, axis):
        line_at, here_at = divmod(index, blocks)
        if axis == "x":
            return line_at * blocks + (here_at ^ 2)
        return (line_at ^ (1 << axis)) * blocks + here_at

    def exchange(value, first, second=None):
        axes = (first, first if second is None else second)
        pairs = [(i, partner(i, axes[i % 2])) for i in range(wide_size * blocks)]
        return lax.ppermute(value, ("wide", "narrow"), pairs)

    def bit_of(axis):
        return chip if axis == "x" else (line >> axis) & 1

    class Scatter:
        def __init__(self, shape, one, two, dims):
            self.shape, self.axes, self.dims = shape, (one, two), dims
            self.kept, self.come = [], []

        def add(self, halves, *others):
            self.sent, kept = (half.reshape(self.shape) for half in halves)
            self.kept.append(kept)
            self.come.append(exchange(after(self.sent, *others), *self.axes))
            self.terms = [(tuple(self.kept), {}), (tuple(self.come), {})]
            self.count = len(self.kept)

        def values(self, extra):
            found = []
            for parts, taken in self.terms:
                taken = {**taken, **extra}
                split = len(parts) > 1
                which = taken.pop(1, None) if split else None
                pieces = []
                for array in parts:
                    at = [taken.get(d, 0) * (n // 2) for d, n in enumerate(array.shape)]
                    size = [n // 2 if d in taken else n for d, n in enumerate(array.shape)]
                    pieces.append(lax.dynamic_slice(array, at, size) if taken else array)
                if which is not None:
                    pieces = [jnp.where(which == 0, *pieces)]
                elif self.count > 1 and not split:
                    pieces = jnp.split(pieces[0], self.count, 1)
                found.append([piece.astype(F32) for piece in pieces])
            return [sum(pieces) for pieces in zip(*found)]

        def advance(self, bit, dim, *axes):
            if dim == 1:
                self.count = 1
            sums = [value.astype(BF) for value in self.values({dim: 1 - bit})]
            self.sent = sums[0] if len(sums) == 1 else jnp.concatenate(sums, 1)
            self.terms = [(parts, {**taken, dim: bit}) for parts, taken in self.terms]
            self.terms.append(((exchange(self.sent, *axes),), {}))

        def turn(self):
            one, two = self.axes
            self.advance(jnp.where(core == 0, bit_of(two), bit_of(one)), 0, two, one)

        def step(self, axis):
            self.advance(bit_of(axis), self.dims[axis], axis)

        def wait(self, *others):
            arrays = tuple(parts for parts, _ in self.terms)
            arrays = lax.optimization_barrier((arrays,) + others)[0]
            self.terms = [(a, taken) for a, (_, taken) in zip(arrays, self.terms)]

        def total(self, *shape):
            return self.values({})[0].reshape(shape)

    def bit_dims(first, *left_out):
        bits = [b for b in reversed(near) if b not in left_out]
        return (2,) * len(bits), {b: first + n for n, b in enumerate(bits)}

    def places(*axes):
        return tuple(2 if axis == "x" else 3 + axis for axis in axes)

    def both(own_part, mate_part):
        return jnp.concatenate([own_part, mate_part], 0)

    def after(value, *others):
        return lax.optimization_barrier((value,) + others)[0]

    rows_wide = width // wide_size
    quarter = width // 4

    def home(own, far):
        far = far.astype(F32)
        return jnp.where((jnp.arange(2) == chip)[:, None, None], own[None], far[None])

    own = jnp.concatenate([item(image_tokens, chip), item(text_states, chip)], 0)
    far = to_chip(
        jnp.concatenate([item(image_tokens, 1 - chip), item(text_states, 1 - chip)], 0)
    )
    own_mate = to_mate(own)
    place = jnp.stack([here, core, chip] + [(line >> b) & 1 for b in near]).astype(jnp.int32)
    first = project(place, own, own_mate, self_qkv, norm_gains, norm_shifts, 0, block, None)
    far = after(far, first[0])
    far_mate = to_mate(far)
    a, q, k, v = project(
        place, far, far_mate, self_qkv, norm_gains, norm_shifts, 1, block, first
    )
    text_all = jnp.concatenate(
        chosen(both(own[block:], far[block:]), both(own_mate[block:], far_mate[block:])), 0
    )
    slot_block = text_states.shape[1]
    slots = slot_block * blocks
    slot_order = jnp.stack([(2 * chip) ^ k for k in (0, 2, 1, 3)])
    slot = (slot_order[:, None] * slot_block + jnp.arange(slot_block)[None, :]).reshape(slots)
    kept = item(text_mask, chip).reshape(blocks, slot_block)
    kept = jnp.concatenate([item(kept, (2 * chip) ^ k) for k in (0, 2, 1, 3)], 0)
    length = item(caption_lengths, chip)
    live = ((slot < length) & ((kept == 1) | (slot == 0))).astype(F32).reshape(slots, 1)


    rows = 2 * block
    cot_far = to_chip(after(item(cotangent, 1 - chip), q))
    o, o_mate, log_self = self_forward(place, q, k, v, blocks)
    o_other = to_mate(after(o_mate, cot_far))
    text_all = after(text_all, o_mate)
    tk = dot(text_all, cross_kv[0], 1, 0).astype(BF)
    tv = dot(text_all, cross_kv[1], 1, 0).astype(BF)
    e3 = both(item(cotangent, chip), cot_far)
    os_rows, h1, c, qc, oc, log_cross, h2, m = middle_forward(
        place,
        live,
        own,
        far,
        o,
        o_other,
        self_out,
        norm_gains,
        norm_shifts,
        out_biases,
        cross_query,
        tk,
        tv,
        cross_out,
        block,
    )
    e3_mate, m_mate = to_mate(e3), to_mate(m)
    c_mate, oc_mate, os_mate = to_mate(c), to_mate(oc), to_mate(os_rows)
    bias_row = mlp_bias.reshape(1, -1)
    sums = (h2, out_biases)
    g, g_mate, kept, kept_mate, hidden_sums = [], [], [], [], []
    for part in range(2):
        units, sent, stay, hidden_sum, dm, *outs = mlp_part(
            place, m, e3, mlp_in, mlp_out, bias_row, *sums, part, TILE
        )
        g.append(units)
        g_mate.append(to_mate(units))
        kept.append(stay)
        kept_mate.append(to_mate(sent))
        hidden_sums.append(hidden_sum)
        if part == 0:
            sums = (outs[0], after(dm, e3_mate, m_mate, c_mate, oc_mate, os_mate))
    layer_out, out_far = outs
    out_far = to_chip(out_far)
    up_bits = (near[1], near[0])
    shape, dims = bit_dims(2, near[0], near[-1])
    dims[near[-1]] = 1
    down = Scatter(
        (2, 1) + shape + (quarter, mlp_out.shape[0] // wide_size), near[0], "x", dims
    )
    shape, dims = bit_dims(2, *up_bits)
    dims["x"] = 1
    up = Scatter((2, 1) + shape + (rows_wide, mlp_in.shape[1] // 4), *up_bits, dims)
    for part in range(2):
        down.add(
            grad_down(
                place, places(near[0], "x"), g[part], g_mate[part], e3, e3_mate, wide_size // 4
            )
        )
        kept[part] = after(kept[part], down.sent)
        up.add(
            grad_up(
                place, places(*up_bits), m, m_mate, kept[part], kept_mate[part], up_bits, wide_size
            )
        )
        if part == 0:
            g[1] = after(g[1], up.sent, out_far)
    dm = after(dm, up.sent)

    f2, dqc, f1, e1, do_own, do_other, *cols, dt, row_sums = middle_backward(
        place,
        live,
        dm,
        e3,
        h1,
        h2,
        qc,
        oc,
        log_cross,
        self_out,
        norm_gains,
        cross_query,
        tk,
        tv,
        cross_out,
        block,
    )
    dt_mate, do_mate = to_mate(dt), to_mate(do_other)
    cols_mate = [to_mate(part) for part in cols]
    down.wait(row_sums)
    down.turn()
    up.wait(row_sums, down.sent)
    up.turn()
    dt = after(dt, up.sent, down.sent)
    shape, dims = bit_dims(1, near[0])
    outer = Scatter((2,) + shape + (5, rows_wide, quarter), near[0], "x", dims)
    outer_halves = (
        grad_square(
            place,
            places(near[0], "x"),
            [
                [(oc, 0, f2, (), True), (oc_mate, 0, cols_mate[0], (), False)],
                [(text_all, 0, dt, (0,), True), (text_all, 0, dt_mate, (0,), True)],
                [(text_all, 0, dt, (1,), True), (text_all, 0, dt_mate, (1,), True)],
                [(c, 0, dqc, (), True), (c_mate, 0, cols_mate[1], (), False)],
                [(os_rows, 0, f1, (), True), (os_mate, 0, cols_mate[2], (), False)],
            ],
            wide_size,
        )
    )
    down.wait(outer_halves)
    down.step(near[1])
    up.wait(outer_halves, down.sent)
    for axis in near[2:]:
        up.step(axis)
    outer.add(outer_halves, down.sent, up.sent)
    do_mate = after(do_mate, down.sent, up.sent)
    d = self_backward(place, q, k, v, o, o_mate, do_own, do_mate, log_self, blocks)
    d, d_mate = d[:3], d[3:]
    d_other = [to_mate(part) for part in d_mate]
    for axis in near[2:]:
        down.wait(d)
        down.step(axis)
    d = after(d, down.sent)
    shape, dims = bit_dims(1, near[0])
    inner_shape, inner_dims = bit_dims(1, *up_bits)
    inner_shape = (2,) + inner_shape + (3, rows_wide, 2 * quarter)
    inner_dims["x"] = len(inner_shape) - 1
    inner = Scatter(inner_shape, *up_bits, inner_dims)
    inner.add(
        grad_square(
            place,
            places(*up_bits),
            [[(a, 0, d[j], (), False), (a, 1, d_mate[j], (), False)] for j in range(3)],
            wide_size,
            up_bits,
        )
    )
    up.wait(inner.sent)
    up.step("x")
    d_other = after(d_other, inner.sent, up.sent)
    grad_own, grad_far, late = first_backward(
        place, d, d_other, self_qkv, norm_gains, own, far, e1, block
    )
    image_far = to_chip(grad_far)
    late = jnp.concatenate(
        [late, row_sums[:7], jnp.concatenate(hidden_sums, 1).reshape(-1, width)]
    )
    late = late + to_mate(late)
    outer.wait(grad_far)
    outer.turn()
    inner.wait(outer.sent)
    inner.turn()
    late = after(late, inner.sent)
    for axis in near[1:]:
        late = late + exchange(late, axis)
    late_far = exchange(after(late, inner.sent), near[0])
    outer.wait(inner.sent)
    outer.step(near[1])
    late = late + after(late_far, outer.sent)
    late_far = to_chip(late)
    inner.wait(outer.sent)
    inner.step("x")
    dt = (dt.astype(F32) + dt_mate.astype(F32)).astype(BF)
    dt_own = lax.dynamic_slice_in_dim(dt, core * 2 * slot_block, 2 * slot_block, 1)
    dt_own = after(dt_own, inner.sent)
    grad_text = dot(dt_own[0], cross_kv[0], 1, 1) + dot(dt_own[1], cross_kv[1], 1, 1)
    text_far = to_chip(grad_text[slot_block:])
    for axis in near[2:]:
        outer.wait(inner.sent)
        outer.step(axis)
        inner.wait(outer.sent)
        inner.step(axis)
    down.wait(inner.sent)
    up.wait(inner.sent)
    outer.wait(inner.sent)
    inner.wait(inner.sent)
    late = late + after(late_far, inner.sent)
    image_far, out_far, text_far = after((image_far, out_far, text_far), inner.sent)

    outer_part = outer.total(5, rows_wide, quarter)
    inner_part = inner.total(3, rows_wide, quarter)
    down_part = transposed(place, down.total(quarter, mlp_out.shape[0] // wide_size))

    gains = jnp.stack([late[0], late[2], late[3]])
    shifts = jnp.stack([late[1], late[4], late[5]])
    return (
        home(layer_out, out_far),
        home(grad_own, image_far),
        home(grad_text[:slot_block], text_far),
        inner_part,
        outer_part[4],
        outer_part[3],
        outer_part[1:3],
        outer_part[0],
        up.total(rows_wide, mlp_in.shape[1] // 4),
        down_part,
        gains,
        shifts,
        late[6:9],
        late[9:].reshape(-1),
    )


def solution(mesh):
    rows = P("wide", "narrow", None)
    whole = P()
    return jax.shard_map(
        body,
        mesh=mesh,
        in_specs=(rows, rows, P("wide"), P("wide", None)) + (whole,) * 11 + (rows,),
        out_specs=(rows,) * 3
        + (
            P(None, "wide", "narrow"),
            P("wide", "narrow"),
            P("wide", "narrow"),
            P(None, "wide", "narrow"),
        )
        + (P("wide", "narrow"),) * 3
        + (whole,) * 4,
        check_vma=False,
    )
```
